256 devices in a mesh: dp: 8 (over x, core), ctx: 32 (over y, z).
Axes of the slice: x: 4, y: 4, z: 8, core: 2. Of those that a mesh axis runs over, the one named last changes fastest.
Arguments:
- tokens: bfloat16 [32768, 4096], P(('dp', 'ctx')), parts along dimension 0, may hold values from -6 to 6
- pick_flags: int32 [32768], P(('dp', 'ctx')), parts along dimension 0, may hold values from 0 to 1, as said below
- gate_scales: bfloat16 [32768], P(('dp', 'ctx')), parts along dimension 0, may hold values from 0.099609375 to 1
- attn_gain: float32 [4096], replicated, may hold values from 0.4 to 1.6
- query_weight: bfloat16 [4096, 4096], P(None, 'ctx')
- key_weight: bfloat16 [4096, 1024], P(None, 'ctx')
- value_matrix: bfloat16 [4096, 1024], P(None, 'ctx'), may hold values from -0.09375 to 0.09375
- output_weight: bfloat16 [4096, 4096], P('ctx'), may hold values from -0.09375 to 0.09375
- ffn_gain: float32 [4096], replicated, may hold values from 0.25 to 1.75
- gate_weight: bfloat16 [4096, 11264], P(None, 'ctx'), may hold values from -0.09375 to 0.09375
- up_weight: bfloat16 [4096, 11264], P(None, 'ctx'), may hold values from -0.09375 to 0.09375
- down_weight: bfloat16 [11264, 4096], P('ctx'), may hold values from -0.0546875 to 0.0546875
Outputs:
- block_out: bfloat16 [32768, 4096], P(('dp', 'ctx')), parts along dimension 0
The draws below stay inside these ranges and needn't reach their ends.
There are 8 independent parts, one for each index of `dp`. The reference program is written for one: setup_inputs(seed, part) draws one part's arguments, and reference() takes and returns one part's arrays. A program takes and returns all parts, laid end to end along the dimension named above; an argument that names none is the same for every part. Nothing has to cross between parts.
Inputs may be any that keep to these rules, and one draw needn't show every extreme that they name: `pick_flags`: each device's 128 tokens hold at most 32 picks, the first device exactly 32; each document holds exactly 512 picks; a device may hold none.
All inputs are finite; a program needn't handle non-finite values.
Results may differ from the reference program's by a relative error of at most 0.01.
Values may be sent and summed in bfloat16 or wider, within the bound.
A program may use at most 128 MiB of HBM per device.

```python
import jax
import jax.numpy as jnp
from jax import lax

MODEL_WIDTH = 4096
QUERY_HEADS = 32
KEY_VALUE_HEADS = 8
HEAD_SIZE = 128
FF = 11264
TOK_DEV = 128
PICK_DEV = 16
MOST = 32
PICKED_TOKENS = 512
TOKENS = 4096
N_CTX = 32


def draw_pick_flags(key, part):
    counts = jnp.full((N_CTX,), PICK_DEV, jnp.int32)
    others = 1 + jax.random.permutation(jax.random.fold_in(key, 1), N_CTX - 1)
    counts = counts.at[0].set(MOST).at[others[0]].set(0)
    remain = others[1:]
    for mixing in range(3):
        shuffled = jax.random.permutation(jax.random.fold_in(key, 10 + mixing), remain)
        givers = shuffled[0::2]
        takers = shuffled[1::2]
        give_now = counts[givers]
        take_now = counts[takers]
        upper_bound = jnp.minimum(give_now, MOST - take_now)
        lower_bound = -jnp.minimum(take_now, MOST - give_now)
        amount = jax.random.randint(jax.random.fold_in(key, 20 + mixing), givers.shape, lower_bound, upper_bound + 1)
        counts = counts.at[givers].add(-amount).at[takers].add(amount)
    device_keys = jax.random.split(jax.random.fold_in(key, 2), N_CTX)
    shuffled_ids = jax.vmap(lambda single: jax.random.permutation(single, TOK_DEV))(device_keys)
    picked = (shuffled_ids < counts[:, None]).astype(jnp.int32)
    return picked.reshape(TOK_DEV * N_CTX)


def repeated_keys(key):
    return jax.random.normal(jax.random.fold_in(key, 71), (MODEL_WIDTH, HEAD_SIZE * KEY_VALUE_HEADS), jnp.float32) * MODEL_WIDTH ** (-0.5)


def draw_key_weight(key, part):
    return repeated_keys(key).astype(jnp.bfloat16)


def draw_query_weight(key, part):
    noise = jax.random.normal(jax.random.fold_in(key, 72), (MODEL_WIDTH, QUERY_HEADS * HEAD_SIZE), jnp.float32) * MODEL_WIDTH ** (-0.5)
    return noise.astype(jnp.bfloat16)


def levels(stream_key, dims, shards, least, top_value):
    loudness, own = 1.0, jax.random.fold_in(stream_key, 6)
    for axis_at, parts in shards:
        steps = jnp.exp(jax.random.uniform(jax.random.fold_in(own, axis_at), (parts,), jnp.float32, least / len(shards), top_value / len(shards)))
        loudness = loudness * jnp.repeat(steps, dims[axis_at] // parts).reshape([-1 if axis == axis_at else 1 for axis in range(len(dims))])
    return loudness


def centred(stream_key, dims, deviation, reach, pieces=(), kind=jnp.bfloat16):
    level = levels(stream_key, dims, pieces, -0.22, 0.18) if pieces else 1.0
    result = jax.random.normal(stream_key, dims, jnp.float32) * deviation * level
    return jnp.minimum(jnp.maximum(result, -reach), reach).astype(kind)


def setup_inputs(seed: int = 0, part: int = 0) -> dict:
    splits = jax.random.split(jax.random.key(seed), 13)
    part_keys = jax.random.split(jax.random.fold_in(splits[12], part), 13)
    return {
        "tokens": centred(part_keys[0], (TOKENS, MODEL_WIDTH), 1.0, 6.0, ((0, 32),)),
        "pick_flags": draw_pick_flags(jax.random.fold_in(jax.random.fold_in(splits[12], part), 71), part),
        "gate_scales": jnp.clip(0.099609375 + 0.9003906 * jax.random.uniform(part_keys[2], (TOKENS,), jnp.float32) ** levels(part_keys[2], (TOKENS,), ((0, 32),), -0.2, 0.2), 0.099609375, 1.0).astype(jnp.bfloat16),
        "attn_gain": jnp.clip(jax.random.uniform(splits[3], (MODEL_WIDTH,), jnp.float32, 0.4, 1.6), 0.4, 1.6),
        "query_weight": draw_query_weight(jax.random.fold_in(splits[12], 71), part),
        "key_weight": draw_key_weight(jax.random.fold_in(splits[12], 71), part),
        "value_matrix": centred(splits[6], (MODEL_WIDTH, HEAD_SIZE * KEY_VALUE_HEADS), MODEL_WIDTH ** -0.5, 0.09375, ((1, 32),)),
        "output_weight": centred(splits[7], (QUERY_HEADS * HEAD_SIZE, MODEL_WIDTH), (QUERY_HEADS * HEAD_SIZE) ** -0.5, 0.09375, ((0, 32),)),
        "ffn_gain": jnp.clip(1.0 + 0.15 * jax.random.normal(splits[8], (MODEL_WIDTH,), jnp.float32), 0.25, 1.75),
        "gate_weight": centred(splits[9], (MODEL_WIDTH, FF), MODEL_WIDTH ** -0.5, 0.09375, ((1, 32),)),
        "up_weight": centred(splits[10], (MODEL_WIDTH, FF), MODEL_WIDTH ** -0.5, 0.09375, ((1, 32),)),
        "down_weight": centred(splits[11], (FF, MODEL_WIDTH), FF ** -0.5, 0.0546875, ((0, 32),)),
    }


norm_eps = 1e-05
rope_base = 500000.0

def rms_scale(matrix, gain_vec):
    mean_square = lax.optimization_barrier(jnp.mean(matrix * matrix, axis=-1, keepdims=True))
    return matrix * lax.rsqrt(mean_square + norm_eps) * gain_vec

def apply_rotary(values, token_positions):
    half_dim = values.shape[-1] // 2
    frequency = rope_base ** (-(jnp.arange(half_dim, dtype=jnp.float32) * 2.0) / values.shape[-1])
    angles = token_positions.astype(jnp.float32)[:, None] * frequency[None, :]
    cosine = jnp.cos(angles)[:, None, :]
    sine_part = jnp.sin(angles)[:, None, :]
    lower_half = values[..., :half_dim]
    upper_half = values[..., half_dim:]
    return jnp.concatenate((lower_half * cosine - upper_half * sine_part, upper_half * cosine + lower_half * sine_part), axis=-1)

def rounded(values):
    return lax.optimization_barrier(values.astype(jnp.bfloat16)).astype(jnp.float32)

def reference(tokens, pick_flags, gate_scales, attn_gain, query_weight, key_weight, value_matrix, output_weight, ffn_gain, gate_weight, up_weight, down_weight):
    picked_index = jnp.nonzero(pick_flags, size=PICKED_TOKENS)[0].astype(jnp.int32)
    picked_rows = tokens[picked_index]
    scales = gate_scales[picked_index].astype(jnp.float32)
    normalized_rows = rms_scale(picked_rows.astype(jnp.float32), attn_gain).astype(jnp.bfloat16)
    queries = jnp.dot(normalized_rows, query_weight, preferred_element_type=jnp.float32).reshape(PICKED_TOKENS, QUERY_HEADS, HEAD_SIZE)
    queries = apply_rotary(queries, picked_index).astype(jnp.bfloat16)
    unrotated_keys = jnp.dot(normalized_rows, key_weight, preferred_element_type=jnp.float32).astype(jnp.bfloat16)
    repeated_values = jnp.dot(normalized_rows, value_matrix, preferred_element_type=jnp.float32).astype(jnp.bfloat16)
    repeated_values = jnp.transpose(repeated_values.reshape(PICKED_TOKENS, HEAD_SIZE, KEY_VALUE_HEADS), (0, 2, 1))
    key_heads = jnp.transpose(unrotated_keys.astype(jnp.float32).reshape(PICKED_TOKENS, HEAD_SIZE, KEY_VALUE_HEADS), (0, 2, 1))
    rotated_keys = apply_rotary(key_heads, picked_index).astype(jnp.bfloat16)
    query_group_width = QUERY_HEADS // KEY_VALUE_HEADS
    allowed = picked_index[None, :] <= picked_index[:, None]

    def one_head(head_no):
        query_one = lax.dynamic_index_in_dim(queries, head_no, 1, keepdims=False)
        key_one = lax.dynamic_index_in_dim(rotated_keys, head_no // query_group_width, 1, keepdims=False)
        value_one = lax.dynamic_index_in_dim(repeated_values, head_no // query_group_width, 1, keepdims=False)
        scores = jnp.dot(query_one, key_one.T, preferred_element_type=jnp.float32) / jnp.sqrt(jnp.float32(HEAD_SIZE))
        scores = jnp.where(allowed, scores, -jnp.inf)
        row_max = lax.optimization_barrier(jnp.max(scores, axis=1, keepdims=True))
        exp_terms = jnp.exp(scores - row_max)
        prob_bf = (exp_terms / lax.optimization_barrier(jnp.sum(exp_terms, axis=1, keepdims=True))).astype(jnp.bfloat16)
        return jnp.dot(prob_bf, value_one, preferred_element_type=jnp.float32).astype(jnp.bfloat16)
    heads_out = lax.map(one_head, jnp.arange(QUERY_HEADS, dtype=jnp.int32))
    heads_out = jnp.transpose(heads_out, (1, 0, 2)).reshape(PICKED_TOKENS, QUERY_HEADS * HEAD_SIZE)
    head_width = QUERY_HEADS * HEAD_SIZE // N_CTX

    def add_attn(block_no, total):
        first_row = (block_no * head_width).astype(jnp.int32)
        left = lax.dynamic_slice_in_dim(heads_out, first_row, head_width, 1)
        right = lax.dynamic_slice_in_dim(output_weight, first_row, head_width, 0)
        return total + rounded(jnp.dot(left, right, preferred_element_type=jnp.float32))
    attn_sum = lax.fori_loop(0, N_CTX, add_attn, jnp.zeros((PICKED_TOKENS, MODEL_WIDTH), jnp.float32))
    mixed = picked_rows.astype(jnp.float32) + attn_sum
    normed_ffn = rms_scale(mixed, ffn_gain).astype(jnp.bfloat16)
    unit_width = FF // N_CTX

    def add_ffn(block_no, total):
        first_row = (block_no * unit_width).astype(jnp.int32)
        gate_proj = jnp.dot(normed_ffn, lax.dynamic_slice_in_dim(gate_weight, first_row, unit_width, 1), preferred_element_type=jnp.float32)
        up_proj = jnp.dot(normed_ffn, lax.dynamic_slice_in_dim(up_weight, first_row, unit_width, 1), preferred_element_type=jnp.float32)
        hidden = (jax.nn.silu(gate_proj) * up_proj).astype(jnp.bfloat16)
        return total + rounded(jnp.dot(hidden, lax.dynamic_slice_in_dim(down_weight, first_row, unit_width, 0), preferred_element_type=jnp.float32))
    ffn_sum = lax.fori_loop(0, N_CTX, add_ffn, jnp.zeros((PICKED_TOKENS, MODEL_WIDTH), jnp.float32))
    final = (picked_rows.astype(jnp.float32) + scales[:, None] * (attn_sum + ffn_sum)).astype(jnp.bfloat16)
    return tokens.at[picked_index].set(final)
```

```python
import jax
import jax.numpy as jnp
from jax import lax
from jax.sharding import PartitionSpec as P

QUERY_HEADS = 32
KEY_VALUE_HEADS = 8
HEAD_SIZE = 128
PICK_DEV = 16
MOST = 32


norm_eps = 1e-05
rope_base = 500000.0


def rms_scale(matrix, gain_vec):
    mean_square = jnp.mean(matrix * matrix, axis=-1, keepdims=True)
    return matrix * lax.rsqrt(mean_square + norm_eps) * gain_vec


def apply_rotary(values, token_positions):
    half_dim = values.shape[-1] // 2
    frequency = rope_base ** (-(jnp.arange(half_dim, dtype=jnp.float32) * 2.0) / values.shape[-1])
    angles = token_positions.astype(jnp.float32)[:, None] * frequency[None, :]
    cosine = jnp.cos(angles)
    sine_part = jnp.sin(angles)
    lower_half = values[..., :half_dim]
    upper_half = values[..., half_dim:]
    return jnp.concatenate(
        (
            lower_half * cosine - upper_half * sine_part,
            upper_half * cosine + lower_half * sine_part,
        ),
        axis=-1,
    )


def reduce_scatter_rows(partial, ctx_size):
    rows, width = partial.shape
    pieces = lax.all_to_all(
        partial.reshape(ctx_size, rows // ctx_size, width), "ctx", 0, 0, tiled=True
    )
    return jnp.sum(pieces.astype(jnp.float32), axis=0)


def body(
    tokens,
    pick_flags,
    gate_scales,
    attn_gain,
    query_weight,
    key_weight,
    value_matrix,
    output_weight,
    ffn_gain,
    gate_weight,
    up_weight,
    down_weight,
):
    tok_local, width = tokens.shape
    ctx_size = lax.axis_size("ctx")
    my_index = lax.axis_index("ctx")
    picked_count = PICK_DEV * ctx_size
    half_pick = PICK_DEV // 2
    half_cycle = ctx_size // 2
    slot_of = jnp.cumsum(pick_flags) - 1
    token_ids = jnp.arange(tok_local, dtype=jnp.int32)
    slot_match = (jnp.arange(MOST, dtype=jnp.int32)[:, None] == slot_of[None, :]) & (
        pick_flags[None, :] == 1
    )
    chosen = jnp.sum(jnp.where(slot_match, token_ids[None, :], 0), axis=1)
    filled = jnp.any(slot_match, axis=1)
    local_index = jnp.where(filled, chosen, -1)
    padded_rows = jnp.where(filled[:, None], tokens[chosen], jnp.zeros((), jnp.bfloat16))
    padded_gate = jnp.where(filled, gate_scales[chosen], jnp.zeros((), jnp.bfloat16))
    lane = jnp.arange(128, dtype=jnp.int32)[None, :]
    extra = jnp.where(
        lane == 0,
        local_index.astype(jnp.bfloat16)[:, None],
        jnp.where(lane == 1, padded_gate[:, None], jnp.zeros((), jnp.bfloat16)),
    )
    packed = jnp.concatenate((padded_rows, extra), axis=1)
    all_packed = lax.all_gather(packed, "ctx", axis=0, tiled=True)
    all_rows = all_packed[:, :width]
    all_index = all_packed[:, width].astype(jnp.int32)
    all_gate = all_packed[:, width + 1]
    counts = jnp.sum((all_index >= 0).reshape(ctx_size, MOST).astype(jnp.int32), axis=1)
    run_ends = jnp.cumsum(counts)
    run_starts = run_ends - counts
    order_ids = jnp.arange(picked_count, dtype=jnp.int32)
    owner_of = order_ids // PICK_DEV
    within = order_ids % PICK_DEV
    low_part = within < half_pick
    rank_block = jnp.where(low_part, owner_of, (owner_of + half_cycle) % ctx_size)
    rank_inner = jnp.where(low_part, 2 * within, 2 * (within - half_pick) + 1)
    rank_ids = rank_block * PICK_DEV + rank_inner
    source = jnp.sum((run_ends[None, :] <= rank_ids[:, None]).astype(jnp.int32), axis=1)
    flat_row = source * MOST + rank_ids - run_starts[source]
    picked_rows = all_rows[flat_row]
    scales = all_gate[flat_row].astype(jnp.float32)
    token_positions = source * tok_local + all_index[flat_row]
    normalized_rows = rms_scale(picked_rows.astype(jnp.float32), attn_gain).astype(jnp.bfloat16)
    queries = jnp.dot(normalized_rows, query_weight, preferred_element_type=jnp.float32)
    queries = apply_rotary(queries, token_positions).astype(jnp.bfloat16)
    kv_weight = jnp.concatenate((key_weight, value_matrix), axis=1)
    kv_local = jnp.einsum(
        "pd,dc->cp", normalized_rows, kv_weight, preferred_element_type=jnp.float32
    ).astype(jnp.bfloat16)
    comps = key_weight.shape[1] // KEY_VALUE_HEADS
    query_group_width = QUERY_HEADS // KEY_VALUE_HEADS
    by_head = jnp.transpose(
        kv_local.reshape(2, comps, KEY_VALUE_HEADS, picked_count), (2, 0, 1, 3)
    )
    send = jnp.repeat(by_head, query_group_width, axis=0)
    got = lax.all_to_all(send, "ctx", 0, 0, tiled=True)
    key_cols = got[:, 0].reshape(ctx_size * comps, picked_count)
    value_cols = got[:, 1].reshape(ctx_size * comps, picked_count)
    keys_here = apply_rotary(key_cols.T.astype(jnp.float32), token_positions).astype(jnp.bfloat16)
    values_here = value_cols.T
    scores = jnp.dot(queries, keys_here.T, preferred_element_type=jnp.float32) / jnp.sqrt(
        jnp.float32(HEAD_SIZE)
    )
    allowed = token_positions[None, :] <= token_positions[:, None]
    scores = jnp.where(allowed, scores, -jnp.inf)
    row_max = jnp.max(scores, axis=1, keepdims=True)
    exp_terms = jnp.exp(scores - row_max)
    prob_bf = (exp_terms / jnp.sum(exp_terms, axis=1, keepdims=True)).astype(jnp.bfloat16)
    head_out = jnp.dot(prob_bf, values_here, preferred_element_type=jnp.float32).astype(jnp.bfloat16)
    own_start = my_index * PICK_DEV
    own_rows = lax.dynamic_slice_in_dim(picked_rows, own_start, PICK_DEV, 0).astype(jnp.float32)
    attn_own = reduce_scatter_rows(
        jnp.dot(head_out, output_weight, preferred_element_type=jnp.float32).astype(jnp.bfloat16),
        ctx_size,
    )
    mixed_own = own_rows + attn_own
    normed_own = rms_scale(mixed_own, ffn_gain).astype(jnp.bfloat16)
    normed_ffn = lax.all_gather(normed_own, "ctx", axis=0, tiled=True)
    gate_proj = jnp.dot(normed_ffn, gate_weight, preferred_element_type=jnp.float32)
    up_proj = jnp.dot(normed_ffn, up_weight, preferred_element_type=jnp.float32)
    hidden = (jax.nn.silu(gate_proj) * up_proj).astype(jnp.bfloat16)
    ffn_own = reduce_scatter_rows(
        jnp.dot(hidden, down_weight, preferred_element_type=jnp.float32).astype(jnp.bfloat16),
        ctx_size,
    )
    scale_own = lax.dynamic_slice_in_dim(scales, own_start, PICK_DEV, 0)
    final_own = (own_rows + scale_own[:, None] * (attn_own + ffn_own)).astype(jnp.bfloat16)
    final_all = lax.all_gather(final_own, "ctx", axis=0, tiled=True)
    my_start = run_starts[my_index]
    rank_here = jnp.clip(my_start + slot_of, 0, picked_count - 1)
    inner_here = rank_here % PICK_DEV
    odd_here = inner_here % 2
    owner_here = (rank_here // PICK_DEV + odd_here * half_cycle) % ctx_size
    take_rows = owner_here * PICK_DEV + inner_here // 2 + odd_here * half_pick
    return jnp.where(pick_flags[:, None] == 1, final_all[take_rows], tokens)


def solution(mesh):
    in_specs = (
        P(("dp", "ctx"), None),
        P(("dp", "ctx")),
        P(("dp", "ctx")),
        P(),
        P(None, "ctx"),
        P(None, "ctx"),
        P(None, "ctx"),
        P("ctx", None),
        P(),
        P(None, "ctx"),
        P(None, "ctx"),
        P("ctx", None),
    )
    out_specs = P(("dp", "ctx"), None)
    return jax.shard_map(body, mesh=mesh, in_specs=in_specs, out_specs=out_specs, check_vma=False)
```

```python
import jax
import jax.numpy as jnp
from jax import lax
from jax.sharding import PartitionSpec as P

QUERY_HEADS = 32
KEY_VALUE_HEADS = 8
HEAD_SIZE = 128
PICK_DEV = 16
MOST = 32


norm_eps = 1e-05
rope_base = 500000.0


def rms_scale(matrix, gain_vec):
    mean_square = jnp.mean(matrix * matrix, axis=-1, keepdims=True)
    return matrix * lax.rsqrt(mean_square + norm_eps) * gain_vec


def apply_rotary(values, token_positions):
    half_dim = values.shape[-1] // 2
    frequency = rope_base ** (-(jnp.arange(half_dim, dtype=jnp.float32) * 2.0) / values.shape[-1])
    angles = token_positions.astype(jnp.float32)[:, None] * frequency[None, :]
    cosine = jnp.cos(angles)
    sine_part = jnp.sin(angles)
    lower_half = values[..., :half_dim]
    upper_half = values[..., half_dim:]
    return jnp.concatenate(
        (
            lower_half * cosine - upper_half * sine_part,
            upper_half * cosine + lower_half * sine_part,
        ),
        axis=-1,
    )


def reduce_scatter_rows(partial, ctx_size):
    rows, width = partial.shape
    pieces = lax.all_to_all(
        partial.reshape(ctx_size, rows // ctx_size, width), "ctx", 0, 0, tiled=True
    )
    return jnp.sum(pieces.astype(jnp.float32), axis=0)


def body(
    tokens,
    pick_flags,
    gate_scales,
    attn_gain,
    query_weight,
    key_weight,
    value_matrix,
    output_weight,
    ffn_gain,
    gate_weight,
    up_weight,
    down_weight,
):
    tok_local, width = tokens.shape
    ctx_size = lax.axis_size("ctx")
    my_index = lax.axis_index("ctx")
    picked_count = PICK_DEV * ctx_size
    slots = MOST * ctx_size
    half_pick = PICK_DEV // 2
    half_cycle = ctx_size // 2
    slot_of = jnp.cumsum(pick_flags) - 1
    token_ids = jnp.arange(tok_local, dtype=jnp.int32)
    slot_match = (jnp.arange(MOST, dtype=jnp.int32)[:, None] == slot_of[None, :]) & (
        pick_flags[None, :] == 1
    )
    chosen = jnp.sum(jnp.where(slot_match, token_ids[None, :], 0), axis=1)
    filled = jnp.any(slot_match, axis=1)
    local_index = jnp.where(filled, chosen, -1)
    padded_rows = jnp.where(filled[:, None], tokens[chosen], jnp.zeros((), jnp.bfloat16))
    padded_gate = jnp.where(filled, gate_scales[chosen], jnp.zeros((), jnp.bfloat16))
    lane = jnp.arange(128, dtype=jnp.int32)[None, :]
    extra = jnp.where(
        lane == 0,
        local_index.astype(jnp.bfloat16)[:, None],
        jnp.where(lane == 1, padded_gate[:, None], jnp.zeros((), jnp.bfloat16)),
    )
    packed = jnp.concatenate((padded_rows, extra), axis=1)
    all_packed = lax.all_gather(packed, "ctx", axis=0, tiled=True)
    all_index = all_packed[:, width].astype(jnp.int32)
    slot_filled = all_index >= 0
    counts = jnp.sum(slot_filled.reshape(ctx_size, MOST).astype(jnp.int32), axis=1)
    run_ends = jnp.cumsum(counts)
    run_starts = run_ends - counts
    slot_ids = jnp.arange(slots, dtype=jnp.int32)
    slot_pos = (slot_ids // MOST) * tok_local + all_index
    rope_pos = jnp.where(slot_filled, slot_pos, 0)
    never = jnp.int32(1 << 30)
    mask_pos = jnp.where(slot_filled, slot_pos, never)
    normalized = rms_scale(all_packed[:, :width].astype(jnp.float32), attn_gain).astype(jnp.bfloat16)
    queries = jnp.dot(normalized, query_weight, preferred_element_type=jnp.float32)
    queries = apply_rotary(queries, rope_pos).astype(jnp.bfloat16)
    kv_weight = jnp.concatenate((key_weight, value_matrix), axis=1)
    kv_local = jnp.einsum(
        "pd,dc->cp", normalized, kv_weight, preferred_element_type=jnp.float32
    ).astype(jnp.bfloat16)
    comps = key_weight.shape[1] // KEY_VALUE_HEADS
    query_group_width = QUERY_HEADS // KEY_VALUE_HEADS
    by_head = jnp.transpose(kv_local.reshape(2, comps, KEY_VALUE_HEADS, slots), (2, 0, 1, 3))
    send = jnp.repeat(by_head, query_group_width, axis=0)
    got = lax.all_to_all(send, "ctx", 0, 0, tiled=True)
    key_cols = got[:, 0].reshape(ctx_size * comps, slots)
    value_cols = got[:, 1].reshape(ctx_size * comps, slots)
    keys_here = apply_rotary(key_cols.T.astype(jnp.float32), rope_pos).astype(jnp.bfloat16)
    values_here = value_cols.T
    scores = jnp.dot(queries, keys_here.T, preferred_element_type=jnp.float32) / jnp.sqrt(
        jnp.float32(HEAD_SIZE)
    )
    allowed = mask_pos[None, :] <= mask_pos[:, None]
    scores = jnp.where(allowed, scores, -jnp.inf)
    row_max = jnp.max(scores, axis=1, keepdims=True)
    exp_terms = jnp.exp(scores - row_max)
    prob_bf = (exp_terms / jnp.sum(exp_terms, axis=1, keepdims=True)).astype(jnp.bfloat16)
    head_pad = jnp.dot(prob_bf, values_here, preferred_element_type=jnp.float32).astype(jnp.bfloat16)
    order_ids = jnp.arange(picked_count, dtype=jnp.int32)
    owner_of = order_ids // PICK_DEV
    within = order_ids % PICK_DEV
    low_part = within < half_pick
    rank_block = jnp.where(low_part, owner_of, (owner_of + half_cycle) % ctx_size)
    rank_inner = jnp.where(low_part, 2 * within, 2 * (within - half_pick) + 1)
    rank_ids = rank_block * PICK_DEV + rank_inner
    before = (run_ends[None, :] <= rank_ids[:, None]).astype(jnp.int32)
    source = jnp.sum(before, axis=1)
    flat_row = rank_ids + jnp.sum(before * (MOST - counts)[None, :], axis=1)
    pick_onehot = (flat_row[:, None] == slot_ids[None, :]).astype(jnp.bfloat16)
    head_out = jnp.dot(pick_onehot, head_pad, preferred_element_type=jnp.float32).astype(jnp.bfloat16)
    own_start = my_index * PICK_DEV
    own_flat = lax.dynamic_slice_in_dim(flat_row, own_start, PICK_DEV, 0)
    own_packed = all_packed[own_flat]
    own_rows = own_packed[:, :width].astype(jnp.float32)
    scale_own = own_packed[:, width + 1].astype(jnp.float32)
    attn_own = reduce_scatter_rows(
        jnp.dot(head_out, output_weight, preferred_element_type=jnp.float32).astype(jnp.bfloat16),
        ctx_size,
    )
    mixed_own = own_rows + attn_own
    normed_own = rms_scale(mixed_own, ffn_gain).astype(jnp.bfloat16)
    normed_ffn = lax.all_gather(normed_own, "ctx", axis=0, tiled=True)
    gate_proj = jnp.dot(normed_ffn, gate_weight, preferred_element_type=jnp.float32)
    up_proj = jnp.dot(normed_ffn, up_weight, preferred_element_type=jnp.float32)
    hidden = (jax.nn.silu(gate_proj) * up_proj).astype(jnp.bfloat16)
    ffn_own = reduce_scatter_rows(
        jnp.dot(hidden, down_weight, preferred_element_type=jnp.float32).astype(jnp.bfloat16),
        ctx_size,
    )
    final_own = (own_rows + scale_own[:, None] * (attn_own + ffn_own)).astype(jnp.bfloat16)
    own_source = lax.dynamic_slice_in_dim(source, own_start, PICK_DEV, 0)
    targets = jnp.arange(ctx_size, dtype=jnp.int32)[:, None]
    first_half = (own_source[None, :half_pick] == targets)[:, :, None]
    second_half = (own_source[None, half_pick:] == targets)[:, :, None]
    zero = jnp.zeros((), jnp.bfloat16)
    back = jnp.where(
        first_half,
        final_own[None, :half_pick],
        jnp.where(second_half, final_own[None, half_pick:], zero),
    )
    returned = lax.all_to_all(back, "ctx", 0, 0, tiled=True).reshape(ctx_size * half_pick, width)
    my_start = run_starts[my_index]
    rank_here = jnp.clip(my_start + slot_of, 0, picked_count - 1)
    inner_here = rank_here % PICK_DEV
    odd_here = inner_here % 2
    owner_here = (rank_here // PICK_DEV + odd_here * half_cycle) % ctx_size
    take_rows = owner_here * half_pick + inner_here // 2
    return jnp.where(pick_flags[:, None] == 1, returned[take_rows], tokens)


def solution(mesh):
    in_specs = (
        P(("dp", "ctx"), None),
        P(("dp", "ctx")),
        P(("dp", "ctx")),
        P(),
        P(None, "ctx"),
        P(None, "ctx"),
        P(None, "ctx"),
        P("ctx", None),
        P(),
        P(None, "ctx"),
        P(None, "ctx"),
        P("ctx", None),
    )
    out_specs = P(("dp", "ctx"), None)
    return jax.shard_map(body, mesh=mesh, in_specs=in_specs, out_specs=out_specs, check_vma=False)
```

```python
import jax
import jax.numpy as jnp
from jax import lax
from jax.sharding import Mesh, PartitionSpec as P

QUERY_HEADS = 32
KEY_VALUE_HEADS = 8
HEAD_SIZE = 128
PICK_DEV = 16
MOST = 32
Z_RUN = 8
GROUP = ("cy", "cz")


norm_eps = 1e-05
rope_base = 500000.0


def rms_scale(matrix, gain_vec):
    mean_square = jnp.mean(matrix * matrix, axis=-1, keepdims=True)
    return matrix * lax.rsqrt(mean_square + norm_eps) * gain_vec


def apply_rotary(values, token_positions):
    half_dim = values.shape[-1] // 2
    frequency = rope_base ** (-(jnp.arange(half_dim, dtype=jnp.float32) * 2.0) / values.shape[-1])
    angles = token_positions.astype(jnp.float32)[:, None] * frequency[None, :]
    cosine = jnp.cos(angles)
    sine_part = jnp.sin(angles)
    lower_half = values[..., :half_dim]
    upper_half = values[..., half_dim:]
    return jnp.concatenate(
        (
            lower_half * cosine - upper_half * sine_part,
            upper_half * cosine + lower_half * sine_part,
        ),
        axis=-1,
    )


def reduce_scatter_rows(partial, y_size, z_size):
    rows, width = partial.shape
    blocks = partial.reshape(z_size, y_size, rows // (y_size * z_size), width)
    over_y = lax.all_to_all(blocks, "cy", 1, 1, tiled=True)
    part = jnp.sum(over_y.astype(jnp.float32), axis=1).astype(jnp.bfloat16)
    over_z = lax.all_to_all(part, "cz", 0, 0, tiled=True)
    return jnp.sum(over_z.astype(jnp.float32), axis=0)


def gather_rows(x):
    return lax.all_gather(lax.all_gather(x, "cy", axis=0, tiled=True), "cz", axis=0, tiled=True)


def body(
    tokens,
    pick_flags,
    gate_scales,
    attn_gain,
    query_weight,
    key_weight,
    value_matrix,
    output_weight,
    ffn_gain,
    gate_weight,
    up_weight,
    down_weight,
):
    tok_local, width = tokens.shape
    y_size = lax.axis_size("cy")
    z_size = lax.axis_size("cz")
    ctx_size = y_size * z_size
    my_index = lax.axis_index("cy") * z_size + lax.axis_index("cz")
    blk = jnp.arange(ctx_size, dtype=jnp.int32)
    block_dev = (blk % y_size) * z_size + blk // y_size
    picked_count = PICK_DEV * ctx_size
    slots = MOST * ctx_size
    half_pick = PICK_DEV // 2
    half_cycle = ctx_size // 2
    slot_of = jnp.cumsum(pick_flags) - 1
    token_ids = jnp.arange(tok_local, dtype=jnp.int32)
    slot_match = (jnp.arange(MOST, dtype=jnp.int32)[:, None] == slot_of[None, :]) & (
        pick_flags[None, :] == 1
    )
    chosen = jnp.sum(jnp.where(slot_match, token_ids[None, :], 0), axis=1)
    filled = jnp.any(slot_match, axis=1)
    local_index = jnp.where(filled, chosen, -1)
    padded_rows = jnp.where(filled[:, None], tokens[chosen], jnp.zeros((), jnp.bfloat16))
    padded_gate = jnp.where(filled, gate_scales[chosen], jnp.zeros((), jnp.bfloat16))
    lane = jnp.arange(128, dtype=jnp.int32)[None, :]
    extra = jnp.where(
        lane == 0,
        local_index.astype(jnp.bfloat16)[:, None],
        jnp.where(lane == 1, padded_gate[:, None], jnp.zeros((), jnp.bfloat16)),
    )
    packed = jnp.concatenate((padded_rows, extra), axis=1)
    all_packed = gather_rows(packed)
    all_index = all_packed[:, width].astype(jnp.int32)
    slot_filled = all_index >= 0
    counts_blk = jnp.sum(slot_filled.reshape(ctx_size, MOST).astype(jnp.int32), axis=1)
    counts = counts_blk.reshape(z_size, y_size).T.reshape(ctx_size)
    run_ends = jnp.cumsum(counts)
    run_starts = run_ends - counts
    slot_ids = jnp.arange(slots, dtype=jnp.int32)
    slot_pos = block_dev[slot_ids // MOST] * tok_local + all_index
    rope_pos = jnp.where(slot_filled, slot_pos, 0)
    never = jnp.int32(1 << 30)
    mask_pos = jnp.where(slot_filled, slot_pos, never)
    normalized = rms_scale(all_packed[:, :width].astype(jnp.float32), attn_gain).astype(jnp.bfloat16)
    queries = jnp.dot(normalized, query_weight, preferred_element_type=jnp.float32)
    queries = apply_rotary(queries, rope_pos).astype(jnp.bfloat16)
    kv_weight = jnp.concatenate((key_weight, value_matrix), axis=1)
    kv_local = jnp.einsum(
        "pd,dc->cp", normalized, kv_weight, preferred_element_type=jnp.float32
    ).astype(jnp.bfloat16)
    comps = key_weight.shape[1] // KEY_VALUE_HEADS
    query_group_width = QUERY_HEADS // KEY_VALUE_HEADS
    by_head = jnp.transpose(kv_local.reshape(2, comps, KEY_VALUE_HEADS, slots), (2, 0, 1, 3))
    send = jnp.repeat(by_head, query_group_width, axis=0)
    got = lax.all_to_all(send, GROUP, 0, 0, tiled=True)
    key_cols = got[:, 0].reshape(ctx_size * comps, slots)
    value_cols = got[:, 1].reshape(ctx_size * comps, slots)
    keys_here = apply_rotary(key_cols.T.astype(jnp.float32), rope_pos).astype(jnp.bfloat16)
    values_here = value_cols.T
    scores = jnp.dot(queries, keys_here.T, preferred_element_type=jnp.float32) / jnp.sqrt(
        jnp.float32(HEAD_SIZE)
    )
    allowed = mask_pos[None, :] <= mask_pos[:, None]
    scores = jnp.where(allowed, scores, -jnp.inf)
    row_max = jnp.max(scores, axis=1, keepdims=True)
    exp_terms = jnp.exp(scores - row_max)
    prob_bf = (exp_terms / jnp.sum(exp_terms, axis=1, keepdims=True)).astype(jnp.bfloat16)
    head_pad = jnp.dot(prob_bf, values_here, preferred_element_type=jnp.float32).astype(jnp.bfloat16)
    order_ids = jnp.arange(picked_count, dtype=jnp.int32)
    owner_of = order_ids // PICK_DEV
    within = order_ids % PICK_DEV
    low_part = within < half_pick
    rank_block = jnp.where(low_part, owner_of, (owner_of + half_cycle) % ctx_size)
    rank_inner = jnp.where(low_part, 2 * within, 2 * (within - half_pick) + 1)
    rank_ids = rank_block * PICK_DEV + rank_inner
    before = (run_ends[None, :] <= rank_ids[:, None]).astype(jnp.int32)
    source = jnp.sum(before, axis=1)
    offset = rank_ids - jnp.sum(before * counts[None, :], axis=1)
    flat_row = ((source % z_size) * y_size + source // z_size) * MOST + offset
    flat_blocked = flat_row.reshape(ctx_size, PICK_DEV)[block_dev].reshape(picked_count)
    pick_onehot = (flat_blocked[:, None] == slot_ids[None, :]).astype(jnp.bfloat16)
    head_out = jnp.dot(pick_onehot, head_pad, preferred_element_type=jnp.float32).astype(jnp.bfloat16)
    own_start = my_index * PICK_DEV
    own_flat = lax.dynamic_slice_in_dim(flat_row, own_start, PICK_DEV, 0)
    own_packed = all_packed[own_flat]
    own_rows = own_packed[:, :width].astype(jnp.float32)
    scale_own = own_packed[:, width + 1].astype(jnp.float32)
    attn_own = reduce_scatter_rows(
        jnp.dot(head_out, output_weight, preferred_element_type=jnp.float32).astype(jnp.bfloat16),
        y_size,
        z_size,
    )
    mixed_own = own_rows + attn_own
    normed_own = rms_scale(mixed_own, ffn_gain).astype(jnp.bfloat16)
    normed_ffn = gather_rows(normed_own)
    gate_proj = jnp.dot(normed_ffn, gate_weight, preferred_element_type=jnp.float32)
    up_proj = jnp.dot(normed_ffn, up_weight, preferred_element_type=jnp.float32)
    hidden = (jax.nn.silu(gate_proj) * up_proj).astype(jnp.bfloat16)
    ffn_own = reduce_scatter_rows(
        jnp.dot(hidden, down_weight, preferred_element_type=jnp.float32).astype(jnp.bfloat16),
        y_size,
        z_size,
    )
    final_own = (own_rows + scale_own[:, None] * (attn_own + ffn_own)).astype(jnp.bfloat16)
    own_source = lax.dynamic_slice_in_dim(source, own_start, PICK_DEV, 0)
    targets = jnp.arange(ctx_size, dtype=jnp.int32)[:, None]
    first_half = (own_source[None, :half_pick] == targets)[:, :, None]
    second_half = (own_source[None, half_pick:] == targets)[:, :, None]
    zero = jnp.zeros((), jnp.bfloat16)
    back = jnp.where(
        first_half,
        final_own[None, :half_pick],
        jnp.where(second_half, final_own[None, half_pick:], zero),
    )
    returned = lax.all_to_all(back, GROUP, 0, 0, tiled=True).reshape(ctx_size * half_pick, width)
    my_start = run_starts[my_index]
    rank_here = jnp.clip(my_start + slot_of, 0, picked_count - 1)
    inner_here = rank_here % PICK_DEV
    odd_here = inner_here % 2
    owner_here = (rank_here // PICK_DEV + odd_here * half_cycle) % ctx_size
    take_rows = owner_here * half_pick + inner_here // 2
    return jnp.where(pick_flags[:, None] == 1, returned[take_rows], tokens)


def solution(mesh):
    dp_size, ctx_size = mesh.devices.shape
    z_size = Z_RUN if ctx_size % Z_RUN == 0 else ctx_size
    split = Mesh(mesh.devices.reshape(dp_size, ctx_size // z_size, z_size), ("dp", "cy", "cz"))
    rows = ("dp", "cy", "cz")
    in_specs = (
        P(rows, None),
        P(rows),
        P(rows),
        P(),
        P(None, GROUP),
        P(None, GROUP),
        P(None, GROUP),
        P(GROUP, None),
        P(),
        P(None, GROUP),
        P(None, GROUP),
        P(GROUP, None),
    )
    out_specs = P(rows, None)
    return jax.shard_map(body, mesh=split, in_specs=in_specs, out_specs=out_specs, check_vma=False)
```

```python
import functools

import jax
import jax.numpy as jnp
from jax import lax
from jax.experimental import pallas as pl
from jax.experimental.pallas import tpu as pltpu
from jax.sharding import Mesh, PartitionSpec as P

QUERY_HEADS = 32
KEY_VALUE_HEADS = 8
HEAD_SIZE = 128
PICK_DEV = 16
MOST = 32
Z_RUN = 8
GROUP = ("cy", "cz")


norm_eps = 1e-05
rope_base = 500000.0


def rms_scale(matrix, gain_vec):
    mean_square = jnp.mean(matrix * matrix, axis=-1, keepdims=True)
    return matrix * lax.rsqrt(mean_square + norm_eps) * gain_vec


def apply_rotary(values, token_positions):
    half_dim = values.shape[-1] // 2
    frequency = rope_base ** (-(jnp.arange(half_dim, dtype=jnp.float32) * 2.0) / values.shape[-1])
    angles = token_positions.astype(jnp.float32)[:, None] * frequency[None, :]
    cosine = jnp.cos(angles)
    sine_part = jnp.sin(angles)
    lower_half = values[..., :half_dim]
    upper_half = values[..., half_dim:]
    return jnp.concatenate(
        (
            lower_half * cosine - upper_half * sine_part,
            upper_half * cosine + lower_half * sine_part,
        ),
        axis=-1,
    )


MESH_ID = pl.DeviceIdType.MESH


def _zring_rs_kernel(n, x_ref, out_ref, recv, sendbuf, send_sem, recv_sem, credit):
    me = lax.axis_index("cz")
    right = lax.rem(me + 1, n)
    left = lax.rem(me + n - 1, n)
    half = x_ref.shape[2] // 2
    dest = (right, left)
    sender = (left, right)

    barrier = pltpu.get_barrier_semaphore()
    for neighbour in (left, right):
        pl.semaphore_signal(barrier, inc=1, device_id={"cz": neighbour}, device_id_type=MESH_ID)
    pl.semaphore_wait(barrier, 2)

    for step in range(n - 1):
        slot = step % 2
        copies = []
        for d in range(2):
            if step == 0:
                first = lax.rem(me + n - 1, n) if d == 0 else lax.rem(me + 1, n)
                src = x_ref.at[first, :, pl.ds(d * half, half)]
            else:
                pl.semaphore_wait(credit.at[d], 1)
                src = sendbuf.at[d, (step - 1) % 2]
            copy = pltpu.make_async_remote_copy(
                src_ref=src,
                dst_ref=recv.at[d, slot],
                send_sem=send_sem.at[d, slot],
                recv_sem=recv_sem.at[d, slot],
                device_id={"cz": dest[d]},
                device_id_type=MESH_ID,
            )
            copy.start()
            copies.append(copy)
        for d in range(2):
            copies[d].wait_recv()
            if d == 0:
                chunk = lax.rem(me + 2 * n - step - 2, n)
            else:
                chunk = lax.rem(me + step + 2, n)
            total = recv[d, slot].astype(jnp.float32) + x_ref[chunk, :, pl.ds(d * half, half)].astype(
                jnp.float32
            )
            if step == n - 2:
                out_ref[:, pl.ds(d * half, half)] = total
            else:
                sendbuf[d, slot] = total.astype(sendbuf.dtype)
            if step <= n - 3:
                pl.semaphore_signal(credit.at[d], inc=1, device_id={"cz": sender[d]}, device_id_type=MESH_ID)
        for d in range(2):
            copies[d].wait_send()


def zring_reduce_scatter(x, collective_id):
    n, rows, cols = x.shape
    half = cols // 2
    return pl.pallas_call(
        functools.partial(_zring_rs_kernel, n),
        out_shape=jax.ShapeDtypeStruct((rows, cols), jnp.float32),
        in_specs=[pl.BlockSpec(memory_space=pltpu.VMEM)],
        out_specs=pl.BlockSpec(memory_space=pltpu.VMEM),
        scratch_shapes=[
            pltpu.VMEM((2, 2, rows, half), x.dtype),
            pltpu.VMEM((2, 2, rows, half), x.dtype),
            pltpu.SemaphoreType.DMA((2, 2)),
            pltpu.SemaphoreType.DMA((2, 2)),
            pltpu.SemaphoreType.REGULAR((2,)),
        ],
        compiler_params=pltpu.CompilerParams(collective_id=collective_id, has_side_effects=True),
    )(x)


def reduce_scatter_rows(partial, y_size, z_size, collective_id):
    rows, width = partial.shape
    own = rows // (y_size * z_size)
    over_z = zring_reduce_scatter(partial.reshape(z_size, y_size * own, width), collective_id)
    part = over_z.astype(jnp.bfloat16).reshape(y_size, own, width)
    over_y = lax.all_to_all(part, "cy", 0, 0, tiled=True)
    return jnp.sum(over_y.astype(jnp.float32), axis=0)


def gather_rows(x):
    return lax.all_gather(lax.all_gather(x, "cy", axis=0, tiled=True), "cz", axis=0, tiled=True)


def body(
    tokens,
    pick_flags,
    gate_scales,
    attn_gain,
    query_weight,
    key_weight,
    value_matrix,
    output_weight,
    ffn_gain,
    gate_weight,
    up_weight,
    down_weight,
):
    tok_local, width = tokens.shape
    y_size = lax.axis_size("cy")
    z_size = lax.axis_size("cz")
    ctx_size = y_size * z_size
    my_index = lax.axis_index("cy") * z_size + lax.axis_index("cz")
    blk = jnp.arange(ctx_size, dtype=jnp.int32)
    block_dev = (blk % y_size) * z_size + blk // y_size
    picked_count = PICK_DEV * ctx_size
    slots = MOST * ctx_size
    half_pick = PICK_DEV // 2
    half_cycle = ctx_size // 2
    slot_of = jnp.cumsum(pick_flags) - 1
    token_ids = jnp.arange(tok_local, dtype=jnp.int32)
    slot_match = (jnp.arange(MOST, dtype=jnp.int32)[:, None] == slot_of[None, :]) & (
        pick_flags[None, :] == 1
    )
    chosen = jnp.sum(jnp.where(slot_match, token_ids[None, :], 0), axis=1)
    filled = jnp.any(slot_match, axis=1)
    local_index = jnp.where(filled, chosen, -1)
    padded_rows = jnp.where(filled[:, None], tokens[chosen], jnp.zeros((), jnp.bfloat16))
    padded_gate = jnp.where(filled, gate_scales[chosen], jnp.zeros((), jnp.bfloat16))
    lane = jnp.arange(128, dtype=jnp.int32)[None, :]
    extra = jnp.where(
        lane == 0,
        local_index.astype(jnp.bfloat16)[:, None],
        jnp.where(lane == 1, padded_gate[:, None], jnp.zeros((), jnp.bfloat16)),
    )
    packed = jnp.concatenate((padded_rows, extra), axis=1)
    all_packed = lax.all_gather(packed, GROUP, axis=0, tiled=True)
    all_index = all_packed[:, width].astype(jnp.int32)
    slot_filled = all_index >= 0
    counts = jnp.sum(slot_filled.reshape(ctx_size, MOST).astype(jnp.int32), axis=1)
    run_ends = jnp.cumsum(counts)
    run_starts = run_ends - counts
    slot_ids = jnp.arange(slots, dtype=jnp.int32)
    slot_pos = (slot_ids // MOST) * tok_local + all_index
    rope_pos = jnp.where(slot_filled, slot_pos, 0)
    never = jnp.int32(1 << 30)
    mask_pos = jnp.where(slot_filled, slot_pos, never)
    normalized = rms_scale(all_packed[:, :width].astype(jnp.float32), attn_gain).astype(jnp.bfloat16)
    queries = jnp.dot(normalized, query_weight, preferred_element_type=jnp.float32)
    queries = apply_rotary(queries, rope_pos).astype(jnp.bfloat16)
    kv_weight = jnp.concatenate((key_weight, value_matrix), axis=1)
    kv_local = jnp.einsum(
        "pd,dc->cp", normalized, kv_weight, preferred_element_type=jnp.float32
    ).astype(jnp.bfloat16)
    comps = key_weight.shape[1] // KEY_VALUE_HEADS
    query_group_width = QUERY_HEADS // KEY_VALUE_HEADS
    by_head = jnp.transpose(kv_local.reshape(2, comps, KEY_VALUE_HEADS, slots), (2, 0, 1, 3))
    send = jnp.repeat(by_head, query_group_width, axis=0)
    got = lax.all_to_all(send, GROUP, 0, 0, tiled=True)
    key_cols = got[:, 0].reshape(ctx_size * comps, slots)
    value_cols = got[:, 1].reshape(ctx_size * comps, slots)
    keys_here = apply_rotary(key_cols.T.astype(jnp.float32), rope_pos).astype(jnp.bfloat16)
    values_here = value_cols.T
    scores = jnp.dot(queries, keys_here.T, preferred_element_type=jnp.float32) / jnp.sqrt(
        jnp.float32(HEAD_SIZE)
    )
    allowed = mask_pos[None, :] <= mask_pos[:, None]
    scores = jnp.where(allowed, scores, -jnp.inf)
    row_max = jnp.max(scores, axis=1, keepdims=True)
    exp_terms = jnp.exp(scores - row_max)
    prob_bf = (exp_terms / jnp.sum(exp_terms, axis=1, keepdims=True)).astype(jnp.bfloat16)
    head_pad = jnp.dot(prob_bf, values_here, preferred_element_type=jnp.float32).astype(jnp.bfloat16)
    order_ids = jnp.arange(picked_count, dtype=jnp.int32)
    owner_of = order_ids // PICK_DEV
    within = order_ids % PICK_DEV
    low_part = within < half_pick
    rank_block = jnp.where(low_part, owner_of, (owner_of + half_cycle) % ctx_size)
    rank_inner = jnp.where(low_part, 2 * within, 2 * (within - half_pick) + 1)
    rank_ids = rank_block * PICK_DEV + rank_inner
    before = (run_ends[None, :] <= rank_ids[:, None]).astype(jnp.int32)
    source = jnp.sum(before, axis=1)
    offset = rank_ids - jnp.sum(before * counts[None, :], axis=1)
    flat_row = source * MOST + offset
    flat_blocked = flat_row.reshape(ctx_size, PICK_DEV)[block_dev].reshape(picked_count)
    pick_onehot = (flat_blocked[:, None] == slot_ids[None, :]).astype(jnp.bfloat16)
    head_out = jnp.dot(pick_onehot, head_pad, preferred_element_type=jnp.float32).astype(jnp.bfloat16)
    own_start = my_index * PICK_DEV
    own_flat = lax.dynamic_slice_in_dim(flat_row, own_start, PICK_DEV, 0)
    own_packed = all_packed[own_flat]
    own_rows = own_packed[:, :width].astype(jnp.float32)
    scale_own = own_packed[:, width + 1].astype(jnp.float32)
    attn_own = reduce_scatter_rows(
        jnp.dot(head_out, output_weight, preferred_element_type=jnp.float32).astype(jnp.bfloat16),
        y_size,
        z_size,
        0,
    )
    mixed_own = own_rows + attn_own
    normed_own = rms_scale(mixed_own, ffn_gain).astype(jnp.bfloat16)
    normed_ffn = gather_rows(normed_own)
    gate_proj = jnp.dot(normed_ffn, gate_weight, preferred_element_type=jnp.float32)
    up_proj = jnp.dot(normed_ffn, up_weight, preferred_element_type=jnp.float32)
    hidden = (jax.nn.silu(gate_proj) * up_proj).astype(jnp.bfloat16)
    ffn_own = reduce_scatter_rows(
        jnp.dot(hidden, down_weight, preferred_element_type=jnp.float32).astype(jnp.bfloat16),
        y_size,
        z_size,
        1,
    )
    final_own = (own_rows + scale_own[:, None] * (attn_own + ffn_own)).astype(jnp.bfloat16)
    own_source = lax.dynamic_slice_in_dim(source, own_start, PICK_DEV, 0)
    targets = jnp.arange(ctx_size, dtype=jnp.int32)[:, None]
    first_half = (own_source[None, :half_pick] == targets)[:, :, None]
    second_half = (own_source[None, half_pick:] == targets)[:, :, None]
    zero = jnp.zeros((), jnp.bfloat16)
    back = jnp.where(
        first_half,
        final_own[None, :half_pick],
        jnp.where(second_half, final_own[None, half_pick:], zero),
    )
    returned = lax.all_to_all(back, GROUP, 0, 0, tiled=True).reshape(ctx_size * half_pick, width)
    my_start = run_starts[my_index]
    rank_here = jnp.clip(my_start + slot_of, 0, picked_count - 1)
    inner_here = rank_here % PICK_DEV
    odd_here = inner_here % 2
    owner_here = (rank_here // PICK_DEV + odd_here * half_cycle) % ctx_size
    take_rows = owner_here * half_pick + inner_here // 2
    return jnp.where(pick_flags[:, None] == 1, returned[take_rows], tokens)


def solution(mesh):
    dp_size, ctx_size = mesh.devices.shape
    z_size = Z_RUN if ctx_size % Z_RUN == 0 else ctx_size
    split = Mesh(mesh.devices.reshape(dp_size, ctx_size // z_size, z_size), ("dp", "cy", "cz"))
    rows = ("dp", "cy", "cz")
    in_specs = (
        P(rows, None),
        P(rows),
        P(rows),
        P(),
        P(None, GROUP),
        P(None, GROUP),
        P(None, GROUP),
        P(GROUP, None),
        P(),
        P(None, GROUP),
        P(None, GROUP),
        P(GROUP, None),
    )
    out_specs = P(rows, None)
    return jax.shard_map(body, mesh=split, in_specs=in_specs, out_specs=out_specs, check_vma=False)
```

```python
import functools

import jax
import jax.numpy as jnp
from jax import lax
from jax.experimental import pallas as pl
from jax.experimental.pallas import tpu as pltpu
from jax.sharding import Mesh, PartitionSpec as P

QUERY_HEADS = 32
KEY_VALUE_HEADS = 8
HEAD_SIZE = 128
PICK_DEV = 16
MOST = 32
Z_RUN = 8
GROUP = ("cy", "cz")


norm_eps = 1e-05
rope_base = 500000.0


def rms_scale(matrix, gain_vec):
    mean_square = jnp.mean(matrix * matrix, axis=-1, keepdims=True)
    return matrix * lax.rsqrt(mean_square + norm_eps) * gain_vec


def apply_rotary(values, token_positions):
    half_dim = values.shape[-1] // 2
    frequency = rope_base ** (-(jnp.arange(half_dim, dtype=jnp.float32) * 2.0) / values.shape[-1])
    angles = token_positions.astype(jnp.float32)[:, None] * frequency[None, :]
    cosine = jnp.cos(angles)
    sine_part = jnp.sin(angles)
    lower_half = values[..., :half_dim]
    upper_half = values[..., half_dim:]
    return jnp.concatenate(
        (
            lower_half * cosine - upper_half * sine_part,
            upper_half * cosine + lower_half * sine_part,
        ),
        axis=-1,
    )


MESH_ID = pl.DeviceIdType.MESH
SUB_CHUNKS = 2


def _zring_rs_kernel(n, x_ref, out_ref, recv, sendbuf, send_sem, recv_sem):
    me = lax.axis_index("cz")
    right = lax.rem(me + 1, n)
    left = lax.rem(me + n - 1, n)
    half = x_ref.shape[2] // 2
    piece = x_ref.shape[1] // SUB_CHUNKS
    dest = (right, left)

    barrier = pltpu.get_barrier_semaphore()
    for neighbour in (left, right):
        pl.semaphore_signal(barrier, inc=1, device_id={"cz": neighbour}, device_id_type=MESH_ID)
    pl.semaphore_wait(barrier, 2)

    def link(d, slot, k, src):
        return pltpu.make_async_remote_copy(
            src_ref=src,
            dst_ref=recv.at[d, slot, k],
            send_sem=send_sem.at[d, slot, k],
            recv_sem=recv_sem.at[d, slot, k],
            device_id={"cz": dest[d]},
            device_id_type=MESH_ID,
        )

    sends = []
    for k in range(SUB_CHUNKS):
        for d in range(2):
            first = lax.rem(me + n - 1, n) if d == 0 else lax.rem(me + 1, n)
            copy = link(d, 0, k, x_ref.at[first, pl.ds(k * piece, piece), pl.ds(d * half, half)])
            copy.start()
            sends.append(copy)
    for step in range(n - 1):
        for k in range(SUB_CHUNKS):
            for d in range(2):
                link(d, step, k, sendbuf.at[d, step, k]).wait_recv()
                if d == 0:
                    chunk = lax.rem(me + 2 * n - step - 2, n)
                else:
                    chunk = lax.rem(me + step + 2, n)
                total = recv[d, step, k].astype(jnp.float32) + x_ref[
                    chunk, pl.ds(k * piece, piece), pl.ds(d * half, half)
                ].astype(jnp.float32)
                if step == n - 2:
                    out_ref[pl.ds(k * piece, piece), pl.ds(d * half, half)] = total
                else:
                    sendbuf[d, step, k] = total.astype(sendbuf.dtype)
                    copy = link(d, step + 1, k, sendbuf.at[d, step, k])
                    copy.start()
                    sends.append(copy)
    for copy in sends:
        copy.wait_send()


def zring_reduce_scatter(x, collective_id):
    n, rows, cols = x.shape
    half = cols // 2
    piece = rows // SUB_CHUNKS
    return pl.pallas_call(
        functools.partial(_zring_rs_kernel, n),
        out_shape=jax.ShapeDtypeStruct((rows, cols), jnp.float32),
        in_specs=[pl.BlockSpec(memory_space=pltpu.VMEM)],
        out_specs=pl.BlockSpec(memory_space=pltpu.VMEM),
        scratch_shapes=[
            pltpu.VMEM((2, n - 1, SUB_CHUNKS, piece, half), x.dtype),
            pltpu.VMEM((2, n - 1, SUB_CHUNKS, piece, half), x.dtype),
            pltpu.SemaphoreType.DMA((2, n - 1, SUB_CHUNKS)),
            pltpu.SemaphoreType.DMA((2, n - 1, SUB_CHUNKS)),
        ],
        compiler_params=pltpu.CompilerParams(collective_id=collective_id, has_side_effects=True),
    )(x)


def reduce_scatter_rows(partial, y_size, z_size, collective_id):
    rows, width = partial.shape
    own = rows // (y_size * z_size)
    over_z = zring_reduce_scatter(partial.reshape(z_size, y_size * own, width), collective_id)
    part = over_z.astype(jnp.bfloat16).reshape(y_size, own, width)
    over_y = lax.all_to_all(part, "cy", 0, 0, tiled=True)
    return jnp.sum(over_y.astype(jnp.float32), axis=0)


def gather_rows(x):
    return lax.all_gather(lax.all_gather(x, "cy", axis=0, tiled=True), "cz", axis=0, tiled=True)


def body(
    tokens,
    pick_flags,
    gate_scales,
    attn_gain,
    query_weight,
    key_weight,
    value_matrix,
    output_weight,
    ffn_gain,
    gate_weight,
    up_weight,
    down_weight,
):
    tok_local, width = tokens.shape
    y_size = lax.axis_size("cy")
    z_size = lax.axis_size("cz")
    ctx_size = y_size * z_size
    my_index = lax.axis_index("cy") * z_size + lax.axis_index("cz")
    blk = jnp.arange(ctx_size, dtype=jnp.int32)
    block_dev = (blk % y_size) * z_size + blk // y_size
    picked_count = PICK_DEV * ctx_size
    slots = MOST * ctx_size
    half_pick = PICK_DEV // 2
    half_cycle = ctx_size // 2
    slot_of = jnp.cumsum(pick_flags) - 1
    token_ids = jnp.arange(tok_local, dtype=jnp.int32)
    slot_match = (jnp.arange(MOST, dtype=jnp.int32)[:, None] == slot_of[None, :]) & (
        pick_flags[None, :] == 1
    )
    chosen = jnp.sum(jnp.where(slot_match, token_ids[None, :], 0), axis=1)
    filled = jnp.any(slot_match, axis=1)
    local_index = jnp.where(filled, chosen, -1)
    padded_rows = jnp.where(filled[:, None], tokens[chosen], jnp.zeros((), jnp.bfloat16))
    padded_gate = jnp.where(filled, gate_scales[chosen], jnp.zeros((), jnp.bfloat16))
    lane = jnp.arange(128, dtype=jnp.int32)[None, :]
    extra = jnp.where(
        lane == 0,
        local_index.astype(jnp.bfloat16)[:, None],
        jnp.where(lane == 1, padded_gate[:, None], jnp.zeros((), jnp.bfloat16)),
    )
    packed = jnp.concatenate((padded_rows, extra), axis=1)
    all_packed = lax.all_gather(packed, GROUP, axis=0, tiled=True)
    all_index = all_packed[:, width].astype(jnp.int32)
    slot_filled = all_index >= 0
    counts = jnp.sum(slot_filled.reshape(ctx_size, MOST).astype(jnp.int32), axis=1)
    run_ends = jnp.cumsum(counts)
    run_starts = run_ends - counts
    slot_ids = jnp.arange(slots, dtype=jnp.int32)
    slot_pos = (slot_ids // MOST) * tok_local + all_index
    rope_pos = jnp.where(slot_filled, slot_pos, 0)
    never = jnp.int32(1 << 30)
    mask_pos = jnp.where(slot_filled, slot_pos, never)
    normalized = rms_scale(all_packed[:, :width].astype(jnp.float32), attn_gain).astype(jnp.bfloat16)
    queries = jnp.dot(normalized, query_weight, preferred_element_type=jnp.float32)
    queries = apply_rotary(queries, rope_pos).astype(jnp.bfloat16)
    kv_weight = jnp.concatenate((key_weight, value_matrix), axis=1)
    kv_local = jnp.einsum(
        "pd,dc->cp", normalized, kv_weight, preferred_element_type=jnp.float32
    ).astype(jnp.bfloat16)
    comps = key_weight.shape[1] // KEY_VALUE_HEADS
    query_group_width = QUERY_HEADS // KEY_VALUE_HEADS
    by_head = jnp.transpose(kv_local.reshape(2, comps, KEY_VALUE_HEADS, slots), (2, 0, 1, 3))
    send = jnp.repeat(by_head, query_group_width, axis=0)
    got = lax.all_to_all(send, GROUP, 0, 0, tiled=True)
    key_cols = got[:, 0].reshape(ctx_size * comps, slots)
    value_cols = got[:, 1].reshape(ctx_size * comps, slots)
    keys_here = apply_rotary(key_cols.T.astype(jnp.float32), rope_pos).astype(jnp.bfloat16)
    values_here = value_cols.T
    scores = jnp.dot(queries, keys_here.T, preferred_element_type=jnp.float32) / jnp.sqrt(
        jnp.float32(HEAD_SIZE)
    )
    allowed = mask_pos[None, :] <= mask_pos[:, None]
    scores = jnp.where(allowed, scores, -jnp.inf)
    row_max = jnp.max(scores, axis=1, keepdims=True)
    exp_terms = jnp.exp(scores - row_max)
    prob_bf = (exp_terms / jnp.sum(exp_terms, axis=1, keepdims=True)).astype(jnp.bfloat16)
    head_pad = jnp.dot(prob_bf, values_here, preferred_element_type=jnp.float32).astype(jnp.bfloat16)
    order_ids = jnp.arange(picked_count, dtype=jnp.int32)
    owner_of = order_ids // PICK_DEV
    within = order_ids % PICK_DEV
    low_part = within < half_pick
    rank_block = jnp.where(low_part, owner_of, (owner_of + half_cycle) % ctx_size)
    rank_inner = jnp.where(low_part, 2 * within, 2 * (within - half_pick) + 1)
    rank_ids = rank_block * PICK_DEV + rank_inner
    before = (run_ends[None, :] <= rank_ids[:, None]).astype(jnp.int32)
    source = jnp.sum(before, axis=1)
    offset = rank_ids - jnp.sum(before * counts[None, :], axis=1)
    flat_row = source * MOST + offset
    flat_blocked = flat_row.reshape(ctx_size, PICK_DEV)[block_dev].reshape(picked_count)
    pick_onehot = (flat_blocked[:, None] == slot_ids[None, :]).astype(jnp.bfloat16)
    head_out = jnp.dot(pick_onehot, head_pad, preferred_element_type=jnp.float32).astype(jnp.bfloat16)
    own_start = my_index * PICK_DEV
    own_flat = lax.dynamic_slice_in_dim(flat_row, own_start, PICK_DEV, 0)
    own_packed = all_packed[own_flat]
    own_rows = own_packed[:, :width].astype(jnp.float32)
    scale_own = own_packed[:, width + 1].astype(jnp.float32)
    attn_own = reduce_scatter_rows(
        jnp.dot(head_out, output_weight, preferred_element_type=jnp.float32).astype(jnp.bfloat16),
        y_size,
        z_size,
        0,
    )
    mixed_own = own_rows + attn_own
    normed_own = rms_scale(mixed_own, ffn_gain).astype(jnp.bfloat16)
    normed_ffn = gather_rows(normed_own)
    gate_proj = jnp.dot(normed_ffn, gate_weight, preferred_element_type=jnp.float32)
    up_proj = jnp.dot(normed_ffn, up_weight, preferred_element_type=jnp.float32)
    hidden = (jax.nn.silu(gate_proj) * up_proj).astype(jnp.bfloat16)
    ffn_own = reduce_scatter_rows(
        jnp.dot(hidden, down_weight, preferred_element_type=jnp.float32).astype(jnp.bfloat16),
        y_size,
        z_size,
        1,
    )
    final_own = (own_rows + scale_own[:, None] * (attn_own + ffn_own)).astype(jnp.bfloat16)
    own_source = lax.dynamic_slice_in_dim(source, own_start, PICK_DEV, 0)
    targets = jnp.arange(ctx_size, dtype=jnp.int32)[:, None]
    first_half = (own_source[None, :half_pick] == targets)[:, :, None]
    second_half = (own_source[None, half_pick:] == targets)[:, :, None]
    zero = jnp.zeros((), jnp.bfloat16)
    back = jnp.where(
        first_half,
        final_own[None, :half_pick],
        jnp.where(second_half, final_own[None, half_pick:], zero),
    )
    returned = lax.all_to_all(back, GROUP, 0, 0, tiled=True).reshape(ctx_size * half_pick, width)
    my_start = run_starts[my_index]
    rank_here = jnp.clip(my_start + slot_of, 0, picked_count - 1)
    inner_here = rank_here % PICK_DEV
    odd_here = inner_here % 2
    owner_here = (rank_here // PICK_DEV + odd_here * half_cycle) % ctx_size
    take_rows = owner_here * half_pick + inner_here // 2
    return jnp.where(pick_flags[:, None] == 1, returned[take_rows], tokens)


def solution(mesh):
    dp_size, ctx_size = mesh.devices.shape
    z_size = Z_RUN if ctx_size % Z_RUN == 0 else ctx_size
    split = Mesh(mesh.devices.reshape(dp_size, ctx_size // z_size, z_size), ("dp", "cy", "cz"))
    rows = ("dp", "cy", "cz")
    in_specs = (
        P(rows, None),
        P(rows),
        P(rows),
        P(),
        P(None, GROUP),
        P(None, GROUP),
        P(None, GROUP),
        P(GROUP, None),
        P(),
        P(None, GROUP),
        P(None, GROUP),
        P(GROUP, None),
    )
    out_specs = P(rows, None)
    return jax.shard_map(body, mesh=split, in_specs=in_specs, out_specs=out_specs, check_vma=False)
```

```python
import functools

import jax
import jax.numpy as jnp
from jax import lax
from jax.experimental import pallas as pl
from jax.experimental.pallas import tpu as pltpu
from jax.sharding import Mesh, PartitionSpec as P

QUERY_HEADS = 32
KEY_VALUE_HEADS = 8
HEAD_SIZE = 128
PICK_DEV = 16
MOST = 32
Z_RUN = 8
GROUP = ("cy", "cz")


norm_eps = 1e-05
rope_base = 500000.0


def rms_scale(matrix, gain_vec):
    mean_square = jnp.mean(matrix * matrix, axis=-1, keepdims=True)
    return matrix * lax.rsqrt(mean_square + norm_eps) * gain_vec


def apply_rotary(values, token_positions):
    half_dim = values.shape[-1] // 2
    frequency = rope_base ** (-(jnp.arange(half_dim, dtype=jnp.float32) * 2.0) / values.shape[-1])
    angles = token_positions.astype(jnp.float32)[:, None] * frequency[None, :]
    cosine = jnp.cos(angles)
    sine_part = jnp.sin(angles)
    lower_half = values[..., :half_dim]
    upper_half = values[..., half_dim:]
    return jnp.concatenate(
        (
            lower_half * cosine - upper_half * sine_part,
            upper_half * cosine + lower_half * sine_part,
        ),
        axis=-1,
    )


MESH_ID = pl.DeviceIdType.MESH
SUB_CHUNKS = 2


def _enter(nz, ny):
    me_z = lax.axis_index("cz")
    me_y = lax.axis_index("cy")
    barrier = pltpu.get_barrier_semaphore()
    for neighbour in (lax.rem(me_z + nz - 1, nz), lax.rem(me_z + 1, nz)):
        pl.semaphore_signal(barrier, inc=1, device_id={"cz": neighbour}, device_id_type=MESH_ID)
    for shift in range(1, ny):
        pl.semaphore_signal(barrier, inc=1, device_id={"cy": lax.rem(me_y + shift, ny)}, device_id_type=MESH_ID)
    pl.semaphore_wait(barrier, 2 + ny - 1)
    return me_z, me_y


def _rs_kernel(n, ny, x_ref, out_ref, recv, sendbuf, send_sem, recv_sem, zsum, ybuf, yrecv, ysend_sem, yrecv_sem):
    me, me_y = _enter(n, ny)
    right = lax.rem(me + 1, n)
    left = lax.rem(me + n - 1, n)
    half = x_ref.shape[2] // 2
    piece = x_ref.shape[1] // SUB_CHUNKS
    own = out_ref.shape[0]
    dest = (right, left)

    def link(d, slot, k, src):
        return pltpu.make_async_remote_copy(
            src_ref=src,
            dst_ref=recv.at[d, slot, k],
            send_sem=send_sem.at[d, slot, k],
            recv_sem=recv_sem.at[d, slot, k],
            device_id={"cz": dest[d]},
            device_id_type=MESH_ID,
        )

    sends = []
    for k in range(SUB_CHUNKS):
        for d in range(2):
            first = lax.rem(me + n - 1, n) if d == 0 else lax.rem(me + 1, n)
            copy = link(d, 0, k, x_ref.at[first, pl.ds(k * piece, piece), pl.ds(d * half, half)])
            copy.start()
            sends.append(copy)
    for step in range(n - 1):
        for k in range(SUB_CHUNKS):
            for d in range(2):
                link(d, step, k, sendbuf.at[d, step, k]).wait_recv()
                if d == 0:
                    chunk = lax.rem(me + 2 * n - step - 2, n)
                else:
                    chunk = lax.rem(me + step + 2, n)
                total = recv[d, step, k].astype(jnp.float32) + x_ref[
                    chunk, pl.ds(k * piece, piece), pl.ds(d * half, half)
                ].astype(jnp.float32)
                if step == n - 2:
                    zsum[pl.ds(k * piece, piece), pl.ds(d * half, half)] = total
                else:
                    sendbuf[d, step, k] = total.astype(sendbuf.dtype)
                    copy = link(d, step + 1, k, sendbuf.at[d, step, k])
                    copy.start()
                    sends.append(copy)
    ysends = []
    for shift in range(1, ny):
        peer = lax.rem(me_y + shift, ny)
        ybuf[shift - 1] = zsum[pl.ds(pl.multiple_of(peer * own, own), own), :].astype(ybuf.dtype)
        copy = pltpu.make_async_remote_copy(
            src_ref=ybuf.at[shift - 1],
            dst_ref=yrecv.at[shift - 1],
            send_sem=ysend_sem.at[shift - 1],
            recv_sem=yrecv_sem.at[shift - 1],
            device_id={"cy": peer},
            device_id_type=MESH_ID,
        )
        copy.start()
        ysends.append(copy)
    total = zsum[pl.ds(pl.multiple_of(me_y * own, own), own), :]
    for shift in range(1, ny):
        ysends[shift - 1].wait_recv()
        total = total + yrecv[shift - 1].astype(jnp.float32)
    out_ref[...] = total
    for copy in sends + ysends:
        copy.wait_send()


def reduce_scatter_kernel(x, ny, collective_id):
    n, rows, cols = x.shape
    half = cols // 2
    piece = rows // SUB_CHUNKS
    own = rows // ny
    return pl.pallas_call(
        functools.partial(_rs_kernel, n, ny),
        out_shape=jax.ShapeDtypeStruct((own, cols), jnp.float32),
        in_specs=[pl.BlockSpec(memory_space=pltpu.VMEM)],
        out_specs=pl.BlockSpec(memory_space=pltpu.VMEM),
        scratch_shapes=[
            pltpu.VMEM((2, n - 1, SUB_CHUNKS, piece, half), x.dtype),
            pltpu.VMEM((2, n - 1, SUB_CHUNKS, piece, half), x.dtype),
            pltpu.SemaphoreType.DMA((2, n - 1, SUB_CHUNKS)),
            pltpu.SemaphoreType.DMA((2, n - 1, SUB_CHUNKS)),
            pltpu.VMEM((rows, cols), jnp.float32),
            pltpu.VMEM((ny - 1, own, cols), x.dtype),
            pltpu.VMEM((ny - 1, own, cols), x.dtype),
            pltpu.SemaphoreType.DMA((ny - 1,)),
            pltpu.SemaphoreType.DMA((ny - 1,)),
        ],
        compiler_params=pltpu.CompilerParams(collective_id=collective_id, has_side_effects=True),
    )(x)


def _ag_kernel(n, ny, x_ref, out_ref, own_sem, ysend_sem, yrecv_sem, send_sem, recv_sem):
    me, me_y = _enter(n, ny)
    right = lax.rem(me + 1, n)
    left = lax.rem(me + n - 1, n)
    rows = x_ref.shape[0]
    half = rows // 2
    dest = (right, left)
    mine = pltpu.make_async_copy(x_ref, out_ref.at[me, me_y], own_sem.at[0])
    mine.start()
    ysends = []
    for shift in range(1, ny):
        peer = lax.rem(me_y + shift, ny)
        copy = pltpu.make_async_remote_copy(
            src_ref=x_ref,
            dst_ref=out_ref.at[me, me_y],
            send_sem=ysend_sem.at[shift - 1],
            recv_sem=yrecv_sem.at[me_y],
            device_id={"cy": peer},
            device_id_type=MESH_ID,
        )
        copy.start()
        ysends.append(copy)
    mine.wait()
    for shift in range(1, ny):
        peer = lax.rem(me_y + shift, ny)
        pltpu.make_async_remote_copy(
            src_ref=x_ref,
            dst_ref=out_ref.at[me, peer],
            send_sem=ysend_sem.at[shift - 1],
            recv_sem=yrecv_sem.at[peer],
            device_id={"cy": peer},
            device_id_type=MESH_ID,
        ).wait_recv()

    def link(d, step, idx):
        rows_here = pl.ds(d * half, half)
        return pltpu.make_async_remote_copy(
            src_ref=out_ref.at[idx, :, rows_here],
            dst_ref=out_ref.at[idx, :, rows_here],
            send_sem=send_sem.at[d, step],
            recv_sem=recv_sem.at[d, step],
            device_id={"cz": dest[d]},
            device_id_type=MESH_ID,
        )

    sends = []
    for step in range(n - 1):
        for d in range(2):
            if step > 0:
                got = lax.rem(me + n - step, n) if d == 0 else lax.rem(me + step, n)
                link(d, step - 1, got).wait_recv()
            idx = lax.rem(me + n - step, n) if d == 0 else lax.rem(me + step, n)
            copy = link(d, step, idx)
            copy.start()
            sends.append(copy)
    for d in range(2):
        got = lax.rem(me + 1, n) if d == 0 else lax.rem(me + n - 1, n)
        link(d, n - 2, got).wait_recv()
    for copy in ysends + sends:
        copy.wait_send()


def all_gather_kernel(x, n, ny, collective_id):
    rows, cols = x.shape
    out = pl.pallas_call(
        functools.partial(_ag_kernel, n, ny),
        out_shape=jax.ShapeDtypeStruct((n, ny, rows, cols), x.dtype),
        in_specs=[pl.BlockSpec(memory_space=pltpu.VMEM)],
        out_specs=pl.BlockSpec(memory_space=pltpu.VMEM),
        scratch_shapes=[
            pltpu.SemaphoreType.DMA((1,)),
            pltpu.SemaphoreType.DMA((ny - 1,)),
            pltpu.SemaphoreType.DMA((ny,)),
            pltpu.SemaphoreType.DMA((2, n - 1)),
            pltpu.SemaphoreType.DMA((2, n - 1)),
        ],
        compiler_params=pltpu.CompilerParams(collective_id=collective_id, has_side_effects=True),
    )(x)
    return out.reshape(n * ny * rows, cols)


def body(
    tokens,
    pick_flags,
    gate_scales,
    attn_gain,
    query_weight,
    key_weight,
    value_matrix,
    output_weight,
    ffn_gain,
    gate_weight,
    up_weight,
    down_weight,
):
    tok_local, width = tokens.shape
    y_size = lax.axis_size("cy")
    z_size = lax.axis_size("cz")
    ctx_size = y_size * z_size
    my_index = lax.axis_index("cy") * z_size + lax.axis_index("cz")
    blk = jnp.arange(ctx_size, dtype=jnp.int32)
    block_dev = (blk % y_size) * z_size + blk // y_size
    picked_count = PICK_DEV * ctx_size
    slots = MOST * ctx_size
    half_pick = PICK_DEV // 2
    half_cycle = ctx_size // 2
    slot_of = jnp.cumsum(pick_flags) - 1
    token_ids = jnp.arange(tok_local, dtype=jnp.int32)
    slot_match = (jnp.arange(MOST, dtype=jnp.int32)[:, None] == slot_of[None, :]) & (
        pick_flags[None, :] == 1
    )
    chosen = jnp.sum(jnp.where(slot_match, token_ids[None, :], 0), axis=1)
    filled = jnp.any(slot_match, axis=1)
    local_index = jnp.where(filled, chosen, -1)
    padded_rows = jnp.where(filled[:, None], tokens[chosen], jnp.zeros((), jnp.bfloat16))
    padded_gate = jnp.where(filled, gate_scales[chosen], jnp.zeros((), jnp.bfloat16))
    lane = jnp.arange(128, dtype=jnp.int32)[None, :]
    extra = jnp.where(
        lane == 0,
        local_index.astype(jnp.bfloat16)[:, None],
        jnp.where(lane == 1, padded_gate[:, None], jnp.zeros((), jnp.bfloat16)),
    )
    packed = jnp.concatenate((padded_rows, extra), axis=1)
    all_packed = lax.all_gather(packed, GROUP, axis=0, tiled=True)
    all_index = all_packed[:, width].astype(jnp.int32)
    slot_filled = all_index >= 0
    counts = jnp.sum(slot_filled.reshape(ctx_size, MOST).astype(jnp.int32), axis=1)
    run_ends = jnp.cumsum(counts)
    run_starts = run_ends - counts
    slot_ids = jnp.arange(slots, dtype=jnp.int32)
    slot_pos = (slot_ids // MOST) * tok_local + all_index
    rope_pos = jnp.where(slot_filled, slot_pos, 0)
    never = jnp.int32(1 << 30)
    mask_pos = jnp.where(slot_filled, slot_pos, never)
    normalized = rms_scale(all_packed[:, :width].astype(jnp.float32), attn_gain).astype(jnp.bfloat16)
    queries = jnp.dot(normalized, query_weight, preferred_element_type=jnp.float32)
    queries = apply_rotary(queries, rope_pos).astype(jnp.bfloat16)
    kv_weight = jnp.concatenate((key_weight, value_matrix), axis=1)
    kv_local = jnp.einsum(
        "pd,dc->cp", normalized, kv_weight, preferred_element_type=jnp.float32
    ).astype(jnp.bfloat16)
    comps = key_weight.shape[1] // KEY_VALUE_HEADS
    query_group_width = QUERY_HEADS // KEY_VALUE_HEADS
    by_head = jnp.transpose(kv_local.reshape(2, comps, KEY_VALUE_HEADS, slots), (2, 0, 1, 3))
    send = jnp.repeat(by_head, query_group_width, axis=0)
    got = lax.all_to_all(send, GROUP, 0, 0, tiled=True)
    key_cols = got[:, 0].reshape(ctx_size * comps, slots)
    value_cols = got[:, 1].reshape(ctx_size * comps, slots)
    keys_here = apply_rotary(key_cols.T.astype(jnp.float32), rope_pos).astype(jnp.bfloat16)
    values_here = value_cols.T
    scores = jnp.dot(queries, keys_here.T, preferred_element_type=jnp.float32) / jnp.sqrt(
        jnp.float32(HEAD_SIZE)
    )
    allowed = mask_pos[None, :] <= mask_pos[:, None]
    scores = jnp.where(allowed, scores, -jnp.inf)
    row_max = jnp.max(scores, axis=1, keepdims=True)
    exp_terms = jnp.exp(scores - row_max)
    prob_bf = (exp_terms / jnp.sum(exp_terms, axis=1, keepdims=True)).astype(jnp.bfloat16)
    head_pad = jnp.dot(prob_bf, values_here, preferred_element_type=jnp.float32).astype(jnp.bfloat16)
    order_ids = jnp.arange(picked_count, dtype=jnp.int32)
    owner_of = order_ids // PICK_DEV
    within = order_ids % PICK_DEV
    low_part = within < half_pick
    rank_block = jnp.where(low_part, owner_of, (owner_of + half_cycle) % ctx_size)
    rank_inner = jnp.where(low_part, 2 * within, 2 * (within - half_pick) + 1)
    rank_ids = rank_block * PICK_DEV + rank_inner
    before = (run_ends[None, :] <= rank_ids[:, None]).astype(jnp.int32)
    source = jnp.sum(before, axis=1)
    offset = rank_ids - jnp.sum(before * counts[None, :], axis=1)
    flat_row = source * MOST + offset
    flat_blocked = flat_row.reshape(ctx_size, PICK_DEV)[block_dev].reshape(picked_count)
    pick_onehot = (flat_blocked[:, None] == slot_ids[None, :]).astype(jnp.bfloat16)
    head_out = jnp.dot(pick_onehot, head_pad, preferred_element_type=jnp.float32).astype(jnp.bfloat16)
    own_start = my_index * PICK_DEV
    own_flat = lax.dynamic_slice_in_dim(flat_row, own_start, PICK_DEV, 0)
    own_packed = all_packed[own_flat]
    own_rows = own_packed[:, :width].astype(jnp.float32)
    scale_own = own_packed[:, width + 1].astype(jnp.float32)
    attn_partial = jnp.dot(head_out, output_weight, preferred_element_type=jnp.float32).astype(jnp.bfloat16)
    attn_own = reduce_scatter_kernel(attn_partial.reshape(z_size, y_size * PICK_DEV, width), y_size, 0)
    mixed_own = own_rows + attn_own
    normed_own = rms_scale(mixed_own, ffn_gain).astype(jnp.bfloat16)
    normed_ffn = all_gather_kernel(normed_own, z_size, y_size, 2)
    gate_proj = jnp.dot(normed_ffn, gate_weight, preferred_element_type=jnp.float32)
    up_proj = jnp.dot(normed_ffn, up_weight, preferred_element_type=jnp.float32)
    hidden = (jax.nn.silu(gate_proj) * up_proj).astype(jnp.bfloat16)
    ffn_partial = jnp.dot(hidden, down_weight, preferred_element_type=jnp.float32).astype(jnp.bfloat16)
    ffn_own = reduce_scatter_kernel(ffn_partial.reshape(z_size, y_size * PICK_DEV, width), y_size, 1)
    final_own = (own_rows + scale_own[:, None] * (attn_own + ffn_own)).astype(jnp.bfloat16)
    own_source = lax.dynamic_slice_in_dim(source, own_start, PICK_DEV, 0)
    targets = jnp.arange(ctx_size, dtype=jnp.int32)[:, None]
    first_half = (own_source[None, :half_pick] == targets)[:, :, None]
    second_half = (own_source[None, half_pick:] == targets)[:, :, None]
    zero = jnp.zeros((), jnp.bfloat16)
    back = jnp.where(
        first_half,
        final_own[None, :half_pick],
        jnp.where(second_half, final_own[None, half_pick:], zero),
    )
    returned = lax.all_to_all(back, GROUP, 0, 0, tiled=True).reshape(ctx_size * half_pick, width)
    my_start = run_starts[my_index]
    rank_here = jnp.clip(my_start + slot_of, 0, picked_count - 1)
    inner_here = rank_here % PICK_DEV
    odd_here = inner_here % 2
    owner_here = (rank_here // PICK_DEV + odd_here * half_cycle) % ctx_size
    take_rows = owner_here * half_pick + inner_here // 2
    return jnp.where(pick_flags[:, None] == 1, returned[take_rows], tokens)


def solution(mesh):
    dp_size, ctx_size = mesh.devices.shape
    z_size = Z_RUN if ctx_size % Z_RUN == 0 else ctx_size
    split = Mesh(mesh.devices.reshape(dp_size, ctx_size // z_size, z_size), ("dp", "cy", "cz"))
    rows = ("dp", "cy", "cz")
    in_specs = (
        P(rows, None),
        P(rows),
        P(rows),
        P(),
        P(None, GROUP),
        P(None, GROUP),
        P(None, GROUP),
        P(GROUP, None),
        P(),
        P(None, GROUP),
        P(None, GROUP),
        P(GROUP, None),
    )
    out_specs = P(rows, None)
    return jax.shard_map(body, mesh=split, in_specs=in_specs, out_specs=out_specs, check_vma=False)
```

```python
import functools

import jax
import jax.numpy as jnp
from jax import lax
from jax.experimental import pallas as pl
from jax.experimental.pallas import tpu as pltpu
from jax.sharding import Mesh, PartitionSpec as P

QUERY_HEADS = 32
KEY_VALUE_HEADS = 8
HEAD_SIZE = 128
PICK_DEV = 16
MOST = 32
Z_RUN = 8
GROUP = ("cy", "cz")


norm_eps = 1e-05
rope_base = 500000.0


def rms_scale(matrix, gain_vec):
    mean_square = jnp.mean(matrix * matrix, axis=-1, keepdims=True)
    return matrix * lax.rsqrt(mean_square + norm_eps) * gain_vec


def apply_rotary(values, token_positions):
    half_dim = values.shape[-1] // 2
    frequency = rope_base ** (-(jnp.arange(half_dim, dtype=jnp.float32) * 2.0) / values.shape[-1])
    angles = token_positions.astype(jnp.float32)[:, None] * frequency[None, :]
    cosine = jnp.cos(angles)
    sine_part = jnp.sin(angles)
    lower_half = values[..., :half_dim]
    upper_half = values[..., half_dim:]
    return jnp.concatenate(
        (
            lower_half * cosine - upper_half * sine_part,
            upper_half * cosine + lower_half * sine_part,
        ),
        axis=-1,
    )


MESH_ID = pl.DeviceIdType.MESH
SUB_CHUNKS = 2


def _enter(nz, ny):
    me_z = lax.axis_index("cz")
    me_y = lax.axis_index("cy")
    barrier = pltpu.get_barrier_semaphore()
    for neighbour in (lax.rem(me_z + nz - 1, nz), lax.rem(me_z + 1, nz)):
        pl.semaphore_signal(barrier, inc=1, device_id={"cz": neighbour}, device_id_type=MESH_ID)
    for shift in range(1, ny):
        pl.semaphore_signal(barrier, inc=1, device_id={"cy": lax.rem(me_y + shift, ny)}, device_id_type=MESH_ID)
    pl.semaphore_wait(barrier, 2 + ny - 1)
    return me_z, me_y


def _rs_kernel(n, ny, x_ref, out_ref, recv, sendbuf, send_sem, recv_sem, zsum, ybuf, yrecv, ysend_sem, yrecv_sem):
    me, me_y = _enter(n, ny)
    right = lax.rem(me + 1, n)
    left = lax.rem(me + n - 1, n)
    half = x_ref.shape[2] // 2
    piece = x_ref.shape[1] // SUB_CHUNKS
    own = out_ref.shape[0]
    dest = (right, left)

    def link(d, slot, k, src):
        return pltpu.make_async_remote_copy(
            src_ref=src,
            dst_ref=recv.at[d, slot, k],
            send_sem=send_sem.at[d, slot, k],
            recv_sem=recv_sem.at[d, slot, k],
            device_id={"cz": dest[d]},
            device_id_type=MESH_ID,
        )

    sends = []
    for k in range(SUB_CHUNKS):
        for d in range(2):
            first = lax.rem(me + n - 1, n) if d == 0 else lax.rem(me + 1, n)
            copy = link(d, 0, k, x_ref.at[first, pl.ds(k * piece, piece), pl.ds(d * half, half)])
            copy.start()
            sends.append(copy)
    for step in range(n - 1):
        for k in range(SUB_CHUNKS):
            for d in range(2):
                link(d, step, k, sendbuf.at[d, step, k]).wait_recv()
                if d == 0:
                    chunk = lax.rem(me + 2 * n - step - 2, n)
                else:
                    chunk = lax.rem(me + step + 2, n)
                total = recv[d, step, k].astype(jnp.float32) + x_ref[
                    chunk, pl.ds(k * piece, piece), pl.ds(d * half, half)
                ].astype(jnp.float32)
                if step == n - 2:
                    zsum[pl.ds(k * piece, piece), pl.ds(d * half, half)] = total
                else:
                    sendbuf[d, step, k] = total.astype(sendbuf.dtype)
                    copy = link(d, step + 1, k, sendbuf.at[d, step, k])
                    copy.start()
                    sends.append(copy)
    ysends = []
    for shift in range(1, ny):
        peer = lax.rem(me_y + shift, ny)
        ybuf[shift - 1] = zsum[pl.ds(pl.multiple_of(peer * own, own), own), :].astype(ybuf.dtype)
        copy = pltpu.make_async_remote_copy(
            src_ref=ybuf.at[shift - 1],
            dst_ref=yrecv.at[shift - 1],
            send_sem=ysend_sem.at[shift - 1],
            recv_sem=yrecv_sem.at[shift - 1],
            device_id={"cy": peer},
            device_id_type=MESH_ID,
        )
        copy.start()
        ysends.append(copy)
    total = zsum[pl.ds(pl.multiple_of(me_y * own, own), own), :]
    for shift in range(1, ny):
        ysends[shift - 1].wait_recv()
        total = total + yrecv[shift - 1].astype(jnp.float32)
    out_ref[...] = total
    for copy in sends + ysends:
        copy.wait_send()


def reduce_scatter_kernel(x, ny, collective_id):
    n, rows, cols = x.shape
    half = cols // 2
    piece = rows // SUB_CHUNKS
    own = rows // ny
    return pl.pallas_call(
        functools.partial(_rs_kernel, n, ny),
        out_shape=jax.ShapeDtypeStruct((own, cols), jnp.float32),
        in_specs=[pl.BlockSpec(memory_space=pltpu.VMEM)],
        out_specs=pl.BlockSpec(memory_space=pltpu.VMEM),
        scratch_shapes=[
            pltpu.VMEM((2, n - 1, SUB_CHUNKS, piece, half), x.dtype),
            pltpu.VMEM((2, n - 1, SUB_CHUNKS, piece, half), x.dtype),
            pltpu.SemaphoreType.DMA((2, n - 1, SUB_CHUNKS)),
            pltpu.SemaphoreType.DMA((2, n - 1, SUB_CHUNKS)),
            pltpu.VMEM((rows, cols), jnp.float32),
            pltpu.VMEM((ny - 1, own, cols), x.dtype),
            pltpu.VMEM((ny - 1, own, cols), x.dtype),
            pltpu.SemaphoreType.DMA((ny - 1,)),
            pltpu.SemaphoreType.DMA((ny - 1,)),
        ],
        compiler_params=pltpu.CompilerParams(collective_id=collective_id, has_side_effects=True),
    )(x)


def _ag_kernel(n, ny, x_ref, out_ref, own_sem, ysend_sem, yrecv_sem, send_sem, recv_sem):
    me, me_y = _enter(n, ny)
    right = lax.rem(me + 1, n)
    left = lax.rem(me + n - 1, n)
    rows = x_ref.shape[0]
    half = rows // 2
    dest = (right, left)
    mine = pltpu.make_async_copy(x_ref, out_ref.at[me, me_y], own_sem.at[0])
    mine.start()
    ysends = []
    for shift in range(1, ny):
        peer = lax.rem(me_y + shift, ny)
        copy = pltpu.make_async_remote_copy(
            src_ref=x_ref,
            dst_ref=out_ref.at[me, me_y],
            send_sem=ysend_sem.at[shift - 1],
            recv_sem=yrecv_sem.at[me_y],
            device_id={"cy": peer},
            device_id_type=MESH_ID,
        )
        copy.start()
        ysends.append(copy)
    mine.wait()
    for shift in range(1, ny):
        peer = lax.rem(me_y + shift, ny)
        pltpu.make_async_remote_copy(
            src_ref=x_ref,
            dst_ref=out_ref.at[me, peer],
            send_sem=ysend_sem.at[shift - 1],
            recv_sem=yrecv_sem.at[peer],
            device_id={"cy": peer},
            device_id_type=MESH_ID,
        ).wait_recv()

    def link(d, step, idx):
        rows_here = pl.ds(d * half, half)
        return pltpu.make_async_remote_copy(
            src_ref=out_ref.at[idx, :, rows_here],
            dst_ref=out_ref.at[idx, :, rows_here],
            send_sem=send_sem.at[d, step],
            recv_sem=recv_sem.at[d, step],
            device_id={"cz": dest[d]},
            device_id_type=MESH_ID,
        )

    sends = []
    for step in range(n - 1):
        for d in range(2):
            if step > 0:
                got = lax.rem(me + n - step, n) if d == 0 else lax.rem(me + step, n)
                link(d, step - 1, got).wait_recv()
            idx = lax.rem(me + n - step, n) if d == 0 else lax.rem(me + step, n)
            copy = link(d, step, idx)
            copy.start()
            sends.append(copy)
    for d in range(2):
        got = lax.rem(me + 1, n) if d == 0 else lax.rem(me + n - 1, n)
        link(d, n - 2, got).wait_recv()
    for copy in ysends + sends:
        copy.wait_send()


def all_gather_kernel(x, n, ny, collective_id):
    rows, cols = x.shape
    out = pl.pallas_call(
        functools.partial(_ag_kernel, n, ny),
        out_shape=jax.ShapeDtypeStruct((n, ny, rows, cols), x.dtype),
        in_specs=[pl.BlockSpec(memory_space=pltpu.VMEM)],
        out_specs=pl.BlockSpec(memory_space=pltpu.VMEM),
        scratch_shapes=[
            pltpu.SemaphoreType.DMA((1,)),
            pltpu.SemaphoreType.DMA((ny - 1,)),
            pltpu.SemaphoreType.DMA((ny,)),
            pltpu.SemaphoreType.DMA((2, n - 1)),
            pltpu.SemaphoreType.DMA((2, n - 1)),
        ],
        compiler_params=pltpu.CompilerParams(collective_id=collective_id, has_side_effects=True),
    )(x)
    return out.reshape(n * ny * rows, cols)


def body(
    tokens,
    pick_flags,
    gate_scales,
    attn_gain,
    query_weight,
    key_weight,
    value_matrix,
    output_weight,
    ffn_gain,
    gate_weight,
    up_weight,
    down_weight,
):
    tok_local, width = tokens.shape
    y_size = lax.axis_size("cy")
    z_size = lax.axis_size("cz")
    ctx_size = y_size * z_size
    my_index = lax.axis_index("cy") * z_size + lax.axis_index("cz")
    blk = jnp.arange(ctx_size, dtype=jnp.int32)
    block_dev = (blk % y_size) * z_size + blk // y_size
    picked_count = PICK_DEV * ctx_size
    slots = MOST * ctx_size
    half_pick = PICK_DEV // 2
    half_cycle = ctx_size // 2
    slot_of = jnp.cumsum(pick_flags) - 1
    token_ids = jnp.arange(tok_local, dtype=jnp.int32)
    slot_match = (jnp.arange(MOST, dtype=jnp.int32)[:, None] == slot_of[None, :]) & (
        pick_flags[None, :] == 1
    )
    chosen = jnp.sum(jnp.where(slot_match, token_ids[None, :], 0), axis=1)
    filled = jnp.any(slot_match, axis=1)
    local_index = jnp.where(filled, chosen, -1)
    padded_rows = jnp.where(filled[:, None], tokens[chosen], jnp.zeros((), jnp.bfloat16))
    padded_gate = jnp.where(filled, gate_scales[chosen], jnp.zeros((), jnp.bfloat16))
    lane = jnp.arange(128, dtype=jnp.int32)[None, :]
    extra = jnp.where(
        lane == 0,
        local_index.astype(jnp.bfloat16)[:, None],
        jnp.where(lane == 1, padded_gate[:, None], jnp.zeros((), jnp.bfloat16)),
    )
    packed = jnp.concatenate((padded_rows, extra), axis=1)
    lead = MOST // 2
    first_part = lax.all_gather(packed[:lead], GROUP, axis=0, tiled=True)
    second_part = all_gather_kernel(packed[lead:], z_size, y_size, 3)
    all_packed = jnp.concatenate((first_part, second_part), axis=0)
    slot_ids = jnp.arange(slots, dtype=jnp.int32)
    part_blk = (slot_ids % (slots // 2)) // lead
    slot_dev = jnp.where(slot_ids < slots // 2, part_blk, block_dev[part_blk])
    all_index = all_packed[:, width].astype(jnp.int32)
    slot_filled = all_index >= 0
    per_part = jnp.sum(slot_filled.reshape(2, ctx_size, lead).astype(jnp.int32), axis=2)
    dev_ids = jnp.arange(ctx_size, dtype=jnp.int32)
    dev_block = (dev_ids % z_size) * y_size + dev_ids // z_size
    counts = per_part[0] + per_part[1][dev_block]
    run_ends = jnp.cumsum(counts)
    run_starts = run_ends - counts
    slot_pos = slot_dev * tok_local + all_index
    rope_pos = jnp.where(slot_filled, slot_pos, 0)
    never = jnp.int32(1 << 30)
    mask_pos = jnp.where(slot_filled, slot_pos, never)
    normalized = rms_scale(all_packed[:, :width].astype(jnp.float32), attn_gain).astype(jnp.bfloat16)
    queries = jnp.dot(normalized, query_weight, preferred_element_type=jnp.float32)
    queries = apply_rotary(queries, rope_pos).astype(jnp.bfloat16)
    kv_weight = jnp.concatenate((key_weight, value_matrix), axis=1)
    kv_local = jnp.einsum(
        "pd,dc->cp", normalized, kv_weight, preferred_element_type=jnp.float32
    ).astype(jnp.bfloat16)
    comps = key_weight.shape[1] // KEY_VALUE_HEADS
    query_group_width = QUERY_HEADS // KEY_VALUE_HEADS
    by_head = jnp.transpose(kv_local.reshape(2, comps, KEY_VALUE_HEADS, slots), (2, 0, 1, 3))
    send = jnp.repeat(by_head, query_group_width, axis=0)
    got = lax.all_to_all(send, GROUP, 0, 0, tiled=True)
    key_cols = got[:, 0].reshape(ctx_size * comps, slots)
    value_cols = got[:, 1].reshape(ctx_size * comps, slots)
    keys_here = apply_rotary(key_cols.T.astype(jnp.float32), rope_pos).astype(jnp.bfloat16)
    values_here = value_cols.T
    scores = jnp.dot(queries, keys_here.T, preferred_element_type=jnp.float32) / jnp.sqrt(
        jnp.float32(HEAD_SIZE)
    )
    allowed = mask_pos[None, :] <= mask_pos[:, None]
    scores = jnp.where(allowed, scores, -jnp.inf)
    row_max = jnp.max(scores, axis=1, keepdims=True)
    exp_terms = jnp.exp(scores - row_max)
    prob_bf = (exp_terms / jnp.sum(exp_terms, axis=1, keepdims=True)).astype(jnp.bfloat16)
    head_pad = jnp.dot(prob_bf, values_here, preferred_element_type=jnp.float32).astype(jnp.bfloat16)
    order_ids = jnp.arange(picked_count, dtype=jnp.int32)
    owner_of = order_ids // PICK_DEV
    within = order_ids % PICK_DEV
    low_part = within < half_pick
    rank_block = jnp.where(low_part, owner_of, (owner_of + half_cycle) % ctx_size)
    rank_inner = jnp.where(low_part, 2 * within, 2 * (within - half_pick) + 1)
    rank_ids = rank_block * PICK_DEV + rank_inner
    before = (run_ends[None, :] <= rank_ids[:, None]).astype(jnp.int32)
    source = jnp.sum(before, axis=1)
    offset = rank_ids - jnp.sum(before * counts[None, :], axis=1)
    source_block = (source % z_size) * y_size + source // z_size
    flat_row = jnp.where(
        offset < lead, source * lead + offset, slots // 2 + source_block * lead + offset - lead
    )
    flat_blocked = flat_row.reshape(ctx_size, PICK_DEV)[block_dev].reshape(picked_count)
    pick_onehot = (flat_blocked[:, None] == slot_ids[None, :]).astype(jnp.bfloat16)
    head_out = jnp.dot(pick_onehot, head_pad, preferred_element_type=jnp.float32).astype(jnp.bfloat16)
    own_start = my_index * PICK_DEV
    own_flat = lax.dynamic_slice_in_dim(flat_row, own_start, PICK_DEV, 0)
    own_packed = all_packed[own_flat]
    own_rows = own_packed[:, :width].astype(jnp.float32)
    scale_own = own_packed[:, width + 1].astype(jnp.float32)
    attn_partial = jnp.dot(head_out, output_weight, preferred_element_type=jnp.float32).astype(jnp.bfloat16)
    attn_own = reduce_scatter_kernel(attn_partial.reshape(z_size, y_size * PICK_DEV, width), y_size, 0)
    mixed_own = own_rows + attn_own
    normed_own = rms_scale(mixed_own, ffn_gain).astype(jnp.bfloat16)
    normed_ffn = all_gather_kernel(normed_own, z_size, y_size, 2)
    gate_proj = jnp.dot(normed_ffn, gate_weight, preferred_element_type=jnp.float32)
    up_proj = jnp.dot(normed_ffn, up_weight, preferred_element_type=jnp.float32)
    hidden = (jax.nn.silu(gate_proj) * up_proj).astype(jnp.bfloat16)
    ffn_partial = jnp.dot(hidden, down_weight, preferred_element_type=jnp.float32).astype(jnp.bfloat16)
    ffn_own = reduce_scatter_kernel(ffn_partial.reshape(z_size, y_size * PICK_DEV, width), y_size, 1)
    final_own = (own_rows + scale_own[:, None] * (attn_own + ffn_own)).astype(jnp.bfloat16)
    own_source = lax.dynamic_slice_in_dim(source, own_start, PICK_DEV, 0)
    targets = jnp.arange(ctx_size, dtype=jnp.int32)[:, None]
    first_half = (own_source[None, :half_pick] == targets)[:, :, None]
    second_half = (own_source[None, half_pick:] == targets)[:, :, None]
    zero = jnp.zeros((), jnp.bfloat16)
    back = jnp.where(
        first_half,
        final_own[None, :half_pick],
        jnp.where(second_half, final_own[None, half_pick:], zero),
    )
    returned = lax.all_to_all(back, GROUP, 0, 0, tiled=True).reshape(ctx_size * half_pick, width)
    my_start = run_starts[my_index]
    rank_here = jnp.clip(my_start + slot_of, 0, picked_count - 1)
    inner_here = rank_here % PICK_DEV
    odd_here = inner_here % 2
    owner_here = (rank_here // PICK_DEV + odd_here * half_cycle) % ctx_size
    take_rows = owner_here * half_pick + inner_here // 2
    return jnp.where(pick_flags[:, None] == 1, returned[take_rows], tokens)


def solution(mesh):
    dp_size, ctx_size = mesh.devices.shape
    z_size = Z_RUN if ctx_size % Z_RUN == 0 else ctx_size
    split = Mesh(mesh.devices.reshape(dp_size, ctx_size // z_size, z_size), ("dp", "cy", "cz"))
    rows = ("dp", "cy", "cz")
    in_specs = (
        P(rows, None),
        P(rows),
        P(rows),
        P(),
        P(None, GROUP),
        P(None, GROUP),
        P(None, GROUP),
        P(GROUP, None),
        P(),
        P(None, GROUP),
        P(None, GROUP),
        P(GROUP, None),
    )
    out_specs = P(rows, None)
    return jax.shard_map(body, mesh=split, in_specs=in_specs, out_specs=out_specs, check_vma=False)
```

```python
import functools

import jax
import jax.numpy as jnp
from jax import lax
from jax.experimental import pallas as pl
from jax.experimental.pallas import tpu as pltpu
from jax.sharding import Mesh, PartitionSpec as P

QUERY_HEADS = 32
KEY_VALUE_HEADS = 8
HEAD_SIZE = 128
PICK_DEV = 16
MOST = 32
Z_RUN = 8
GROUP = ("cy", "cz")


norm_eps = 1e-05
rope_base = 500000.0


def rms_scale(matrix, gain_vec):
    mean_square = jnp.mean(matrix * matrix, axis=-1, keepdims=True)
    return matrix * lax.rsqrt(mean_square + norm_eps) * gain_vec


def apply_rotary(values, token_positions):
    half_dim = values.shape[-1] // 2
    frequency = rope_base ** (-(jnp.arange(half_dim, dtype=jnp.float32) * 2.0) / values.shape[-1])
    angles = token_positions.astype(jnp.float32)[:, None] * frequency[None, :]
    cosine = jnp.cos(angles)
    sine_part = jnp.sin(angles)
    lower_half = values[..., :half_dim]
    upper_half = values[..., half_dim:]
    return jnp.concatenate(
        (
            lower_half * cosine - upper_half * sine_part,
            upper_half * cosine + lower_half * sine_part,
        ),
        axis=-1,
    )


MESH_ID = pl.DeviceIdType.MESH
SUB_CHUNKS = 2


def _enter(nz, ny):
    me_z = lax.axis_index("cz")
    me_y = lax.axis_index("cy")
    barrier = pltpu.get_barrier_semaphore()
    for neighbour in (lax.rem(me_z + nz - 1, nz), lax.rem(me_z + 1, nz)):
        pl.semaphore_signal(barrier, inc=1, device_id={"cz": neighbour}, device_id_type=MESH_ID)
    for shift in range(1, ny):
        pl.semaphore_signal(barrier, inc=1, device_id={"cy": lax.rem(me_y + shift, ny)}, device_id_type=MESH_ID)
    pl.semaphore_wait(barrier, 2 + ny - 1)
    return me_z, me_y


def _rs_kernel(n, ny, x_ref, out_ref, recv, sendbuf, send_sem, recv_sem, zsum, ybuf, yrecv, ysend_sem, yrecv_sem):
    me, me_y = _enter(n, ny)
    right = lax.rem(me + 1, n)
    left = lax.rem(me + n - 1, n)
    half = x_ref.shape[2] // 2
    piece = x_ref.shape[1] // SUB_CHUNKS
    own = out_ref.shape[0]
    dest = (right, left)

    def link(d, slot, k, src):
        return pltpu.make_async_remote_copy(
            src_ref=src,
            dst_ref=recv.at[d, slot, k],
            send_sem=send_sem.at[d, slot, k],
            recv_sem=recv_sem.at[d, slot, k],
            device_id={"cz": dest[d]},
            device_id_type=MESH_ID,
        )

    sends = []
    for k in range(SUB_CHUNKS):
        for d in range(2):
            first = lax.rem(me + n - 1, n) if d == 0 else lax.rem(me + 1, n)
            copy = link(d, 0, k, x_ref.at[first, pl.ds(k * piece, piece), pl.ds(d * half, half)])
            copy.start()
            sends.append(copy)
    for step in range(n - 1):
        for k in range(SUB_CHUNKS):
            for d in range(2):
                link(d, step, k, sendbuf.at[d, step, k]).wait_recv()
                if d == 0:
                    chunk = lax.rem(me + 2 * n - step - 2, n)
                else:
                    chunk = lax.rem(me + step + 2, n)
                total = recv[d, step, k].astype(jnp.float32) + x_ref[
                    chunk, pl.ds(k * piece, piece), pl.ds(d * half, half)
                ].astype(jnp.float32)
                if step == n - 2:
                    zsum[pl.ds(k * piece, piece), pl.ds(d * half, half)] = total
                else:
                    sendbuf[d, step, k] = total.astype(sendbuf.dtype)
                    copy = link(d, step + 1, k, sendbuf.at[d, step, k])
                    copy.start()
                    sends.append(copy)
    ysends = []
    for shift in range(1, ny):
        peer = lax.rem(me_y + shift, ny)
        ybuf[shift - 1] = zsum[pl.ds(pl.multiple_of(peer * own, own), own), :].astype(ybuf.dtype)
        copy = pltpu.make_async_remote_copy(
            src_ref=ybuf.at[shift - 1],
            dst_ref=yrecv.at[shift - 1],
            send_sem=ysend_sem.at[shift - 1],
            recv_sem=yrecv_sem.at[shift - 1],
            device_id={"cy": peer},
            device_id_type=MESH_ID,
        )
        copy.start()
        ysends.append(copy)
    total = zsum[pl.ds(pl.multiple_of(me_y * own, own), own), :]
    for shift in range(1, ny):
        ysends[shift - 1].wait_recv()
        total = total + yrecv[shift - 1].astype(jnp.float32)
    out_ref[...] = total
    for copy in sends + ysends:
        copy.wait_send()


def reduce_scatter_kernel(x, ny, collective_id):
    n, rows, cols = x.shape
    half = cols // 2
    piece = rows // SUB_CHUNKS
    own = rows // ny
    return pl.pallas_call(
        functools.partial(_rs_kernel, n, ny),
        out_shape=jax.ShapeDtypeStruct((own, cols), jnp.float32),
        in_specs=[pl.BlockSpec(memory_space=pltpu.VMEM)],
        out_specs=pl.BlockSpec(memory_space=pltpu.VMEM),
        scratch_shapes=[
            pltpu.VMEM((2, n - 1, SUB_CHUNKS, piece, half), x.dtype),
            pltpu.VMEM((2, n - 1, SUB_CHUNKS, piece, half), x.dtype),
            pltpu.SemaphoreType.DMA((2, n - 1, SUB_CHUNKS)),
            pltpu.SemaphoreType.DMA((2, n - 1, SUB_CHUNKS)),
            pltpu.VMEM((rows, cols), jnp.float32),
            pltpu.VMEM((ny - 1, own, cols), x.dtype),
            pltpu.VMEM((ny - 1, own, cols), x.dtype),
            pltpu.SemaphoreType.DMA((ny - 1,)),
            pltpu.SemaphoreType.DMA((ny - 1,)),
        ],
        compiler_params=pltpu.CompilerParams(collective_id=collective_id, has_side_effects=True),
    )(x)


def _ag_kernel(n, ny, x_ref, out_ref, own_sem, ysend_sem, yrecv_sem, send_sem, recv_sem):
    me, me_y = _enter(n, ny)
    right = lax.rem(me + 1, n)
    left = lax.rem(me + n - 1, n)
    rows = x_ref.shape[0]
    half = rows // 2
    dest = (right, left)
    mine = pltpu.make_async_copy(x_ref, out_ref.at[me, me_y], own_sem.at[0])
    mine.start()
    ysends = []
    for shift in range(1, ny):
        peer = lax.rem(me_y + shift, ny)
        copy = pltpu.make_async_remote_copy(
            src_ref=x_ref,
            dst_ref=out_ref.at[me, me_y],
            send_sem=ysend_sem.at[shift - 1],
            recv_sem=yrecv_sem.at[me_y],
            device_id={"cy": peer},
            device_id_type=MESH_ID,
        )
        copy.start()
        ysends.append(copy)
    mine.wait()
    for shift in range(1, ny):
        peer = lax.rem(me_y + shift, ny)
        pltpu.make_async_remote_copy(
            src_ref=x_ref,
            dst_ref=out_ref.at[me, peer],
            send_sem=ysend_sem.at[shift - 1],
            recv_sem=yrecv_sem.at[peer],
            device_id={"cy": peer},
            device_id_type=MESH_ID,
        ).wait_recv()

    def link(d, step, k, idx):
        rows_here = pl.ds(d * half, half)
        blocks = pl.ds(k * (ny // SUB_CHUNKS), ny // SUB_CHUNKS)
        return pltpu.make_async_remote_copy(
            src_ref=out_ref.at[idx, blocks, rows_here],
            dst_ref=out_ref.at[idx, blocks, rows_here],
            send_sem=send_sem.at[d, step, k],
            recv_sem=recv_sem.at[d, step, k],
            device_id={"cz": dest[d]},
            device_id_type=MESH_ID,
        )

    sends = []
    for step in range(n - 1):
        for k in range(SUB_CHUNKS):
            for d in range(2):
                if step > 0:
                    got = lax.rem(me + n - step, n) if d == 0 else lax.rem(me + step, n)
                    link(d, step - 1, k, got).wait_recv()
                idx = lax.rem(me + n - step, n) if d == 0 else lax.rem(me + step, n)
                copy = link(d, step, k, idx)
                copy.start()
                sends.append(copy)
    for k in range(SUB_CHUNKS):
        for d in range(2):
            got = lax.rem(me + 1, n) if d == 0 else lax.rem(me + n - 1, n)
            link(d, n - 2, k, got).wait_recv()
    for copy in ysends + sends:
        copy.wait_send()


def all_gather_kernel(x, n, ny, collective_id):
    rows, cols = x.shape
    out = pl.pallas_call(
        functools.partial(_ag_kernel, n, ny),
        out_shape=jax.ShapeDtypeStruct((n, ny, rows, cols), x.dtype),
        in_specs=[pl.BlockSpec(memory_space=pltpu.VMEM)],
        out_specs=pl.BlockSpec(memory_space=pltpu.VMEM),
        scratch_shapes=[
            pltpu.SemaphoreType.DMA((1,)),
            pltpu.SemaphoreType.DMA((ny - 1,)),
            pltpu.SemaphoreType.DMA((ny,)),
            pltpu.SemaphoreType.DMA((2, n - 1, SUB_CHUNKS)),
            pltpu.SemaphoreType.DMA((2, n - 1, SUB_CHUNKS)),
        ],
        compiler_params=pltpu.CompilerParams(collective_id=collective_id, has_side_effects=True),
    )(x)
    return out.reshape(n * ny * rows, cols)


def _ag2_kernel(n, ny, x_ref, out1, out2, own_sem, y1_send, y1_recv, z1_send, z1_recv, z2_send, z2_recv, y2_send, y2_recv):
    me, me_y = _enter(n, ny)
    right = lax.rem(me + 1, n)
    left = lax.rem(me + n - 1, n)
    r = out1.shape[2]
    half = r // 2
    dest = (right, left)
    mine1 = pltpu.make_async_copy(x_ref.at[pl.ds(0, r)], out1.at[me, me_y], own_sem.at[0])
    mine2 = pltpu.make_async_copy(x_ref.at[pl.ds(r, r)], out2.at[me_y, me], own_sem.at[1])
    mine1.start()
    mine2.start()

    def to_y(shift, src, dst, send_sem, recv_sem, sender):
        peer = lax.rem(me_y + shift, ny)
        return pltpu.make_async_remote_copy(
            src_ref=src,
            dst_ref=dst,
            send_sem=send_sem.at[shift - 1],
            recv_sem=recv_sem.at[sender],
            device_id={"cy": peer},
            device_id_type=MESH_ID,
        )

    sends = []
    for shift in range(1, ny):
        copy = to_y(shift, x_ref.at[pl.ds(0, r)], out1.at[me, me_y], y1_send, y1_recv, me_y)
        copy.start()
        sends.append(copy)

    def ring2(d, step, idx, src=None):
        rows_here = pl.ds(d * half, half)
        return pltpu.make_async_remote_copy(
            src_ref=out2.at[me_y, idx, rows_here] if src is None else src,
            dst_ref=out2.at[me_y, idx, rows_here],
            send_sem=z2_send.at[d, step],
            recv_sem=z2_recv.at[d, step],
            device_id={"cz": dest[d]},
            device_id_type=MESH_ID,
        )

    for step in range(n - 1):
        for d in range(2):
            idx = lax.rem(me + n - step, n) if d == 0 else lax.rem(me + step, n)
            if step == 0:
                copy = ring2(d, 0, idx, x_ref.at[pl.ds(r + d * half, half)])
            else:
                ring2(d, step - 1, idx).wait_recv()
                copy = ring2(d, step, idx)
            copy.start()
            sends.append(copy)
    for d in range(2):
        got = lax.rem(me + 1, n) if d == 0 else lax.rem(me + n - 1, n)
        ring2(d, n - 2, got).wait_recv()
    mine2.wait()
    ysends2 = []
    for shift in range(1, ny):
        copy = to_y(shift, out2.at[me_y], out2.at[me_y], y2_send, y2_recv, me_y)
        copy.start()
        ysends2.append(copy)

    mine1.wait()
    for shift in range(1, ny):
        peer = lax.rem(me_y + shift, ny)
        to_y(shift, x_ref.at[pl.ds(0, r)], out1.at[me, peer], y1_send, y1_recv, peer).wait_recv()

    def ring1(d, step, k, idx):
        rows_here = pl.ds(d * half, half)
        blocks = pl.ds(k * (ny // SUB_CHUNKS), ny // SUB_CHUNKS)
        return pltpu.make_async_remote_copy(
            src_ref=out1.at[idx, blocks, rows_here],
            dst_ref=out1.at[idx, blocks, rows_here],
            send_sem=z1_send.at[d, step, k],
            recv_sem=z1_recv.at[d, step, k],
            device_id={"cz": dest[d]},
            device_id_type=MESH_ID,
        )

    for step in range(n - 1):
        for k in range(SUB_CHUNKS):
            for d in range(2):
                if step > 0:
                    got = lax.rem(me + n - step, n) if d == 0 else lax.rem(me + step, n)
                    ring1(d, step - 1, k, got).wait_recv()
                idx = lax.rem(me + n - step, n) if d == 0 else lax.rem(me + step, n)
                copy = ring1(d, step, k, idx)
                copy.start()
                sends.append(copy)
    for k in range(SUB_CHUNKS):
        for d in range(2):
            got = lax.rem(me + 1, n) if d == 0 else lax.rem(me + n - 1, n)
            ring1(d, n - 2, k, got).wait_recv()
    for shift in range(1, ny):
        peer = lax.rem(me_y + shift, ny)
        to_y(shift, out2.at[me_y], out2.at[peer], y2_send, y2_recv, peer).wait_recv()
    for copy in sends + ysends2:
        copy.wait_send()


def all_gather_two_way(x, n, ny, collective_id):
    rows, cols = x.shape
    r = rows // 2
    out1, out2 = pl.pallas_call(
        functools.partial(_ag2_kernel, n, ny),
        out_shape=(
            jax.ShapeDtypeStruct((n, ny, r, cols), x.dtype),
            jax.ShapeDtypeStruct((ny, n, r, cols), x.dtype),
        ),
        in_specs=[pl.BlockSpec(memory_space=pltpu.VMEM)],
        out_specs=(pl.BlockSpec(memory_space=pltpu.VMEM), pl.BlockSpec(memory_space=pltpu.VMEM)),
        scratch_shapes=[
            pltpu.SemaphoreType.DMA((2,)),
            pltpu.SemaphoreType.DMA((ny - 1,)),
            pltpu.SemaphoreType.DMA((ny,)),
            pltpu.SemaphoreType.DMA((2, n - 1, SUB_CHUNKS)),
            pltpu.SemaphoreType.DMA((2, n - 1, SUB_CHUNKS)),
            pltpu.SemaphoreType.DMA((2, n - 1)),
            pltpu.SemaphoreType.DMA((2, n - 1)),
            pltpu.SemaphoreType.DMA((ny - 1,)),
            pltpu.SemaphoreType.DMA((ny,)),
        ],
        compiler_params=pltpu.CompilerParams(collective_id=collective_id, has_side_effects=True),
    )(x)
    return out1.reshape(n * ny * r, cols), out2.reshape(ny * n * r, cols)


def body(
    tokens,
    pick_flags,
    gate_scales,
    attn_gain,
    query_weight,
    key_weight,
    value_matrix,
    output_weight,
    ffn_gain,
    gate_weight,
    up_weight,
    down_weight,
):
    tok_local, width = tokens.shape
    y_size = lax.axis_size("cy")
    z_size = lax.axis_size("cz")
    ctx_size = y_size * z_size
    my_index = lax.axis_index("cy") * z_size + lax.axis_index("cz")
    blk = jnp.arange(ctx_size, dtype=jnp.int32)
    block_dev = (blk % y_size) * z_size + blk // y_size
    picked_count = PICK_DEV * ctx_size
    slots = MOST * ctx_size
    half_pick = PICK_DEV // 2
    half_cycle = ctx_size // 2
    slot_of = jnp.cumsum(pick_flags) - 1
    token_ids = jnp.arange(tok_local, dtype=jnp.int32)
    slot_match = (jnp.arange(MOST, dtype=jnp.int32)[:, None] == slot_of[None, :]) & (
        pick_flags[None, :] == 1
    )
    chosen = jnp.sum(jnp.where(slot_match, token_ids[None, :], 0), axis=1)
    filled = jnp.any(slot_match, axis=1)
    local_index = jnp.where(filled, chosen, -1)
    padded_rows = jnp.where(filled[:, None], tokens[chosen], jnp.zeros((), jnp.bfloat16))
    padded_gate = jnp.where(filled, gate_scales[chosen], jnp.zeros((), jnp.bfloat16))
    lane = jnp.arange(128, dtype=jnp.int32)[None, :]
    extra = jnp.where(
        lane == 0,
        local_index.astype(jnp.bfloat16)[:, None],
        jnp.where(lane == 1, padded_gate[:, None], jnp.zeros((), jnp.bfloat16)),
    )
    packed = jnp.concatenate((padded_rows, extra), axis=1)
    lead = MOST // 2
    part_one, part_two = all_gather_two_way(packed, z_size, y_size, 3)
    slot_ids = jnp.arange(slots, dtype=jnp.int32)
    part_blk = (slot_ids % (slots // 2)) // lead
    slot_dev = jnp.where(
        slot_ids < slots // 2, (part_blk % y_size) * z_size + part_blk // y_size, part_blk
    )
    all_index = jnp.concatenate((part_one[:, width], part_two[:, width])).astype(jnp.int32)
    slot_filled = all_index >= 0
    per_part = jnp.sum(slot_filled.reshape(2, ctx_size, lead).astype(jnp.int32), axis=2)
    counts = per_part[0].reshape(z_size, y_size).T.reshape(ctx_size) + per_part[1]
    run_ends = jnp.cumsum(counts)
    run_starts = run_ends - counts
    slot_pos = slot_dev * tok_local + all_index
    rope_pos = jnp.where(slot_filled, slot_pos, 0)
    never = jnp.int32(1 << 30)
    mask_pos = jnp.where(slot_filled, slot_pos, never)
    normalized = jnp.concatenate(
        (
            rms_scale(part_one[:, :width].astype(jnp.float32), attn_gain).astype(jnp.bfloat16),
            rms_scale(part_two[:, :width].astype(jnp.float32), attn_gain).astype(jnp.bfloat16),
        ),
        axis=0,
    )
    queries = jnp.dot(normalized, query_weight, preferred_element_type=jnp.float32)
    queries = apply_rotary(queries, rope_pos).astype(jnp.bfloat16)
    kv_weight = jnp.concatenate((key_weight, value_matrix), axis=1)
    kv_local = jnp.einsum(
        "pd,dc->cp", normalized, kv_weight, preferred_element_type=jnp.float32
    ).astype(jnp.bfloat16)
    comps = key_weight.shape[1] // KEY_VALUE_HEADS
    query_group_width = QUERY_HEADS // KEY_VALUE_HEADS
    by_head = jnp.transpose(kv_local.reshape(2, comps, KEY_VALUE_HEADS, slots), (2, 0, 1, 3))
    send = jnp.repeat(by_head, query_group_width, axis=0)
    got = lax.all_to_all(send, GROUP, 0, 0, tiled=True)
    key_cols = got[:, 0].reshape(ctx_size * comps, slots)
    value_cols = got[:, 1].reshape(ctx_size * comps, slots)
    keys_here = apply_rotary(key_cols.T.astype(jnp.float32), rope_pos).astype(jnp.bfloat16)
    values_here = value_cols.T
    scores = jnp.dot(queries, keys_here.T, preferred_element_type=jnp.float32) / jnp.sqrt(
        jnp.float32(HEAD_SIZE)
    )
    allowed = mask_pos[None, :] <= mask_pos[:, None]
    scores = jnp.where(allowed, scores, -jnp.inf)
    row_max = jnp.max(scores, axis=1, keepdims=True)
    exp_terms = jnp.exp(scores - row_max)
    prob_bf = (exp_terms / jnp.sum(exp_terms, axis=1, keepdims=True)).astype(jnp.bfloat16)
    head_pad = jnp.dot(prob_bf, values_here, preferred_element_type=jnp.float32).astype(jnp.bfloat16)
    order_ids = jnp.arange(picked_count, dtype=jnp.int32)
    owner_of = order_ids // PICK_DEV
    within = order_ids % PICK_DEV
    low_part = within < half_pick
    rank_block = jnp.where(low_part, owner_of, (owner_of + half_cycle) % ctx_size)
    rank_inner = jnp.where(low_part, 2 * within, 2 * (within - half_pick) + 1)
    rank_ids = rank_block * PICK_DEV + rank_inner
    before = (run_ends[None, :] <= rank_ids[:, None]).astype(jnp.int32)
    source = jnp.sum(before, axis=1)
    offset = rank_ids - jnp.sum(before * counts[None, :], axis=1)
    source_block = (source % z_size) * y_size + source // z_size
    flat_row = jnp.where(
        offset < lead, source_block * lead + offset, slots // 2 + source * lead + offset - lead
    )
    flat_blocked = flat_row.reshape(ctx_size, PICK_DEV)[block_dev].reshape(picked_count)
    pick_onehot = (flat_blocked[:, None] == slot_ids[None, :]).astype(jnp.bfloat16)
    head_out = jnp.dot(pick_onehot, head_pad, preferred_element_type=jnp.float32).astype(jnp.bfloat16)
    own_start = my_index * PICK_DEV
    own_flat = lax.dynamic_slice_in_dim(flat_row, own_start, PICK_DEV, 0)
    part_slots = jnp.arange(slots // 2, dtype=jnp.int32)[None, :]
    pick_one = (own_flat[:, None] == part_slots).astype(jnp.bfloat16)
    pick_two = (own_flat[:, None] - slots // 2 == part_slots).astype(jnp.bfloat16)
    own_packed = jnp.dot(pick_one, part_one, preferred_element_type=jnp.float32) + jnp.dot(
        pick_two, part_two, preferred_element_type=jnp.float32
    )
    own_rows = own_packed[:, :width]
    scale_own = own_packed[:, width + 1]
    attn_partial = jnp.dot(head_out, output_weight, preferred_element_type=jnp.float32).astype(jnp.bfloat16)
    attn_own = reduce_scatter_kernel(attn_partial.reshape(z_size, y_size * PICK_DEV, width), y_size, 0)
    mixed_own = own_rows + attn_own
    normed_own = rms_scale(mixed_own, ffn_gain).astype(jnp.bfloat16)
    normed_ffn = all_gather_kernel(normed_own, z_size, y_size, 2)
    gate_proj = jnp.dot(normed_ffn, gate_weight, preferred_element_type=jnp.float32)
    up_proj = jnp.dot(normed_ffn, up_weight, preferred_element_type=jnp.float32)
    hidden = (jax.nn.silu(gate_proj) * up_proj).astype(jnp.bfloat16)
    ffn_partial = jnp.dot(hidden, down_weight, preferred_element_type=jnp.float32).astype(jnp.bfloat16)
    ffn_own = reduce_scatter_kernel(ffn_partial.reshape(z_size, y_size * PICK_DEV, width), y_size, 1)
    final_own = (own_rows + scale_own[:, None] * (attn_own + ffn_own)).astype(jnp.bfloat16)
    own_source = lax.dynamic_slice_in_dim(source, own_start, PICK_DEV, 0)
    targets = jnp.arange(ctx_size, dtype=jnp.int32)[:, None]
    first_half = (own_source[None, :half_pick] == targets)[:, :, None]
    second_half = (own_source[None, half_pick:] == targets)[:, :, None]
    zero = jnp.zeros((), jnp.bfloat16)
    back = jnp.where(
        first_half,
        final_own[None, :half_pick],
        jnp.where(second_half, final_own[None, half_pick:], zero),
    )
    returned = lax.all_to_all(back, GROUP, 0, 0, tiled=True).reshape(ctx_size * half_pick, width)
    my_start = run_starts[my_index]
    rank_here = jnp.clip(my_start + slot_of, 0, picked_count - 1)
    inner_here = rank_here % PICK_DEV
    odd_here = inner_here % 2
    owner_here = (rank_here // PICK_DEV + odd_here * half_cycle) % ctx_size
    take_rows = owner_here * half_pick + inner_here // 2
    return jnp.where(pick_flags[:, None] == 1, returned[take_rows], tokens)


def solution(mesh):
    dp_size, ctx_size = mesh.devices.shape
    z_size = Z_RUN if ctx_size % Z_RUN == 0 else ctx_size
    split = Mesh(mesh.devices.reshape(dp_size, ctx_size // z_size, z_size), ("dp", "cy", "cz"))
    rows = ("dp", "cy", "cz")
    in_specs = (
        P(rows, None),
        P(rows),
        P(rows),
        P(),
        P(None, GROUP),
        P(None, GROUP),
        P(None, GROUP),
        P(GROUP, None),
        P(),
        P(None, GROUP),
        P(None, GROUP),
        P(GROUP, None),
    )
    out_specs = P(rows, None)
    return jax.shard_map(body, mesh=split, in_specs=in_specs, out_specs=out_specs, check_vma=False)
```

```python
import functools

import jax
import jax.numpy as jnp
from jax import lax
from jax.experimental import pallas as pl
from jax.experimental.pallas import tpu as pltpu
from jax.sharding import Mesh, PartitionSpec as P

QUERY_HEADS = 32
KEY_VALUE_HEADS = 8
HEAD_SIZE = 128
PICK_DEV = 16
MOST = 32
Z_RUN = 8
GROUP = ("cy", "cz")


norm_eps = 1e-05
rope_base = 500000.0


def rms_scale(matrix, gain_vec):
    mean_square = jnp.mean(matrix * matrix, axis=-1, keepdims=True)
    return matrix * lax.rsqrt(mean_square + norm_eps) * gain_vec


def apply_rotary(values, token_positions):
    half_dim = values.shape[-1] // 2
    frequency = rope_base ** (-(jnp.arange(half_dim, dtype=jnp.float32) * 2.0) / values.shape[-1])
    angles = token_positions.astype(jnp.float32)[:, None] * frequency[None, :]
    cosine = jnp.cos(angles)
    sine_part = jnp.sin(angles)
    lower_half = values[..., :half_dim]
    upper_half = values[..., half_dim:]
    return jnp.concatenate(
        (
            lower_half * cosine - upper_half * sine_part,
            upper_half * cosine + lower_half * sine_part,
        ),
        axis=-1,
    )


MESH_ID = pl.DeviceIdType.MESH
SUB_CHUNKS = 2


def _enter(nz, ny):
    me_z = lax.axis_index("cz")
    me_y = lax.axis_index("cy")
    barrier = pltpu.get_barrier_semaphore()
    for neighbour in (lax.rem(me_z + nz - 1, nz), lax.rem(me_z + 1, nz)):
        pl.semaphore_signal(barrier, inc=1, device_id={"cz": neighbour}, device_id_type=MESH_ID)
    for shift in range(1, ny):
        pl.semaphore_signal(barrier, inc=1, device_id={"cy": lax.rem(me_y + shift, ny)}, device_id_type=MESH_ID)
    pl.semaphore_wait(barrier, 2 + ny - 1)
    return me_z, me_y


def _rs_kernel(n, ny, a_ref, w_ref, out_ref, recv, sendbuf, firstbuf, send_sem, recv_sem, zsum, ybuf, yrecv, ysend_sem, yrecv_sem):
    me, me_y = _enter(n, ny)
    right = lax.rem(me + 1, n)
    left = lax.rem(me + n - 1, n)
    half = w_ref.shape[1] // 2
    piece = a_ref.shape[1] // SUB_CHUNKS
    own = out_ref.shape[0]
    dest = (right, left)

    def part(chunk, k, d):
        return jnp.dot(
            a_ref[chunk, pl.ds(k * piece, piece), :],
            w_ref[:, pl.ds(d * half, half)],
            preferred_element_type=jnp.float32,
        ).astype(sendbuf.dtype)

    def link(d, slot, k, src):
        return pltpu.make_async_remote_copy(
            src_ref=src,
            dst_ref=recv.at[d, slot, k],
            send_sem=send_sem.at[d, slot, k],
            recv_sem=recv_sem.at[d, slot, k],
            device_id={"cz": dest[d]},
            device_id_type=MESH_ID,
        )

    sends = []
    for k in range(SUB_CHUNKS):
        for d in range(2):
            first = lax.rem(me + n - 1, n) if d == 0 else lax.rem(me + 1, n)
            firstbuf[d, k] = part(first, k, d)
            copy = link(d, 0, k, firstbuf.at[d, k])
            copy.start()
            sends.append(copy)
    for step in range(n - 1):
        for k in range(SUB_CHUNKS):
            for d in range(2):
                if d == 0:
                    chunk = lax.rem(me + 2 * n - step - 2, n)
                else:
                    chunk = lax.rem(me + step + 2, n)
                mine = part(chunk, k, d).astype(jnp.float32)
                link(d, step, k, sendbuf.at[d, step, k]).wait_recv()
                total = recv[d, step, k].astype(jnp.float32) + mine
                if step == n - 2:
                    zsum[pl.ds(k * piece, piece), pl.ds(d * half, half)] = total
                else:
                    sendbuf[d, step, k] = total.astype(sendbuf.dtype)
                    copy = link(d, step + 1, k, sendbuf.at[d, step, k])
                    copy.start()
                    sends.append(copy)
    ysends = []
    for shift in range(1, ny):
        peer = lax.rem(me_y + shift, ny)
        ybuf[shift - 1] = zsum[pl.ds(pl.multiple_of(peer * own, own), own), :].astype(ybuf.dtype)
        copy = pltpu.make_async_remote_copy(
            src_ref=ybuf.at[shift - 1],
            dst_ref=yrecv.at[shift - 1],
            send_sem=ysend_sem.at[shift - 1],
            recv_sem=yrecv_sem.at[shift - 1],
            device_id={"cy": peer},
            device_id_type=MESH_ID,
        )
        copy.start()
        ysends.append(copy)
    total = zsum[pl.ds(pl.multiple_of(me_y * own, own), own), :]
    for shift in range(1, ny):
        ysends[shift - 1].wait_recv()
        total = total + yrecv[shift - 1].astype(jnp.float32)
    out_ref[...] = total
    for copy in sends + ysends:
        copy.wait_send()


def reduce_scatter_kernel(a, w, ny, collective_id):
    n, rows, _ = a.shape
    cols = w.shape[1]
    half = cols // 2
    piece = rows // SUB_CHUNKS
    own = rows // ny
    return pl.pallas_call(
        functools.partial(_rs_kernel, n, ny),
        out_shape=jax.ShapeDtypeStruct((own, cols), jnp.float32),
        in_specs=[pl.BlockSpec(memory_space=pltpu.VMEM), pl.BlockSpec(memory_space=pltpu.VMEM)],
        out_specs=pl.BlockSpec(memory_space=pltpu.VMEM),
        scratch_shapes=[
            pltpu.VMEM((2, n - 1, SUB_CHUNKS, piece, half), w.dtype),
            pltpu.VMEM((2, n - 1, SUB_CHUNKS, piece, half), w.dtype),
            pltpu.VMEM((2, SUB_CHUNKS, piece, half), w.dtype),
            pltpu.SemaphoreType.DMA((2, n - 1, SUB_CHUNKS)),
            pltpu.SemaphoreType.DMA((2, n - 1, SUB_CHUNKS)),
            pltpu.VMEM((rows, cols), jnp.float32),
            pltpu.VMEM((ny - 1, own, cols), w.dtype),
            pltpu.VMEM((ny - 1, own, cols), w.dtype),
            pltpu.SemaphoreType.DMA((ny - 1,)),
            pltpu.SemaphoreType.DMA((ny - 1,)),
        ],
        compiler_params=pltpu.CompilerParams(collective_id=collective_id, has_side_effects=True),
    )(a, w)


def _ag_kernel(n, ny, x_ref, out_ref, own_sem, ysend_sem, yrecv_sem, send_sem, recv_sem):
    me, me_y = _enter(n, ny)
    right = lax.rem(me + 1, n)
    left = lax.rem(me + n - 1, n)
    rows = x_ref.shape[0]
    half = rows // 2
    dest = (right, left)
    mine = pltpu.make_async_copy(x_ref, out_ref.at[me, me_y], own_sem.at[0])
    mine.start()
    ysends = []
    for shift in range(1, ny):
        peer = lax.rem(me_y + shift, ny)
        copy = pltpu.make_async_remote_copy(
            src_ref=x_ref,
            dst_ref=out_ref.at[me, me_y],
            send_sem=ysend_sem.at[shift - 1],
            recv_sem=yrecv_sem.at[me_y],
            device_id={"cy": peer},
            device_id_type=MESH_ID,
        )
        copy.start()
        ysends.append(copy)
    mine.wait()
    for shift in range(1, ny):
        peer = lax.rem(me_y + shift, ny)
        pltpu.make_async_remote_copy(
            src_ref=x_ref,
            dst_ref=out_ref.at[me, peer],
            send_sem=ysend_sem.at[shift - 1],
            recv_sem=yrecv_sem.at[peer],
            device_id={"cy": peer},
            device_id_type=MESH_ID,
        ).wait_recv()

    def link(d, step, k, idx):
        rows_here = pl.ds(d * half, half)
        blocks = pl.ds(k * (ny // SUB_CHUNKS), ny // SUB_CHUNKS)
        return pltpu.make_async_remote_copy(
            src_ref=out_ref.at[idx, blocks, rows_here],
            dst_ref=out_ref.at[idx, blocks, rows_here],
            send_sem=send_sem.at[d, step, k],
            recv_sem=recv_sem.at[d, step, k],
            device_id={"cz": dest[d]},
            device_id_type=MESH_ID,
        )

    sends = []
    for step in range(n - 1):
        for k in range(SUB_CHUNKS):
            for d in range(2):
                if step > 0:
                    got = lax.rem(me + n - step, n) if d == 0 else lax.rem(me + step, n)
                    link(d, step - 1, k, got).wait_recv()
                idx = lax.rem(me + n - step, n) if d == 0 else lax.rem(me + step, n)
                copy = link(d, step, k, idx)
                copy.start()
                sends.append(copy)
    for k in range(SUB_CHUNKS):
        for d in range(2):
            got = lax.rem(me + 1, n) if d == 0 else lax.rem(me + n - 1, n)
            link(d, n - 2, k, got).wait_recv()
    for copy in ysends + sends:
        copy.wait_send()


def all_gather_kernel(x, n, ny, collective_id):
    rows, cols = x.shape
    out = pl.pallas_call(
        functools.partial(_ag_kernel, n, ny),
        out_shape=jax.ShapeDtypeStruct((n, ny, rows, cols), x.dtype),
        in_specs=[pl.BlockSpec(memory_space=pltpu.VMEM)],
        out_specs=pl.BlockSpec(memory_space=pltpu.VMEM),
        scratch_shapes=[
            pltpu.SemaphoreType.DMA((1,)),
            pltpu.SemaphoreType.DMA((ny - 1,)),
            pltpu.SemaphoreType.DMA((ny,)),
            pltpu.SemaphoreType.DMA((2, n - 1, SUB_CHUNKS)),
            pltpu.SemaphoreType.DMA((2, n - 1, SUB_CHUNKS)),
        ],
        compiler_params=pltpu.CompilerParams(collective_id=collective_id, has_side_effects=True),
    )(x)
    return out.reshape(n * ny * rows, cols)


def _ag2_kernel(n, ny, x_ref, out1, out2, own_sem, y1_send, y1_recv, z1_send, z1_recv, z2_send, z2_recv, y2_send, y2_recv):
    me, me_y = _enter(n, ny)
    right = lax.rem(me + 1, n)
    left = lax.rem(me + n - 1, n)
    r = out1.shape[2]
    half = r // 2
    dest = (right, left)
    mine1 = pltpu.make_async_copy(x_ref.at[pl.ds(0, r)], out1.at[me, me_y], own_sem.at[0])
    mine2 = pltpu.make_async_copy(x_ref.at[pl.ds(r, r)], out2.at[me_y, me], own_sem.at[1])
    mine1.start()
    mine2.start()

    def to_y(shift, src, dst, send_sem, recv_sem, sender):
        peer = lax.rem(me_y + shift, ny)
        return pltpu.make_async_remote_copy(
            src_ref=src,
            dst_ref=dst,
            send_sem=send_sem.at[shift - 1],
            recv_sem=recv_sem.at[sender],
            device_id={"cy": peer},
            device_id_type=MESH_ID,
        )

    sends = []
    for shift in range(1, ny):
        copy = to_y(shift, x_ref.at[pl.ds(0, r)], out1.at[me, me_y], y1_send, y1_recv, me_y)
        copy.start()
        sends.append(copy)

    def ring2(d, step, idx, src=None):
        rows_here = pl.ds(d * half, half)
        return pltpu.make_async_remote_copy(
            src_ref=out2.at[me_y, idx, rows_here] if src is None else src,
            dst_ref=out2.at[me_y, idx, rows_here],
            send_sem=z2_send.at[d, step],
            recv_sem=z2_recv.at[d, step],
            device_id={"cz": dest[d]},
            device_id_type=MESH_ID,
        )

    for step in range(n - 1):
        for d in range(2):
            idx = lax.rem(me + n - step, n) if d == 0 else lax.rem(me + step, n)
            if step == 0:
                copy = ring2(d, 0, idx, x_ref.at[pl.ds(r + d * half, half)])
            else:
                ring2(d, step - 1, idx).wait_recv()
                copy = ring2(d, step, idx)
            copy.start()
            sends.append(copy)
    for d in range(2):
        got = lax.rem(me + 1, n) if d == 0 else lax.rem(me + n - 1, n)
        ring2(d, n - 2, got).wait_recv()
    mine2.wait()
    ysends2 = []
    for shift in range(1, ny):
        copy = to_y(shift, out2.at[me_y], out2.at[me_y], y2_send, y2_recv, me_y)
        copy.start()
        ysends2.append(copy)

    mine1.wait()
    for shift in range(1, ny):
        peer = lax.rem(me_y + shift, ny)
        to_y(shift, x_ref.at[pl.ds(0, r)], out1.at[me, peer], y1_send, y1_recv, peer).wait_recv()

    def ring1(d, step, idx):
        rows_here = pl.ds(d * half, half)
        return pltpu.make_async_remote_copy(
            src_ref=out1.at[idx, :, rows_here],
            dst_ref=out1.at[idx, :, rows_here],
            send_sem=z1_send.at[d, step],
            recv_sem=z1_recv.at[d, step],
            device_id={"cz": dest[d]},
            device_id_type=MESH_ID,
        )

    for step in range(n - 1):
        for d in range(2):
            if step > 0:
                got = lax.rem(me + n - step, n) if d == 0 else lax.rem(me + step, n)
                ring1(d, step - 1, got).wait_recv()
            idx = lax.rem(me + n - step, n) if d == 0 else lax.rem(me + step, n)
            copy = ring1(d, step, idx)
            copy.start()
            sends.append(copy)
    for d in range(2):
        got = lax.rem(me + 1, n) if d == 0 else lax.rem(me + n - 1, n)
        ring1(d, n - 2, got).wait_recv()
    for shift in range(1, ny):
        peer = lax.rem(me_y + shift, ny)
        to_y(shift, out2.at[me_y], out2.at[peer], y2_send, y2_recv, peer).wait_recv()
    for copy in sends + ysends2:
        copy.wait_send()


def all_gather_two_way(x, n, ny, collective_id):
    rows, cols = x.shape
    r = rows // 2
    out1, out2 = pl.pallas_call(
        functools.partial(_ag2_kernel, n, ny),
        out_shape=(
            jax.ShapeDtypeStruct((n, ny, r, cols), x.dtype),
            jax.ShapeDtypeStruct((ny, n, r, cols), x.dtype),
        ),
        in_specs=[pl.BlockSpec(memory_space=pltpu.VMEM)],
        out_specs=(pl.BlockSpec(memory_space=pltpu.VMEM), pl.BlockSpec(memory_space=pltpu.VMEM)),
        scratch_shapes=[
            pltpu.SemaphoreType.DMA((2,)),
            pltpu.SemaphoreType.DMA((ny - 1,)),
            pltpu.SemaphoreType.DMA((ny,)),
            pltpu.SemaphoreType.DMA((2, n - 1)),
            pltpu.SemaphoreType.DMA((2, n - 1)),
            pltpu.SemaphoreType.DMA((2, n - 1)),
            pltpu.SemaphoreType.DMA((2, n - 1)),
            pltpu.SemaphoreType.DMA((ny - 1,)),
            pltpu.SemaphoreType.DMA((ny,)),
        ],
        compiler_params=pltpu.CompilerParams(collective_id=collective_id, has_side_effects=True),
    )(x)
    return out1.reshape(n * ny * r, cols), out2.reshape(ny * n * r, cols)


def body(
    tokens,
    pick_flags,
    gate_scales,
    attn_gain,
    query_weight,
    key_weight,
    value_matrix,
    output_weight,
    ffn_gain,
    gate_weight,
    up_weight,
    down_weight,
):
    tok_local, width = tokens.shape
    y_size = lax.axis_size("cy")
    z_size = lax.axis_size("cz")
    ctx_size = y_size * z_size
    my_index = lax.axis_index("cy") * z_size + lax.axis_index("cz")
    blk = jnp.arange(ctx_size, dtype=jnp.int32)
    block_dev = (blk % y_size) * z_size + blk // y_size
    picked_count = PICK_DEV * ctx_size
    slots = MOST * ctx_size
    half_pick = PICK_DEV // 2
    half_cycle = ctx_size // 2
    slot_of = jnp.cumsum(pick_flags) - 1
    token_ids = jnp.arange(tok_local, dtype=jnp.int32)
    slot_match = (jnp.arange(MOST, dtype=jnp.int32)[:, None] == slot_of[None, :]) & (
        pick_flags[None, :] == 1
    )
    chosen = jnp.sum(jnp.where(slot_match, token_ids[None, :], 0), axis=1)
    filled = jnp.any(slot_match, axis=1)
    local_index = jnp.where(filled, chosen, -1)
    padded_rows = jnp.where(filled[:, None], tokens[chosen], jnp.zeros((), jnp.bfloat16))
    padded_gate = jnp.where(filled, gate_scales[chosen], jnp.zeros((), jnp.bfloat16))
    lane = jnp.arange(128, dtype=jnp.int32)[None, :]
    extra = jnp.where(
        lane == 0,
        local_index.astype(jnp.bfloat16)[:, None],
        jnp.where(lane == 1, padded_gate[:, None], jnp.zeros((), jnp.bfloat16)),
    )
    packed = jnp.concatenate((padded_rows, extra), axis=1)
    lead = MOST // 2
    part_one, part_two = all_gather_two_way(packed, z_size, y_size, 3)
    slot_ids = jnp.arange(slots, dtype=jnp.int32)
    part_blk = (slot_ids % (slots // 2)) // lead
    slot_dev = jnp.where(
        slot_ids < slots // 2, (part_blk % y_size) * z_size + part_blk // y_size, part_blk
    )
    all_index = jnp.concatenate((part_one[:, width], part_two[:, width])).astype(jnp.int32)
    slot_filled = all_index >= 0
    per_part = jnp.sum(slot_filled.reshape(2, ctx_size, lead).astype(jnp.int32), axis=2)
    counts = per_part[0].reshape(z_size, y_size).T.reshape(ctx_size) + per_part[1]
    run_ends = jnp.cumsum(counts)
    run_starts = run_ends - counts
    slot_pos = slot_dev * tok_local + all_index
    rope_pos = jnp.where(slot_filled, slot_pos, 0)
    never = jnp.int32(1 << 30)
    mask_pos = jnp.where(slot_filled, slot_pos, never)
    normalized = jnp.concatenate(
        (
            rms_scale(part_one[:, :width].astype(jnp.float32), attn_gain).astype(jnp.bfloat16),
            rms_scale(part_two[:, :width].astype(jnp.float32), attn_gain).astype(jnp.bfloat16),
        ),
        axis=0,
    )
    queries = jnp.dot(normalized, query_weight, preferred_element_type=jnp.float32)
    queries = apply_rotary(queries, rope_pos).astype(jnp.bfloat16)
    kv_weight = jnp.concatenate((key_weight, value_matrix), axis=1)
    kv_local = jnp.einsum(
        "pd,dc->cp", normalized, kv_weight, preferred_element_type=jnp.float32
    ).astype(jnp.bfloat16)
    comps = key_weight.shape[1] // KEY_VALUE_HEADS
    query_group_width = QUERY_HEADS // KEY_VALUE_HEADS
    by_head = jnp.transpose(kv_local.reshape(2, comps, KEY_VALUE_HEADS, slots), (2, 0, 1, 3))
    send = jnp.repeat(by_head, query_group_width, axis=0)
    got = lax.all_to_all(send, GROUP, 0, 0, tiled=True)
    key_cols = got[:, 0].reshape(ctx_size * comps, slots)
    value_cols = got[:, 1].reshape(ctx_size * comps, slots)
    keys_here = apply_rotary(key_cols.T.astype(jnp.float32), rope_pos).astype(jnp.bfloat16)
    values_here = value_cols.T
    scores = jnp.dot(queries, keys_here.T, preferred_element_type=jnp.float32) / jnp.sqrt(
        jnp.float32(HEAD_SIZE)
    )
    allowed = mask_pos[None, :] <= mask_pos[:, None]
    scores = jnp.where(allowed, scores, -jnp.inf)
    row_max = jnp.max(scores, axis=1, keepdims=True)
    exp_terms = jnp.exp(scores - row_max)
    prob_bf = (exp_terms / jnp.sum(exp_terms, axis=1, keepdims=True)).astype(jnp.bfloat16)
    head_pad = jnp.dot(prob_bf, values_here, preferred_element_type=jnp.float32).astype(jnp.bfloat16)
    order_ids = jnp.arange(picked_count, dtype=jnp.int32)
    owner_of = order_ids // PICK_DEV
    within = order_ids % PICK_DEV
    low_part = within < half_pick
    rank_block = jnp.where(low_part, owner_of, (owner_of + half_cycle) % ctx_size)
    rank_inner = jnp.where(low_part, 2 * within, 2 * (within - half_pick) + 1)
    rank_ids = rank_block * PICK_DEV + rank_inner
    before = (run_ends[None, :] <= rank_ids[:, None]).astype(jnp.int32)
    source = jnp.sum(before, axis=1)
    offset = rank_ids - jnp.sum(before * counts[None, :], axis=1)
    source_block = (source % z_size) * y_size + source // z_size
    flat_row = jnp.where(
        offset < lead, source_block * lead + offset, slots // 2 + source * lead + offset - lead
    )
    flat_blocked = flat_row.reshape(ctx_size, PICK_DEV)[block_dev].reshape(picked_count)
    pick_onehot = (flat_blocked[:, None] == slot_ids[None, :]).astype(jnp.bfloat16)
    head_out = jnp.dot(pick_onehot, head_pad, preferred_element_type=jnp.float32).astype(jnp.bfloat16)
    own_start = my_index * PICK_DEV
    own_flat = lax.dynamic_slice_in_dim(flat_row, own_start, PICK_DEV, 0)
    part_slots = jnp.arange(slots // 2, dtype=jnp.int32)[None, :]
    pick_one = (own_flat[:, None] == part_slots).astype(jnp.bfloat16)
    pick_two = (own_flat[:, None] - slots // 2 == part_slots).astype(jnp.bfloat16)
    own_packed = jnp.dot(pick_one, part_one, preferred_element_type=jnp.float32) + jnp.dot(
        pick_two, part_two, preferred_element_type=jnp.float32
    )
    own_rows = own_packed[:, :width]
    scale_own = own_packed[:, width + 1]
    attn_own = reduce_scatter_kernel(
        head_out.reshape(z_size, y_size * PICK_DEV, head_out.shape[1]), output_weight, y_size, 0
    )
    mixed_own = own_rows + attn_own
    normed_own = rms_scale(mixed_own, ffn_gain).astype(jnp.bfloat16)
    normed_ffn = all_gather_kernel(normed_own, z_size, y_size, 2)
    gate_proj = jnp.dot(normed_ffn, gate_weight, preferred_element_type=jnp.float32)
    up_proj = jnp.dot(normed_ffn, up_weight, preferred_element_type=jnp.float32)
    hidden = (jax.nn.silu(gate_proj) * up_proj).astype(jnp.bfloat16)
    ffn_own = reduce_scatter_kernel(
        hidden.reshape(z_size, y_size * PICK_DEV, hidden.shape[1]), down_weight, y_size, 1
    )
    final_own = (own_rows + scale_own[:, None] * (attn_own + ffn_own)).astype(jnp.bfloat16)
    own_source = lax.dynamic_slice_in_dim(source, own_start, PICK_DEV, 0)
    targets = jnp.arange(ctx_size, dtype=jnp.int32)[:, None]
    first_half = (own_source[None, :half_pick] == targets)[:, :, None]
    second_half = (own_source[None, half_pick:] == targets)[:, :, None]
    zero = jnp.zeros((), jnp.bfloat16)
    back = jnp.where(
        first_half,
        final_own[None, :half_pick],
        jnp.where(second_half, final_own[None, half_pick:], zero),
    )
    returned = lax.all_to_all(back, GROUP, 0, 0, tiled=True).reshape(ctx_size * half_pick, width)
    my_start = run_starts[my_index]
    rank_here = jnp.clip(my_start + slot_of, 0, picked_count - 1)
    inner_here = rank_here % PICK_DEV
    odd_here = inner_here % 2
    owner_here = (rank_here // PICK_DEV + odd_here * half_cycle) % ctx_size
    take_rows = owner_here * half_pick + inner_here // 2
    return jnp.where(pick_flags[:, None] == 1, returned[take_rows], tokens)


def solution(mesh):
    dp_size, ctx_size = mesh.devices.shape
    z_size = Z_RUN if ctx_size % Z_RUN == 0 else ctx_size
    split = Mesh(mesh.devices.reshape(dp_size, ctx_size // z_size, z_size), ("dp", "cy", "cz"))
    rows = ("dp", "cy", "cz")
    in_specs = (
        P(rows, None),
        P(rows),
        P(rows),
        P(),
        P(None, GROUP),
        P(None, GROUP),
        P(None, GROUP),
        P(GROUP, None),
        P(),
        P(None, GROUP),
        P(None, GROUP),
        P(GROUP, None),
    )
    out_specs = P(rows, None)
    return jax.shard_map(body, mesh=split, in_specs=in_specs, out_specs=out_specs, check_vma=False)
```

```python
import functools

import jax
import jax.numpy as jnp
from jax import lax
from jax.experimental import pallas as pl
from jax.experimental.pallas import tpu as pltpu
from jax.sharding import Mesh, PartitionSpec as P

QUERY_HEADS = 32
KEY_VALUE_HEADS = 8
HEAD_SIZE = 128
PICK_DEV = 16
MOST = 32
Z_RUN = 8
GROUP = ("cy", "cz")


norm_eps = 1e-05
rope_base = 500000.0


def rms_scale(matrix, gain_vec):
    mean_square = jnp.mean(matrix * matrix, axis=-1, keepdims=True)
    return matrix * lax.rsqrt(mean_square + norm_eps) * gain_vec


def apply_rotary(values, token_positions):
    half_dim = values.shape[-1] // 2
    frequency = rope_base ** (-(jnp.arange(half_dim, dtype=jnp.float32) * 2.0) / values.shape[-1])
    angles = token_positions.astype(jnp.float32)[:, None] * frequency[None, :]
    cosine = jnp.cos(angles)
    sine_part = jnp.sin(angles)
    lower_half = values[..., :half_dim]
    upper_half = values[..., half_dim:]
    return jnp.concatenate(
        (
            lower_half * cosine - upper_half * sine_part,
            upper_half * cosine + lower_half * sine_part,
        ),
        axis=-1,
    )


MESH_ID = pl.DeviceIdType.MESH
SUB_CHUNKS = 2


def _enter(nz, ny):
    me_z = lax.axis_index("cz")
    me_y = lax.axis_index("cy")
    barrier = pltpu.get_barrier_semaphore()
    for neighbour in (lax.rem(me_z + nz - 1, nz), lax.rem(me_z + 1, nz)):
        pl.semaphore_signal(barrier, inc=1, device_id={"cz": neighbour}, device_id_type=MESH_ID)
    for shift in range(1, ny):
        pl.semaphore_signal(barrier, inc=1, device_id={"cy": lax.rem(me_y + shift, ny)}, device_id_type=MESH_ID)
    pl.semaphore_wait(barrier, 2 + ny - 1)
    return me_z, me_y


def _rs_kernel(n, ny, a_ref, w_ref, out_ref, recv, sendbuf, firstbuf, send_sem, recv_sem, zsum, ybuf, yrecv, ysend_sem, yrecv_sem):
    me, me_y = _enter(n, ny)
    right = lax.rem(me + 1, n)
    left = lax.rem(me + n - 1, n)
    half = w_ref.shape[1] // 2
    piece = a_ref.shape[1] // SUB_CHUNKS
    own = out_ref.shape[0]
    dest = (right, left)

    def part(chunk, k, d):
        return jnp.dot(
            a_ref[chunk, pl.ds(k * piece, piece), :],
            w_ref[:, pl.ds(d * half, half)],
            preferred_element_type=jnp.float32,
        ).astype(sendbuf.dtype)

    def link(d, slot, k, src):
        return pltpu.make_async_remote_copy(
            src_ref=src,
            dst_ref=recv.at[d, slot, k],
            send_sem=send_sem.at[d, slot, k],
            recv_sem=recv_sem.at[d, slot, k],
            device_id={"cz": dest[d]},
            device_id_type=MESH_ID,
        )

    sends = []
    for k in range(SUB_CHUNKS):
        for d in range(2):
            first = lax.rem(me + n - 1, n) if d == 0 else lax.rem(me + 1, n)
            firstbuf[d, k] = part(first, k, d)
            copy = link(d, 0, k, firstbuf.at[d, k])
            copy.start()
            sends.append(copy)
    for step in range(n - 1):
        for k in range(SUB_CHUNKS):
            for d in range(2):
                if d == 0:
                    chunk = lax.rem(me + 2 * n - step - 2, n)
                else:
                    chunk = lax.rem(me + step + 2, n)
                mine = part(chunk, k, d).astype(jnp.float32)
                link(d, step, k, sendbuf.at[d, step, k]).wait_recv()
                total = recv[d, step, k].astype(jnp.float32) + mine
                if step == n - 2:
                    zsum[pl.ds(k * piece, piece), pl.ds(d * half, half)] = total
                else:
                    sendbuf[d, step, k] = total.astype(sendbuf.dtype)
                    copy = link(d, step + 1, k, sendbuf.at[d, step, k])
                    copy.start()
                    sends.append(copy)
    ysends = []
    for shift in range(1, ny):
        peer = lax.rem(me_y + shift, ny)
        ybuf[shift - 1] = zsum[pl.ds(pl.multiple_of(peer * own, own), own), :].astype(ybuf.dtype)
        copy = pltpu.make_async_remote_copy(
            src_ref=ybuf.at[shift - 1],
            dst_ref=yrecv.at[shift - 1],
            send_sem=ysend_sem.at[shift - 1],
            recv_sem=yrecv_sem.at[shift - 1],
            device_id={"cy": peer},
            device_id_type=MESH_ID,
        )
        copy.start()
        ysends.append(copy)
    total = zsum[pl.ds(pl.multiple_of(me_y * own, own), own), :]
    for shift in range(1, ny):
        ysends[shift - 1].wait_recv()
        total = total + yrecv[shift - 1].astype(jnp.float32)
    out_ref[...] = total
    for copy in sends + ysends:
        copy.wait_send()


def reduce_scatter_kernel(a, w, ny, collective_id):
    n, rows, _ = a.shape
    cols = w.shape[1]
    half = cols // 2
    piece = rows // SUB_CHUNKS
    own = rows // ny
    return pl.pallas_call(
        functools.partial(_rs_kernel, n, ny),
        out_shape=jax.ShapeDtypeStruct((own, cols), jnp.float32),
        in_specs=[pl.BlockSpec(memory_space=pltpu.VMEM), pl.BlockSpec(memory_space=pltpu.VMEM)],
        out_specs=pl.BlockSpec(memory_space=pltpu.VMEM),
        scratch_shapes=[
            pltpu.VMEM((2, n - 1, SUB_CHUNKS, piece, half), w.dtype),
            pltpu.VMEM((2, n - 1, SUB_CHUNKS, piece, half), w.dtype),
            pltpu.VMEM((2, SUB_CHUNKS, piece, half), w.dtype),
            pltpu.SemaphoreType.DMA((2, n - 1, SUB_CHUNKS)),
            pltpu.SemaphoreType.DMA((2, n - 1, SUB_CHUNKS)),
            pltpu.VMEM((rows, cols), jnp.float32),
            pltpu.VMEM((ny - 1, own, cols), w.dtype),
            pltpu.VMEM((ny - 1, own, cols), w.dtype),
            pltpu.SemaphoreType.DMA((ny - 1,)),
            pltpu.SemaphoreType.DMA((ny - 1,)),
        ],
        compiler_params=pltpu.CompilerParams(collective_id=collective_id, has_side_effects=True),
    )(a, w)


def _ag_kernel(n, ny, x_ref, out_ref, own_sem, ysend_sem, yrecv_sem, send_sem, recv_sem):
    me, me_y = _enter(n, ny)
    right = lax.rem(me + 1, n)
    left = lax.rem(me + n - 1, n)
    rows = x_ref.shape[0]
    half = rows // 2
    dest = (right, left)
    mine = pltpu.make_async_copy(x_ref, out_ref.at[me, me_y], own_sem.at[0])
    mine.start()
    ysends = []
    for shift in range(1, ny):
        peer = lax.rem(me_y + shift, ny)
        copy = pltpu.make_async_remote_copy(
            src_ref=x_ref,
            dst_ref=out_ref.at[me, me_y],
            send_sem=ysend_sem.at[shift - 1],
            recv_sem=yrecv_sem.at[me_y],
            device_id={"cy": peer},
            device_id_type=MESH_ID,
        )
        copy.start()
        ysends.append(copy)
    mine.wait()
    for shift in range(1, ny):
        peer = lax.rem(me_y + shift, ny)
        pltpu.make_async_remote_copy(
            src_ref=x_ref,
            dst_ref=out_ref.at[me, peer],
            send_sem=ysend_sem.at[shift - 1],
            recv_sem=yrecv_sem.at[peer],
            device_id={"cy": peer},
            device_id_type=MESH_ID,
        ).wait_recv()

    def link(d, step, k, idx):
        rows_here = pl.ds(d * half, half)
        blocks = pl.ds(k * (ny // SUB_CHUNKS), ny // SUB_CHUNKS)
        return pltpu.make_async_remote_copy(
            src_ref=out_ref.at[idx, blocks, rows_here],
            dst_ref=out_ref.at[idx, blocks, rows_here],
            send_sem=send_sem.at[d, step, k],
            recv_sem=recv_sem.at[d, step, k],
            device_id={"cz": dest[d]},
            device_id_type=MESH_ID,
        )

    sends = []
    for step in range(n - 1):
        for k in range(SUB_CHUNKS):
            for d in range(2):
                if step > 0:
                    got = lax.rem(me + n - step, n) if d == 0 else lax.rem(me + step, n)
                    link(d, step - 1, k, got).wait_recv()
                idx = lax.rem(me + n - step, n) if d == 0 else lax.rem(me + step, n)
                copy = link(d, step, k, idx)
                copy.start()
                sends.append(copy)
    for k in range(SUB_CHUNKS):
        for d in range(2):
            got = lax.rem(me + 1, n) if d == 0 else lax.rem(me + n - 1, n)
            link(d, n - 2, k, got).wait_recv()
    for copy in ysends + sends:
        copy.wait_send()


def all_gather_kernel(x, n, ny, collective_id):
    rows, cols = x.shape
    out = pl.pallas_call(
        functools.partial(_ag_kernel, n, ny),
        out_shape=jax.ShapeDtypeStruct((n, ny, rows, cols), x.dtype),
        in_specs=[pl.BlockSpec(memory_space=pltpu.VMEM)],
        out_specs=pl.BlockSpec(memory_space=pltpu.VMEM),
        scratch_shapes=[
            pltpu.SemaphoreType.DMA((1,)),
            pltpu.SemaphoreType.DMA((ny - 1,)),
            pltpu.SemaphoreType.DMA((ny,)),
            pltpu.SemaphoreType.DMA((2, n - 1, SUB_CHUNKS)),
            pltpu.SemaphoreType.DMA((2, n - 1, SUB_CHUNKS)),
        ],
        compiler_params=pltpu.CompilerParams(collective_id=collective_id, has_side_effects=True),
    )(x)
    return out.reshape(n * ny * rows, cols)


def _ag2_kernel(n, ny, x_ref, out1, out2, own_sem, y1_send, y1_recv, z1_send, z1_recv, z2_send, z2_recv, y2_send, y2_recv):
    me, me_y = _enter(n, ny)
    right = lax.rem(me + 1, n)
    left = lax.rem(me + n - 1, n)
    r = out1.shape[2]
    half = r // 2
    dest = (right, left)
    mine1 = pltpu.make_async_copy(x_ref.at[pl.ds(0, r)], out1.at[me, me_y], own_sem.at[0])
    mine2 = pltpu.make_async_copy(x_ref.at[pl.ds(r, r)], out2.at[me_y, me], own_sem.at[1])
    mine1.start()
    mine2.start()

    def to_y(shift, src, dst, send_sem, recv_sem, sender):
        peer = lax.rem(me_y + shift, ny)
        return pltpu.make_async_remote_copy(
            src_ref=src,
            dst_ref=dst,
            send_sem=send_sem.at[shift - 1],
            recv_sem=recv_sem.at[sender],
            device_id={"cy": peer},
            device_id_type=MESH_ID,
        )

    sends = []
    for shift in range(1, ny):
        copy = to_y(shift, x_ref.at[pl.ds(0, r)], out1.at[me, me_y], y1_send, y1_recv, me_y)
        copy.start()
        sends.append(copy)

    def ring2(d, step, idx, src=None):
        rows_here = pl.ds(d * half, half)
        return pltpu.make_async_remote_copy(
            src_ref=out2.at[me_y, idx, rows_here] if src is None else src,
            dst_ref=out2.at[me_y, idx, rows_here],
            send_sem=z2_send.at[d, step],
            recv_sem=z2_recv.at[d, step],
            device_id={"cz": dest[d]},
            device_id_type=MESH_ID,
        )

    for step in range(n - 1):
        for d in range(2):
            idx = lax.rem(me + n - step, n) if d == 0 else lax.rem(me + step, n)
            if step == 0:
                copy = ring2(d, 0, idx, x_ref.at[pl.ds(r + d * half, half)])
            else:
                ring2(d, step - 1, idx).wait_recv()
                copy = ring2(d, step, idx)
            copy.start()
            sends.append(copy)
    for d in range(2):
        got = lax.rem(me + 1, n) if d == 0 else lax.rem(me + n - 1, n)
        ring2(d, n - 2, got).wait_recv()
    mine2.wait()
    ysends2 = []
    for shift in range(1, ny):
        copy = to_y(shift, out2.at[me_y], out2.at[me_y], y2_send, y2_recv, me_y)
        copy.start()
        ysends2.append(copy)

    mine1.wait()
    for shift in range(1, ny):
        peer = lax.rem(me_y + shift, ny)
        to_y(shift, x_ref.at[pl.ds(0, r)], out1.at[me, peer], y1_send, y1_recv, peer).wait_recv()

    def ring1(d, step, k, idx):
        rows_here = pl.ds(d * half, half)
        blocks = pl.ds(k * (ny // SUB_CHUNKS), ny // SUB_CHUNKS)
        return pltpu.make_async_remote_copy(
            src_ref=out1.at[idx, blocks, rows_here],
            dst_ref=out1.at[idx, blocks, rows_here],
            send_sem=z1_send.at[d, step, k],
            recv_sem=z1_recv.at[d, step, k],
            device_id={"cz": dest[d]},
            device_id_type=MESH_ID,
        )

    for step in range(n - 1):
        for k in range(SUB_CHUNKS):
            for d in range(2):
                if step > 0:
                    got = lax.rem(me + n - step, n) if d == 0 else lax.rem(me + step, n)
                    ring1(d, step - 1, k, got).wait_recv()
                idx = lax.rem(me + n - step, n) if d == 0 else lax.rem(me + step, n)
                copy = ring1(d, step, k, idx)
                copy.start()
                sends.append(copy)
    for k in range(SUB_CHUNKS):
        for d in range(2):
            got = lax.rem(me + 1, n) if d == 0 else lax.rem(me + n - 1, n)
            ring1(d, n - 2, k, got).wait_recv()
    for shift in range(1, ny):
        peer = lax.rem(me_y + shift, ny)
        to_y(shift, out2.at[me_y], out2.at[peer], y2_send, y2_recv, peer).wait_recv()
    for copy in sends + ysends2:
        copy.wait_send()


def all_gather_two_way(x, n, ny, collective_id):
    rows, cols = x.shape
    r = rows // 2
    out1, out2 = pl.pallas_call(
        functools.partial(_ag2_kernel, n, ny),
        out_shape=(
            jax.ShapeDtypeStruct((n, ny, r, cols), x.dtype),
            jax.ShapeDtypeStruct((ny, n, r, cols), x.dtype),
        ),
        in_specs=[pl.BlockSpec(memory_space=pltpu.VMEM)],
        out_specs=(pl.BlockSpec(memory_space=pltpu.VMEM), pl.BlockSpec(memory_space=pltpu.VMEM)),
        scratch_shapes=[
            pltpu.SemaphoreType.DMA((2,)),
            pltpu.SemaphoreType.DMA((ny - 1,)),
            pltpu.SemaphoreType.DMA((ny,)),
            pltpu.SemaphoreType.DMA((2, n - 1, SUB_CHUNKS)),
            pltpu.SemaphoreType.DMA((2, n - 1, SUB_CHUNKS)),
            pltpu.SemaphoreType.DMA((2, n - 1)),
            pltpu.SemaphoreType.DMA((2, n - 1)),
            pltpu.SemaphoreType.DMA((ny - 1,)),
            pltpu.SemaphoreType.DMA((ny,)),
        ],
        compiler_params=pltpu.CompilerParams(collective_id=collective_id, has_side_effects=True),
    )(x)
    return out1.reshape(n * ny * r, cols), out2.reshape(ny * n * r, cols)


def body(
    tokens,
    pick_flags,
    gate_scales,
    attn_gain,
    query_weight,
    key_weight,
    value_matrix,
    output_weight,
    ffn_gain,
    gate_weight,
    up_weight,
    down_weight,
):
    tok_local, width = tokens.shape
    y_size = lax.axis_size("cy")
    z_size = lax.axis_size("cz")
    ctx_size = y_size * z_size
    my_index = lax.axis_index("cy") * z_size + lax.axis_index("cz")
    blk = jnp.arange(ctx_size, dtype=jnp.int32)
    block_dev = (blk % y_size) * z_size + blk // y_size
    picked_count = PICK_DEV * ctx_size
    slots = MOST * ctx_size
    half_pick = PICK_DEV // 2
    half_cycle = ctx_size // 2
    slot_of = jnp.cumsum(pick_flags) - 1
    token_ids = jnp.arange(tok_local, dtype=jnp.int32)
    slot_match = (jnp.arange(MOST, dtype=jnp.int32)[:, None] == slot_of[None, :]) & (
        pick_flags[None, :] == 1
    )
    chosen = jnp.sum(jnp.where(slot_match, token_ids[None, :], 0), axis=1)
    filled = jnp.any(slot_match, axis=1)
    local_index = jnp.where(filled, chosen, -1)
    padded_rows = jnp.where(filled[:, None], tokens[chosen], jnp.zeros((), jnp.bfloat16))
    padded_gate = jnp.where(filled, gate_scales[chosen], jnp.zeros((), jnp.bfloat16))
    lane = jnp.arange(128, dtype=jnp.int32)[None, :]
    extra = jnp.where(
        lane == 0,
        local_index.astype(jnp.bfloat16)[:, None],
        jnp.where(lane == 1, padded_gate[:, None], jnp.zeros((), jnp.bfloat16)),
    )
    packed = jnp.concatenate((padded_rows, extra), axis=1)
    lead = MOST // 2
    part_one, part_two = all_gather_two_way(packed, z_size, y_size, 3)
    slot_ids = jnp.arange(slots, dtype=jnp.int32)
    part_blk = (slot_ids % (slots // 2)) // lead
    slot_dev = jnp.where(
        slot_ids < slots // 2, (part_blk % y_size) * z_size + part_blk // y_size, part_blk
    )
    all_index = jnp.concatenate((part_one[:, width], part_two[:, width])).astype(jnp.int32)
    slot_filled = all_index >= 0
    per_part = jnp.sum(slot_filled.reshape(2, ctx_size, lead).astype(jnp.int32), axis=2)
    counts = per_part[0].reshape(z_size, y_size).T.reshape(ctx_size) + per_part[1]
    run_ends = jnp.cumsum(counts)
    run_starts = run_ends - counts
    slot_pos = slot_dev * tok_local + all_index
    rope_pos = jnp.where(slot_filled, slot_pos, 0)
    never = jnp.int32(1 << 30)
    mask_pos = jnp.where(slot_filled, slot_pos, never)
    normalized = jnp.concatenate(
        (
            rms_scale(part_one[:, :width].astype(jnp.float32), attn_gain).astype(jnp.bfloat16),
            rms_scale(part_two[:, :width].astype(jnp.float32), attn_gain).astype(jnp.bfloat16),
        ),
        axis=0,
    )
    queries = jnp.dot(normalized, query_weight, preferred_element_type=jnp.float32)
    queries = apply_rotary(queries, rope_pos).astype(jnp.bfloat16)
    kv_weight = jnp.concatenate((key_weight, value_matrix), axis=1)
    kv_local = jnp.einsum(
        "pd,dc->cp", normalized, kv_weight, preferred_element_type=jnp.float32
    ).astype(jnp.bfloat16)
    comps = key_weight.shape[1] // KEY_VALUE_HEADS
    query_group_width = QUERY_HEADS // KEY_VALUE_HEADS
    by_head = jnp.transpose(kv_local.reshape(2, comps, KEY_VALUE_HEADS, slots), (2, 0, 1, 3))
    send = jnp.repeat(by_head, query_group_width, axis=0)
    got = lax.all_to_all(send, GROUP, 0, 0, tiled=True)
    key_cols = got[:, 0].reshape(ctx_size * comps, slots)
    value_cols = got[:, 1].reshape(ctx_size * comps, slots)
    keys_here = apply_rotary(key_cols.T.astype(jnp.float32), rope_pos).astype(jnp.bfloat16)
    values_here = value_cols.T
    scores = jnp.dot(queries, keys_here.T, preferred_element_type=jnp.float32) / jnp.sqrt(
        jnp.float32(HEAD_SIZE)
    )
    allowed = mask_pos[None, :] <= mask_pos[:, None]
    scores = jnp.where(allowed, scores, -jnp.inf)
    row_max = jnp.max(scores, axis=1, keepdims=True)
    exp_terms = jnp.exp(scores - row_max)
    prob_bf = (exp_terms / jnp.sum(exp_terms, axis=1, keepdims=True)).astype(jnp.bfloat16)
    head_pad = jnp.dot(prob_bf, values_here, preferred_element_type=jnp.float32).astype(jnp.bfloat16)
    order_ids = jnp.arange(picked_count, dtype=jnp.int32)
    owner_of = order_ids // PICK_DEV
    within = order_ids % PICK_DEV
    low_part = within < half_pick
    rank_block = jnp.where(low_part, owner_of, (owner_of + half_cycle) % ctx_size)
    rank_inner = jnp.where(low_part, 2 * within, 2 * (within - half_pick) + 1)
    rank_ids = rank_block * PICK_DEV + rank_inner
    before = (run_ends[None, :] <= rank_ids[:, None]).astype(jnp.int32)
    source = jnp.sum(before, axis=1)
    offset = rank_ids - jnp.sum(before * counts[None, :], axis=1)
    source_block = (source % z_size) * y_size + source // z_size
    flat_row = jnp.where(
        offset < lead, source_block * lead + offset, slots // 2 + source * lead + offset - lead
    )
    flat_blocked = flat_row.reshape(ctx_size, PICK_DEV)[block_dev].reshape(picked_count)
    pick_onehot = (flat_blocked[:, None] == slot_ids[None, :]).astype(jnp.bfloat16)
    head_out = jnp.dot(pick_onehot, head_pad, preferred_element_type=jnp.float32).astype(jnp.bfloat16)
    own_start = my_index * PICK_DEV
    own_flat = lax.dynamic_slice_in_dim(flat_row, own_start, PICK_DEV, 0)
    part_slots = jnp.arange(slots // 2, dtype=jnp.int32)[None, :]
    pick_one = (own_flat[:, None] == part_slots).astype(jnp.bfloat16)
    pick_two = (own_flat[:, None] - slots // 2 == part_slots).astype(jnp.bfloat16)
    own_packed = jnp.dot(pick_one, part_one, preferred_element_type=jnp.float32) + jnp.dot(
        pick_two, part_two, preferred_element_type=jnp.float32
    )
    own_rows = own_packed[:, :width]
    scale_own = own_packed[:, width + 1]
    attn_own = reduce_scatter_kernel(
        head_out.reshape(z_size, y_size * PICK_DEV, head_out.shape[1]), output_weight, y_size, 0
    )
    mixed_own = own_rows + attn_own
    normed_own = rms_scale(mixed_own, ffn_gain).astype(jnp.bfloat16)
    normed_ffn = all_gather_kernel(normed_own, z_size, y_size, 2)
    gate_proj = jnp.dot(normed_ffn, gate_weight, preferred_element_type=jnp.float32)
    up_proj = jnp.dot(normed_ffn, up_weight, preferred_element_type=jnp.float32)
    hidden = (jax.nn.silu(gate_proj) * up_proj).astype(jnp.bfloat16)
    ffn_own = reduce_scatter_kernel(
        hidden.reshape(z_size, y_size * PICK_DEV, hidden.shape[1]), down_weight, y_size, 1
    )
    final_own = (own_rows + scale_own[:, None] * (attn_own + ffn_own)).astype(jnp.bfloat16)
    own_source = lax.dynamic_slice_in_dim(source, own_start, PICK_DEV, 0)
    targets = jnp.arange(ctx_size, dtype=jnp.int32)[:, None]
    first_half = (own_source[None, :half_pick] == targets)[:, :, None]
    second_half = (own_source[None, half_pick:] == targets)[:, :, None]
    zero = jnp.zeros((), jnp.bfloat16)
    back = jnp.where(
        first_half,
        final_own[None, :half_pick],
        jnp.where(second_half, final_own[None, half_pick:], zero),
    )
    returned = lax.all_to_all(back, GROUP, 0, 0, tiled=True).reshape(ctx_size * half_pick, width)
    my_start = run_starts[my_index]
    rank_here = jnp.clip(my_start + slot_of, 0, picked_count - 1)
    inner_here = rank_here % PICK_DEV
    odd_here = inner_here % 2
    owner_here = (rank_here // PICK_DEV + odd_here * half_cycle) % ctx_size
    take_rows = owner_here * half_pick + inner_here // 2
    return jnp.where(pick_flags[:, None] == 1, returned[take_rows], tokens)


def solution(mesh):
    dp_size, ctx_size = mesh.devices.shape
    z_size = Z_RUN if ctx_size % Z_RUN == 0 else ctx_size
    split = Mesh(mesh.devices.reshape(dp_size, ctx_size // z_size, z_size), ("dp", "cy", "cz"))
    rows = ("dp", "cy", "cz")
    in_specs = (
        P(rows, None),
        P(rows),
        P(rows),
        P(),
        P(None, GROUP),
        P(None, GROUP),
        P(None, GROUP),
        P(GROUP, None),
        P(),
        P(None, GROUP),
        P(None, GROUP),
        P(GROUP, None),
    )
    out_specs = P(rows, None)
    return jax.shard_map(body, mesh=split, in_specs=in_specs, out_specs=out_specs, check_vma=False)
```

```python
import functools

import jax
import jax.numpy as jnp
from jax import lax
from jax.experimental import pallas as pl
from jax.experimental.pallas import tpu as pltpu
from jax.sharding import Mesh, PartitionSpec as P

QUERY_HEADS = 32
KEY_VALUE_HEADS = 8
HEAD_SIZE = 128
PICK_DEV = 16
MOST = 32
Z_RUN = 8
GROUP = ("cy", "cz")


norm_eps = 1e-05
rope_base = 500000.0


def rms_scale(matrix, gain_vec):
    mean_square = jnp.mean(matrix * matrix, axis=-1, keepdims=True)
    return matrix * lax.rsqrt(mean_square + norm_eps) * gain_vec


def apply_rotary(values, token_positions):
    half_dim = values.shape[-1] // 2
    frequency = rope_base ** (-(jnp.arange(half_dim, dtype=jnp.float32) * 2.0) / values.shape[-1])
    angles = token_positions.astype(jnp.float32)[:, None] * frequency[None, :]
    cosine = jnp.cos(angles)
    sine_part = jnp.sin(angles)
    lower_half = values[..., :half_dim]
    upper_half = values[..., half_dim:]
    return jnp.concatenate(
        (
            lower_half * cosine - upper_half * sine_part,
            upper_half * cosine + lower_half * sine_part,
        ),
        axis=-1,
    )


MESH_ID = pl.DeviceIdType.MESH
SUB_CHUNKS = 2
RS_PIECES = 16
AG_PIECES = 4


def _enter(nz, ny):
    me_z = lax.axis_index("cz")
    me_y = lax.axis_index("cy")
    barrier = pltpu.get_barrier_semaphore()
    for neighbour in (lax.rem(me_z + nz - 1, nz), lax.rem(me_z + 1, nz)):
        pl.semaphore_signal(barrier, inc=1, device_id={"cz": neighbour}, device_id_type=MESH_ID)
    for shift in range(1, ny):
        pl.semaphore_signal(barrier, inc=1, device_id={"cy": lax.rem(me_y + shift, ny)}, device_id_type=MESH_ID)
    pl.semaphore_wait(barrier, 2 + ny - 1)
    return me_z, me_y


def _rs_kernel(n, ny, x_ref, out_ref, recv, sendbuf, send_sem, recv_sem, zsum, ybuf, yrecv, ysend_sem, yrecv_sem):
    me, me_y = _enter(n, ny)
    right = lax.rem(me + 1, n)
    left = lax.rem(me + n - 1, n)
    half = x_ref.shape[2] // 2
    piece = x_ref.shape[1] // RS_PIECES
    own = out_ref.shape[0]
    dest = (right, left)

    def link(d, slot, k, src):
        return pltpu.make_async_remote_copy(
            src_ref=src,
            dst_ref=recv.at[d, slot, k],
            send_sem=send_sem.at[d, slot, k],
            recv_sem=recv_sem.at[d, slot, k],
            device_id={"cz": dest[d]},
            device_id_type=MESH_ID,
        )

    sends = []
    for k in range(RS_PIECES):
        for d in range(2):
            first = lax.rem(me + n - 1, n) if d == 0 else lax.rem(me + 1, n)
            copy = link(d, 0, k, x_ref.at[first, pl.ds(k * piece, piece), pl.ds(d * half, half)])
            copy.start()
            sends.append(copy)
    for step in range(n - 1):
        for k in range(RS_PIECES):
            for d in range(2):
                link(d, step, k, sendbuf.at[d, step, k]).wait_recv()
                if d == 0:
                    chunk = lax.rem(me + 2 * n - step - 2, n)
                else:
                    chunk = lax.rem(me + step + 2, n)
                total = recv[d, step, k].astype(jnp.float32) + x_ref[
                    chunk, pl.ds(k * piece, piece), pl.ds(d * half, half)
                ].astype(jnp.float32)
                if step == n - 2:
                    zsum[pl.ds(k * piece, piece), pl.ds(d * half, half)] = total
                else:
                    sendbuf[d, step, k] = total.astype(sendbuf.dtype)
                    copy = link(d, step + 1, k, sendbuf.at[d, step, k])
                    copy.start()
                    sends.append(copy)
    ysends = []
    for shift in range(1, ny):
        peer = lax.rem(me_y + shift, ny)
        ybuf[shift - 1] = zsum[pl.ds(pl.multiple_of(peer * own, own), own), :].astype(ybuf.dtype)
        copy = pltpu.make_async_remote_copy(
            src_ref=ybuf.at[shift - 1],
            dst_ref=yrecv.at[shift - 1],
            send_sem=ysend_sem.at[shift - 1],
            recv_sem=yrecv_sem.at[shift - 1],
            device_id={"cy": peer},
            device_id_type=MESH_ID,
        )
        copy.start()
        ysends.append(copy)
    total = zsum[pl.ds(pl.multiple_of(me_y * own, own), own), :]
    for shift in range(1, ny):
        ysends[shift - 1].wait_recv()
        total = total + yrecv[shift - 1].astype(jnp.float32)
    out_ref[...] = total
    for copy in sends + ysends:
        copy.wait_send()


def reduce_scatter_kernel(x, ny, collective_id):
    n, rows, cols = x.shape
    half = cols // 2
    piece = rows // RS_PIECES
    own = rows // ny
    return pl.pallas_call(
        functools.partial(_rs_kernel, n, ny),
        out_shape=jax.ShapeDtypeStruct((own, cols), jnp.float32),
        in_specs=[pl.BlockSpec(memory_space=pltpu.VMEM)],
        out_specs=pl.BlockSpec(memory_space=pltpu.VMEM),
        scratch_shapes=[
            pltpu.VMEM((2, n - 1, RS_PIECES, piece, half), x.dtype),
            pltpu.VMEM((2, n - 1, RS_PIECES, piece, half), x.dtype),
            pltpu.SemaphoreType.DMA((2, n - 1, RS_PIECES)),
            pltpu.SemaphoreType.DMA((2, n - 1, RS_PIECES)),
            pltpu.VMEM((rows, cols), jnp.float32),
            pltpu.VMEM((ny - 1, own, cols), x.dtype),
            pltpu.VMEM((ny - 1, own, cols), x.dtype),
            pltpu.SemaphoreType.DMA((ny - 1,)),
            pltpu.SemaphoreType.DMA((ny - 1,)),
        ],
        compiler_params=pltpu.CompilerParams(collective_id=collective_id, has_side_effects=True),
    )(x)


def _ag_kernel(n, ny, x_ref, out_ref, own_sem, ysend_sem, yrecv_sem, send_sem, recv_sem):
    me, me_y = _enter(n, ny)
    right = lax.rem(me + 1, n)
    left = lax.rem(me + n - 1, n)
    rows = x_ref.shape[0]
    half = rows // 2
    dest = (right, left)
    mine = pltpu.make_async_copy(x_ref, out_ref.at[me, me_y], own_sem.at[0])
    mine.start()
    ysends = []
    for shift in range(1, ny):
        peer = lax.rem(me_y + shift, ny)
        copy = pltpu.make_async_remote_copy(
            src_ref=x_ref,
            dst_ref=out_ref.at[me, me_y],
            send_sem=ysend_sem.at[shift - 1],
            recv_sem=yrecv_sem.at[me_y],
            device_id={"cy": peer},
            device_id_type=MESH_ID,
        )
        copy.start()
        ysends.append(copy)
    mine.wait()
    for shift in range(1, ny):
        peer = lax.rem(me_y + shift, ny)
        pltpu.make_async_remote_copy(
            src_ref=x_ref,
            dst_ref=out_ref.at[me, peer],
            send_sem=ysend_sem.at[shift - 1],
            recv_sem=yrecv_sem.at[peer],
            device_id={"cy": peer},
            device_id_type=MESH_ID,
        ).wait_recv()

    def link(d, step, k, idx):
        rows_here = pl.ds(d * half, half)
        blocks = pl.ds(k * (ny // AG_PIECES), ny // AG_PIECES)
        return pltpu.make_async_remote_copy(
            src_ref=out_ref.at[idx, blocks, rows_here],
            dst_ref=out_ref.at[idx, blocks, rows_here],
            send_sem=send_sem.at[d, step, k],
            recv_sem=recv_sem.at[d, step, k],
            device_id={"cz": dest[d]},
            device_id_type=MESH_ID,
        )

    sends = []
    for step in range(n - 1):
        for k in range(AG_PIECES):
            for d in range(2):
                if step > 0:
                    got = lax.rem(me + n - step, n) if d == 0 else lax.rem(me + step, n)
                    link(d, step - 1, k, got).wait_recv()
                idx = lax.rem(me + n - step, n) if d == 0 else lax.rem(me + step, n)
                copy = link(d, step, k, idx)
                copy.start()
                sends.append(copy)
    for k in range(AG_PIECES):
        for d in range(2):
            got = lax.rem(me + 1, n) if d == 0 else lax.rem(me + n - 1, n)
            link(d, n - 2, k, got).wait_recv()
    for copy in ysends + sends:
        copy.wait_send()


def all_gather_kernel(x, n, ny, collective_id):
    rows, cols = x.shape
    out = pl.pallas_call(
        functools.partial(_ag_kernel, n, ny),
        out_shape=jax.ShapeDtypeStruct((n, ny, rows, cols), x.dtype),
        in_specs=[pl.BlockSpec(memory_space=pltpu.VMEM)],
        out_specs=pl.BlockSpec(memory_space=pltpu.VMEM),
        scratch_shapes=[
            pltpu.SemaphoreType.DMA((1,)),
            pltpu.SemaphoreType.DMA((ny - 1,)),
            pltpu.SemaphoreType.DMA((ny,)),
            pltpu.SemaphoreType.DMA((2, n - 1, AG_PIECES)),
            pltpu.SemaphoreType.DMA((2, n - 1, AG_PIECES)),
        ],
        compiler_params=pltpu.CompilerParams(collective_id=collective_id, has_side_effects=True),
    )(x)
    return out.reshape(n * ny * rows, cols)


def _ag2_kernel(n, ny, x_ref, out1, out2, own_sem, y1_send, y1_recv, z1_send, z1_recv, z2_send, z2_recv, y2_send, y2_recv):
    me, me_y = _enter(n, ny)
    right = lax.rem(me + 1, n)
    left = lax.rem(me + n - 1, n)
    r = out1.shape[2]
    half = r // 2
    dest = (right, left)
    mine1 = pltpu.make_async_copy(x_ref.at[pl.ds(0, r)], out1.at[me, me_y], own_sem.at[0])
    mine2 = pltpu.make_async_copy(x_ref.at[pl.ds(r, r)], out2.at[me_y, me], own_sem.at[1])
    mine1.start()
    mine2.start()

    def to_y(shift, src, dst, send_sem, recv_sem, sender):
        peer = lax.rem(me_y + shift, ny)
        return pltpu.make_async_remote_copy(
            src_ref=src,
            dst_ref=dst,
            send_sem=send_sem.at[shift - 1],
            recv_sem=recv_sem.at[sender],
            device_id={"cy": peer},
            device_id_type=MESH_ID,
        )

    sends = []
    for shift in range(1, ny):
        copy = to_y(shift, x_ref.at[pl.ds(0, r)], out1.at[me, me_y], y1_send, y1_recv, me_y)
        copy.start()
        sends.append(copy)

    def ring2(d, step, idx, src=None):
        rows_here = pl.ds(d * half, half)
        return pltpu.make_async_remote_copy(
            src_ref=out2.at[me_y, idx, rows_here] if src is None else src,
            dst_ref=out2.at[me_y, idx, rows_here],
            send_sem=z2_send.at[d, step],
            recv_sem=z2_recv.at[d, step],
            device_id={"cz": dest[d]},
            device_id_type=MESH_ID,
        )

    for step in range(n - 1):
        for d in range(2):
            idx = lax.rem(me + n - step, n) if d == 0 else lax.rem(me + step, n)
            if step == 0:
                copy = ring2(d, 0, idx, x_ref.at[pl.ds(r + d * half, half)])
            else:
                ring2(d, step - 1, idx).wait_recv()
                copy = ring2(d, step, idx)
            copy.start()
            sends.append(copy)
    for d in range(2):
        got = lax.rem(me + 1, n) if d == 0 else lax.rem(me + n - 1, n)
        ring2(d, n - 2, got).wait_recv()
    mine2.wait()
    ysends2 = []
    for shift in range(1, ny):
        copy = to_y(shift, out2.at[me_y], out2.at[me_y], y2_send, y2_recv, me_y)
        copy.start()
        ysends2.append(copy)

    mine1.wait()
    for shift in range(1, ny):
        peer = lax.rem(me_y + shift, ny)
        to_y(shift, x_ref.at[pl.ds(0, r)], out1.at[me, peer], y1_send, y1_recv, peer).wait_recv()

    def ring1(d, step, idx):
        rows_here = pl.ds(d * half, half)
        return pltpu.make_async_remote_copy(
            src_ref=out1.at[idx, :, rows_here],
            dst_ref=out1.at[idx, :, rows_here],
            send_sem=z1_send.at[d, step],
            recv_sem=z1_recv.at[d, step],
            device_id={"cz": dest[d]},
            device_id_type=MESH_ID,
        )

    for step in range(n - 1):
        for d in range(2):
            if step > 0:
                got = lax.rem(me + n - step, n) if d == 0 else lax.rem(me + step, n)
                ring1(d, step - 1, got).wait_recv()
            idx = lax.rem(me + n - step, n) if d == 0 else lax.rem(me + step, n)
            copy = ring1(d, step, idx)
            copy.start()
            sends.append(copy)
    for d in range(2):
        got = lax.rem(me + 1, n) if d == 0 else lax.rem(me + n - 1, n)
        ring1(d, n - 2, got).wait_recv()
    for shift in range(1, ny):
        peer = lax.rem(me_y + shift, ny)
        to_y(shift, out2.at[me_y], out2.at[peer], y2_send, y2_recv, peer).wait_recv()
    for copy in sends + ysends2:
        copy.wait_send()


def all_gather_two_way(x, n, ny, collective_id):
    rows, cols = x.shape
    r = rows // 2
    out1, out2 = pl.pallas_call(
        functools.partial(_ag2_kernel, n, ny),
        out_shape=(
            jax.ShapeDtypeStruct((n, ny, r, cols), x.dtype),
            jax.ShapeDtypeStruct((ny, n, r, cols), x.dtype),
        ),
        in_specs=[pl.BlockSpec(memory_space=pltpu.VMEM)],
        out_specs=(pl.BlockSpec(memory_space=pltpu.VMEM), pl.BlockSpec(memory_space=pltpu.VMEM)),
        scratch_shapes=[
            pltpu.SemaphoreType.DMA((2,)),
            pltpu.SemaphoreType.DMA((ny - 1,)),
            pltpu.SemaphoreType.DMA((ny,)),
            pltpu.SemaphoreType.DMA((2, n - 1)),
            pltpu.SemaphoreType.DMA((2, n - 1)),
            pltpu.SemaphoreType.DMA((2, n - 1)),
            pltpu.SemaphoreType.DMA((2, n - 1)),
            pltpu.SemaphoreType.DMA((ny - 1,)),
            pltpu.SemaphoreType.DMA((ny,)),
        ],
        compiler_params=pltpu.CompilerParams(collective_id=collective_id, has_side_effects=True),
    )(x)
    return out1.reshape(n * ny * r, cols), out2.reshape(ny * n * r, cols)


def body(
    tokens,
    pick_flags,
    gate_scales,
    attn_gain,
    query_weight,
    key_weight,
    value_matrix,
    output_weight,
    ffn_gain,
    gate_weight,
    up_weight,
    down_weight,
):
    tok_local, width = tokens.shape
    y_size = lax.axis_size("cy")
    z_size = lax.axis_size("cz")
    ctx_size = y_size * z_size
    my_index = lax.axis_index("cy") * z_size + lax.axis_index("cz")
    blk = jnp.arange(ctx_size, dtype=jnp.int32)
    block_dev = (blk % y_size) * z_size + blk // y_size
    picked_count = PICK_DEV * ctx_size
    slots = MOST * ctx_size
    half_pick = PICK_DEV // 2
    half_cycle = ctx_size // 2
    slot_of = jnp.cumsum(pick_flags) - 1
    token_ids = jnp.arange(tok_local, dtype=jnp.int32)
    slot_match = (jnp.arange(MOST, dtype=jnp.int32)[:, None] == slot_of[None, :]) & (
        pick_flags[None, :] == 1
    )
    chosen = jnp.sum(jnp.where(slot_match, token_ids[None, :], 0), axis=1)
    filled = jnp.any(slot_match, axis=1)
    local_index = jnp.where(filled, chosen, -1)
    padded_rows = jnp.where(filled[:, None], tokens[chosen], jnp.zeros((), jnp.bfloat16))
    padded_gate = jnp.where(filled, gate_scales[chosen], jnp.zeros((), jnp.bfloat16))
    lane = jnp.arange(128, dtype=jnp.int32)[None, :]
    extra = jnp.where(
        lane == 0,
        local_index.astype(jnp.bfloat16)[:, None],
        jnp.where(lane == 1, padded_gate[:, None], jnp.zeros((), jnp.bfloat16)),
    )
    packed = jnp.concatenate((padded_rows, extra), axis=1)
    lead = MOST // 2
    part_one, part_two = all_gather_two_way(packed, z_size, y_size, 3)
    slot_ids = jnp.arange(slots, dtype=jnp.int32)
    part_blk = (slot_ids % (slots // 2)) // lead
    slot_dev = jnp.where(
        slot_ids < slots // 2, (part_blk % y_size) * z_size + part_blk // y_size, part_blk
    )
    all_index = jnp.concatenate((part_one[:, width], part_two[:, width])).astype(jnp.int32)
    slot_filled = all_index >= 0
    per_part = jnp.sum(slot_filled.reshape(2, ctx_size, lead).astype(jnp.int32), axis=2)
    counts = per_part[0].reshape(z_size, y_size).T.reshape(ctx_size) + per_part[1]
    run_ends = jnp.cumsum(counts)
    run_starts = run_ends - counts
    slot_pos = slot_dev * tok_local + all_index
    rope_pos = jnp.where(slot_filled, slot_pos, 0)
    never = jnp.int32(1 << 30)
    mask_pos = jnp.where(slot_filled, slot_pos, never)
    normalized = jnp.concatenate(
        (
            rms_scale(part_one[:, :width].astype(jnp.float32), attn_gain).astype(jnp.bfloat16),
            rms_scale(part_two[:, :width].astype(jnp.float32), attn_gain).astype(jnp.bfloat16),
        ),
        axis=0,
    )
    queries = jnp.dot(normalized, query_weight, preferred_element_type=jnp.float32)
    queries = apply_rotary(queries, rope_pos).astype(jnp.bfloat16)
    kv_weight = jnp.concatenate((key_weight, value_matrix), axis=1)
    kv_local = jnp.einsum(
        "pd,dc->cp", normalized, kv_weight, preferred_element_type=jnp.float32
    ).astype(jnp.bfloat16)
    comps = key_weight.shape[1] // KEY_VALUE_HEADS
    query_group_width = QUERY_HEADS // KEY_VALUE_HEADS
    by_head = jnp.transpose(kv_local.reshape(2, comps, KEY_VALUE_HEADS, slots), (2, 0, 1, 3))
    send = jnp.repeat(by_head, query_group_width, axis=0)
    got = lax.all_to_all(send, GROUP, 0, 0, tiled=True)
    key_cols = got[:, 0].reshape(ctx_size * comps, slots)
    value_cols = got[:, 1].reshape(ctx_size * comps, slots)
    keys_here = apply_rotary(key_cols.T.astype(jnp.float32), rope_pos).astype(jnp.bfloat16)
    values_here = value_cols.T
    scores = jnp.dot(queries, keys_here.T, preferred_element_type=jnp.float32) / jnp.sqrt(
        jnp.float32(HEAD_SIZE)
    )
    allowed = mask_pos[None, :] <= mask_pos[:, None]
    scores = jnp.where(allowed, scores, -jnp.inf)
    row_max = jnp.max(scores, axis=1, keepdims=True)
    exp_terms = jnp.exp(scores - row_max)
    prob_bf = (exp_terms / jnp.sum(exp_terms, axis=1, keepdims=True)).astype(jnp.bfloat16)
    head_pad = jnp.dot(prob_bf, values_here, preferred_element_type=jnp.float32).astype(jnp.bfloat16)
    order_ids = jnp.arange(picked_count, dtype=jnp.int32)
    owner_of = order_ids // PICK_DEV
    within = order_ids % PICK_DEV
    low_part = within < half_pick
    rank_block = jnp.where(low_part, owner_of, (owner_of + half_cycle) % ctx_size)
    rank_inner = jnp.where(low_part, 2 * within, 2 * (within - half_pick) + 1)
    rank_ids = rank_block * PICK_DEV + rank_inner
    before = (run_ends[None, :] <= rank_ids[:, None]).astype(jnp.int32)
    source = jnp.sum(before, axis=1)
    offset = rank_ids - jnp.sum(before * counts[None, :], axis=1)
    source_block = (source % z_size) * y_size + source // z_size
    flat_row = jnp.where(
        offset < lead, source_block * lead + offset, slots // 2 + source * lead + offset - lead
    )
    flat_blocked = flat_row.reshape(ctx_size, PICK_DEV)[block_dev].reshape(picked_count)
    pick_onehot = (flat_blocked[:, None] == slot_ids[None, :]).astype(jnp.bfloat16)
    head_out = jnp.dot(pick_onehot, head_pad, preferred_element_type=jnp.float32).astype(jnp.bfloat16)
    own_start = my_index * PICK_DEV
    own_flat = lax.dynamic_slice_in_dim(flat_row, own_start, PICK_DEV, 0)
    part_slots = jnp.arange(slots // 2, dtype=jnp.int32)[None, :]
    pick_one = (own_flat[:, None] == part_slots).astype(jnp.bfloat16)
    pick_two = (own_flat[:, None] - slots // 2 == part_slots).astype(jnp.bfloat16)
    own_packed = jnp.dot(pick_one, part_one, preferred_element_type=jnp.float32) + jnp.dot(
        pick_two, part_two, preferred_element_type=jnp.float32
    )
    own_rows = own_packed[:, :width]
    scale_own = own_packed[:, width + 1]
    attn_partial = jnp.dot(head_out, output_weight, preferred_element_type=jnp.float32).astype(jnp.bfloat16)
    attn_own = reduce_scatter_kernel(attn_partial.reshape(z_size, y_size * PICK_DEV, width), y_size, 0)
    mixed_own = own_rows + attn_own
    normed_own = rms_scale(mixed_own, ffn_gain).astype(jnp.bfloat16)
    normed_ffn = all_gather_kernel(normed_own, z_size, y_size, 2)
    gate_proj = jnp.dot(normed_ffn, gate_weight, preferred_element_type=jnp.float32)
    up_proj = jnp.dot(normed_ffn, up_weight, preferred_element_type=jnp.float32)
    hidden = (jax.nn.silu(gate_proj) * up_proj).astype(jnp.bfloat16)
    ffn_partial = jnp.dot(hidden, down_weight, preferred_element_type=jnp.float32).astype(jnp.bfloat16)
    ffn_own = reduce_scatter_kernel(ffn_partial.reshape(z_size, y_size * PICK_DEV, width), y_size, 1)
    final_own = (own_rows + scale_own[:, None] * (attn_own + ffn_own)).astype(jnp.bfloat16)
    own_source = lax.dynamic_slice_in_dim(source, own_start, PICK_DEV, 0)
    targets = jnp.arange(ctx_size, dtype=jnp.int32)[:, None]
    first_half = (own_source[None, :half_pick] == targets)[:, :, None]
    second_half = (own_source[None, half_pick:] == targets)[:, :, None]
    zero = jnp.zeros((), jnp.bfloat16)
    back = jnp.where(
        first_half,
        final_own[None, :half_pick],
        jnp.where(second_half, final_own[None, half_pick:], zero),
    )
    returned = lax.all_to_all(back, GROUP, 0, 0, tiled=True).reshape(ctx_size * half_pick, width)
    my_start = run_starts[my_index]
    rank_here = jnp.clip(my_start + slot_of, 0, picked_count - 1)
    inner_here = rank_here % PICK_DEV
    odd_here = inner_here % 2
    owner_here = (rank_here // PICK_DEV + odd_here * half_cycle) % ctx_size
    take_rows = owner_here * half_pick + inner_here // 2
    return jnp.where(pick_flags[:, None] == 1, returned[take_rows], tokens)


def solution(mesh):
    dp_size, ctx_size = mesh.devices.shape
    z_size = Z_RUN if ctx_size % Z_RUN == 0 else ctx_size
    split = Mesh(mesh.devices.reshape(dp_size, ctx_size // z_size, z_size), ("dp", "cy", "cz"))
    rows = ("dp", "cy", "cz")
    in_specs = (
        P(rows, None),
        P(rows),
        P(rows),
        P(),
        P(None, GROUP),
        P(None, GROUP),
        P(None, GROUP),
        P(GROUP, None),
        P(),
        P(None, GROUP),
        P(None, GROUP),
        P(GROUP, None),
    )
    out_specs = P(rows, None)
    return jax.shard_map(body, mesh=split, in_specs=in_specs, out_specs=out_specs, check_vma=False)
```
